512 devices in a mesh: fsdp: 16 (over y, x_lo, core), ctx: 32 (over z, x_hi).
Axes of the slice: x: 4 (x_hi: 2, x_lo: 2; x = x_hi * 2 + x_lo), y: 4, z: 16, core: 2. Of those that a mesh axis runs over, the one named last changes fastest.
Arguments:
- token_ids: int32 [8192], P('ctx'), may hold values from 0 to 15
- table: float32 [16, 4096], P(None, 'fsdp'), may hold values from -6 to 6
- norm_gain: float32 [4096], P('fsdp'), may hold values from 0.25 to 1.75
- conv_weight: float32 [4, 4096], P(None, 'fsdp'), may hold values from -4 to 4
- conv_bias: float32 [4096], P('fsdp'), may hold values from -4 to 4
- weight_b: bfloat16 [4096, 128], P('fsdp'), may hold values from -0.09375 to 0.09375
- weight_c: bfloat16 [4096, 128], P('fsdp'), may hold values from -0.09375 to 0.09375
- step_weight: bfloat16 [4096, 64], P('fsdp'), may hold values from -0.1875 to 0.1875
- step_bias: float32 [64], P('fsdp'), as said below
- log_rate: float32 [64], P('fsdp'), as said below
- skip_gain: float32 [64], P('fsdp'), may hold values from 0.25 to 1.75
- out_grad: bfloat16 [8192, 4096], P('ctx', 'fsdp'), may hold values from -6 to 6
Outputs:
- mixer_out: bfloat16 [8192, 4096], P('ctx', 'fsdp')
- grad_embedded: bfloat16 [8192, 4096], P('ctx', 'fsdp')
- grad_table: float32 [16, 4096], P(None, 'fsdp')
- grad_norm_gain: float32 [4096], P('fsdp')
- grad_conv_weight: float32 [4, 4096], P(None, 'fsdp')
- grad_conv_bias: float32 [4096], P('fsdp')
- grad_weight_b: float32 [4096, 128], P('fsdp')
- grad_weight_c: float32 [4096, 128], P('fsdp')
- grad_step_weight: float32 [4096, 64], P('fsdp')
- grad_step_bias: float32 [64], P('fsdp')
- grad_log_rate: float32 [64], P('fsdp')
- grad_skip_gain: float32 [64], P('fsdp')
The draws below stay inside these ranges and needn't reach their ends.
Inputs may be any that keep to these rules, and one draw needn't show every extreme that they name: exp(log_rate) lies between 1 / 16 and 1 for every head. step_bias lies between log(1 / 8192) - 1 and log(0.2) - 1.
All inputs are finite; a program needn't handle non-finite values.
Results may differ from the reference program's by a relative error of at most 0.02.
Values may be sent and summed in bfloat16 or wider, within the bound.
No kernel may reach another device: no remote copies, remote signals or barrier semaphores. Data moves between devices by JAX's collectives and lax.ppermute only.
A program may use at most 64 MiB of HBM per device.

```python
import math
import jax
import jax.numpy as jnp
from jax import lax

D = 4096
HEADS = 64
STATE = 128
VOCAB = 16
KW = 4
SPAN = 256
SEQ_LEN = 8192
N_FSDP = 16


def head_plan(key, portion):
    folded = jax.random.fold_in(key, 7)
    chooser_key, rate_key, size_key = jax.random.split(folded, 3)
    chooser = jax.random.uniform(chooser_key, (HEADS,), jnp.float32)
    rate_blend = jax.random.uniform(rate_key, (HEADS,), jnp.float32)
    size_blend = jax.random.uniform(size_key, (HEADS,), jnp.float32)
    slow_rate = math.log(0.25 / SEQ_LEN) + rate_blend * math.log(4.0)
    fast_rate = math.log(1.0 / 50.0) + rate_blend * math.log(2.0)
    slow_size = math.log(1.0 / SEQ_LEN) + size_blend * math.log(4.0)
    fast_size = math.log(0.05) + size_blend * math.log(4.0)
    slower = chooser < portion
    log_decay = jnp.where(slower, slow_rate, fast_rate)
    log_size = jnp.where(slower, slow_size, fast_size)
    return (log_decay - log_size, log_size - 1.0)


def draw_log_rate(key, part):
    portion = 0.5
    rates, biases = head_plan(key, portion)
    return rates.astype(jnp.float32)


def draw_step_bias(key, part):
    portion = 0.5
    rates, biases = head_plan(key, portion)
    return biases.astype(jnp.float32)


def draw_token_ids(key, part):
    folded = jax.random.fold_in(key, 11)
    cut_key, order_key, upper_key, rank_key, low_key, high_key = jax.random.split(folded, 6)
    quarter = SEQ_LEN // 4
    jitter_reach = SEQ_LEN // 16
    jitter = jax.random.randint(cut_key, (3,), -jitter_reach, jitter_reach + 1, dtype=jnp.int32)
    cut_points = jnp.arange(1, 4, dtype=jnp.int32) * quarter + jitter
    positions = jnp.arange(SEQ_LEN, dtype=jnp.int32)
    regime = jnp.sum((positions[:, None] >= cut_points[None, :]).astype(jnp.int32), axis=1)
    orderings = jax.vmap(lambda subkey: jax.random.permutation(subkey, VOCAB))(jax.random.split(order_key, 4))
    upper_rank = jax.random.randint(upper_key, (SEQ_LEN,), 0, VOCAB, dtype=jnp.int32)
    rank_drawn = jax.random.randint(rank_key, (SEQ_LEN,), 0, upper_rank + 1, dtype=jnp.int32)
    token_values = orderings[regime, rank_drawn].astype(jnp.int32)
    low_spot = jax.random.randint(low_key, (), 0, SEQ_LEN // 2, dtype=jnp.int32)
    high_spot = jax.random.randint(high_key, (), SEQ_LEN // 2, SEQ_LEN, dtype=jnp.int32)
    token_values = token_values.at[low_spot].set(0)
    token_values = token_values.at[high_spot].set(VOCAB - 1)
    return token_values.astype(jnp.int32)


def shard_levels(own_key, dims, cuts, low, top_value):
    def one(position, shards_of):
        steps = jax.random.uniform(jax.random.fold_in(jax.random.fold_in(own_key, 6), position), (shards_of,), jnp.float32, low / len(cuts), top_value / len(cuts))
        return jnp.repeat(jnp.exp(steps), dims[position] // shards_of).reshape((-1,) + (1,) * (len(dims) - position - 1))

    gain = one(*cuts[0])
    for cut in cuts[1:]:
        gain = gain * one(*cut)
    return gain


def gaussian(stream_key, extent, scale, bound, cuts=(), held_as=jnp.bfloat16):
    array = scale * jax.random.normal(stream_key, extent, jnp.float32)
    if cuts:
        array = array * shard_levels(stream_key, extent, cuts, -0.22, 0.18)
    return jnp.clip(array, -bound, bound).astype(held_as)


def setup_inputs(seed: int = 0) -> dict:
    key_list = jax.random.split(jax.random.key(seed), 13)
    token_ids = draw_token_ids(jax.random.fold_in(key_list[12], 71), 0)
    table = gaussian(key_list[1], (VOCAB, D), 1.0, 6.0, ((1, 16),), jnp.float32)
    norm_gain = jnp.clip(1.0 + 0.15 * jax.random.normal(key_list[2], (D,), jnp.float32), 0.25, 1.75)
    conv_weight = gaussian(key_list[3], (KW, D), 0.5, 4.0, ((1, 16),), jnp.float32)
    conv_bias = gaussian(key_list[4], (D,), 0.5, 4.0, ((0, 16),), jnp.float32)
    weight_b = gaussian(key_list[5], (D, STATE), D ** -0.5, 0.09375, ((0, 16),))
    weight_c = gaussian(key_list[6], (D, STATE), D ** -0.5, 0.09375, ((0, 16),))
    step_weight = gaussian(key_list[7], (D, HEADS), (D // 4) ** -0.5, 0.1875, ((0, 16),))
    step_bias = draw_step_bias(jax.random.fold_in(key_list[12], 71), 0)
    log_rate = draw_log_rate(jax.random.fold_in(key_list[12], 71), 0)
    skip_gain = jnp.clip(0.25 + 1.5 * jax.random.uniform(key_list[10], (HEADS,), jnp.float32) ** shard_levels(key_list[10], (HEADS,), ((0, 16),), -0.2, 0.2), 0.25, 1.75)
    out_grad = gaussian(key_list[11], (SEQ_LEN, D), 1.0, 6.0, ((0, 32), (1, 16)))
    return {"token_ids": token_ids, "table": table, "norm_gain": norm_gain, "conv_weight": conv_weight, "conv_bias": conv_bias, "weight_b": weight_b, "weight_c": weight_c, "step_weight": step_weight, "step_bias": step_bias, "log_rate": log_rate, "skip_gain": skip_gain, "out_grad": out_grad}


def round_keep(value):
    rounded = lax.optimization_barrier(value.astype(jnp.bfloat16))
    return rounded.astype(jnp.float32)

def make_normed(embedded, norm_gain):
    scale = lax.rsqrt(lax.optimization_barrier(jnp.mean(embedded * embedded, axis=-1, keepdims=True)) + 1e-05)
    return round_keep(embedded * scale * norm_gain)

def conv_pair(padded, conv_weight, conv_bias):
    radius = conv_weight.shape[0] - 1
    length = padded.shape[-2] - 2 * radius
    forward = conv_bias + jnp.zeros_like(padded[..., :length, :])
    backward = conv_bias + jnp.zeros_like(padded[..., :length, :])
    for offset in range(radius + 1):
        forward = forward + conv_weight[offset] * padded[..., radius - offset:radius - offset + length, :]
        backward = backward + conv_weight[offset] * padded[..., radius + offset:radius + offset + length, :]
    return (round_keep(jax.nn.silu(forward)), round_keep(jax.nn.silu(backward)))

def contract(form, left, right):
    return jnp.einsum(form, left.astype(jnp.float32), right.astype(jnp.float32), precision=lax.Precision.HIGHEST)

def local_terms(xvals, bvals, cvals, step_raw, step_bias, log_rate):
    total_rows = xvals.shape[0]
    heads = step_raw.shape[1]
    blocks = total_rows // SPAN
    b_half = bvals.astype(jnp.bfloat16).reshape(blocks, SPAN, -1)
    c_half = cvals.astype(jnp.bfloat16).reshape(blocks, SPAN, -1)
    steps = jax.nn.softplus(step_raw + step_bias).reshape(blocks, SPAN, heads)
    logdec = -steps * jnp.exp(log_rate)
    cumul = jnp.cumsum(logdec, axis=1)
    cumul_heads = jnp.transpose(cumul, (0, 2, 1))
    steps_heads = jnp.transpose(steps, (0, 2, 1))
    inner = contract('cqn,csn->cqs', c_half, b_half)
    lower = jnp.tril(jnp.ones((SPAN, SPAN), dtype=bool))
    spread = cumul_heads[:, :, :, None] - cumul_heads[:, :, None, :]
    decay = jnp.exp(jnp.where(lower, spread, -jnp.inf))
    mixing = (inner[:, None] * decay * steps_heads[:, :, None, :]).astype(jnp.bfloat16)
    x_half = xvals.astype(jnp.bfloat16).reshape(blocks, SPAN, heads, -1)
    intra = contract('chqs,cshp->cqhp', mixing, x_half)
    ending = cumul[:, -1:, :]
    weights = jnp.exp(ending - cumul) * steps
    b_scaled = (weights[..., None] * b_half[:, :, None, :].astype(jnp.float32)).astype(jnp.bfloat16)
    pieces = contract('cqhn,cqhp->chnp', b_scaled, x_half)
    totals = ending[:, 0, :]

    def advance(carry, inputs):
        total, piece = inputs
        return (jnp.exp(total)[:, None, None] * carry + piece, carry)
    start = jnp.zeros((heads, bvals.shape[1], xvals.shape[1] // heads), jnp.float32)
    final, entries = lax.scan(advance, start, (totals, pieces))
    device_decay = jnp.exp(lax.optimization_barrier(jnp.sum(totals, axis=0)))
    prior_decay = jnp.exp(jnp.cumsum(totals, axis=0) - totals)
    return (intra, final, device_decay, c_half, jnp.exp(cumul), entries, prior_decay)

def carried_terms(c_half, exp_cumul, entries, prior_decay, start_state):
    full_state = entries + prior_decay[:, :, None, None] * start_state[None]
    product = jnp.einsum('cqn,chnp->cqhp', c_half.astype(jnp.float32), full_state, precision=lax.Precision.HIGHEST)
    return exp_cumul[..., None] * product

def branch_output(xvals, bvals, cvals, step_raw, step_bias, log_rate):
    intra, final, device_decay, c_half, exp_cumul, entries, prior_decay = local_terms(xvals, bvals, cvals, step_raw, step_bias, log_rate)
    carried = carried_terms(c_half, exp_cumul, entries, prior_decay, jnp.zeros_like(final))
    return (intra + carried).reshape(xvals.shape)

def mixer_core(fwd_x, rev_x, fwd_b, fwd_c, fwd_step, rev_b, rev_c, rev_step, step_bias, log_rate, skip_gain):
    groups = N_FSDP
    rows = fwd_x.shape[0]
    width = fwd_x.shape[1]
    heads = skip_gain.shape[0]
    group_width = width // groups
    group_heads = heads // groups

    def split_cols(value, per):
        return jnp.transpose(value.reshape(rows, groups, per), (1, 0, 2))
    items = (split_cols(fwd_x, group_width), split_cols(rev_x, group_width), split_cols(fwd_step, group_heads), split_cols(rev_step, group_heads), step_bias.reshape(groups, group_heads), log_rate.reshape(groups, group_heads))

    def one_group(member):
        fx, rx, fs, rs, bias_part, rate_part = member
        forward_y = branch_output(fx, fwd_b, fwd_c, fs, bias_part, rate_part)
        reverse_y = jnp.flip(branch_output(jnp.flip(rx, 0), jnp.flip(rev_b, 0), jnp.flip(rev_c, 0), jnp.flip(rs, 0), bias_part, rate_part), 0)
        return forward_y + reverse_y
    outputs = lax.map(one_group, items)
    mixed = jnp.transpose(outputs, (1, 0, 2)).reshape(rows, width)
    per_channel = jnp.repeat(skip_gain, width // heads)
    return mixed + per_channel * (fwd_x + rev_x)

def reference(token_ids, table, norm_gain, conv_weight, conv_bias, weight_b, weight_c, step_weight, step_bias, log_rate, skip_gain, out_grad):
    onehot = (token_ids[:, None] == jnp.arange(table.shape[0])[None, :]).astype(jnp.float32)
    embedded = jnp.dot(onehot, table, precision=lax.Precision.HIGHEST)

    def front(embedded, norm_gain, conv_weight, conv_bias):
        normed = make_normed(embedded, norm_gain)
        radius = conv_weight.shape[0] - 1
        padded = jnp.pad(normed, ((radius, radius), (0, 0)))
        return conv_pair(padded, conv_weight, conv_bias)
    (fwd_x, rev_x), front_back = jax.vjp(front, embedded, norm_gain, conv_weight, conv_bias)
    fwd_half = fwd_x.astype(jnp.bfloat16)
    rev_half = rev_x.astype(jnp.bfloat16)

    def project(half):
        return (jnp.dot(half, weight_b, preferred_element_type=jnp.float32), jnp.dot(half, weight_c, preferred_element_type=jnp.float32), jnp.dot(half, step_weight, preferred_element_type=jnp.float32))
    fwd_b, fwd_c, fwd_step = project(fwd_half)
    rev_b, rev_c, rev_step = project(rev_half)
    mixed, core_back = jax.vjp(mixer_core, fwd_x, rev_x, fwd_b, fwd_c, fwd_step, rev_b, rev_c, rev_step, step_bias, log_rate, skip_gain)
    grads = core_back(out_grad.astype(jnp.float32))
    d_fx, d_rx, d_fb, d_fc, d_fs, d_rb, d_rc, d_rs, d_bias, d_rate, d_skip = grads

    def project_back(half, d_b, d_c, d_s):
        b_half = d_b.astype(jnp.bfloat16)
        c_half = d_c.astype(jnp.bfloat16)
        s_half = d_s.astype(jnp.bfloat16)
        into_x = jnp.dot(b_half, weight_b.T, preferred_element_type=jnp.float32) + jnp.dot(c_half, weight_c.T, preferred_element_type=jnp.float32) + jnp.dot(s_half, step_weight.T, preferred_element_type=jnp.float32)
        return (into_x, jnp.dot(half.T, b_half, preferred_element_type=jnp.float32), jnp.dot(half.T, c_half, preferred_element_type=jnp.float32), jnp.dot(half.T, s_half, preferred_element_type=jnp.float32))
    into_f, gb_f, gc_f, gs_f = project_back(fwd_half, d_fb, d_fc, d_fs)
    into_r, gb_r, gc_r, gs_r = project_back(rev_half, d_rb, d_rc, d_rs)
    d_embedded, d_gain, d_cw, d_cb = front_back((d_fx + into_f, d_rx + into_r))
    grad_table = jnp.dot(onehot.T, d_embedded, precision=lax.Precision.HIGHEST)
    return (mixed.astype(jnp.bfloat16), d_embedded.astype(jnp.bfloat16), grad_table, d_gain, d_cw, d_cb, gb_f + gb_r, gc_f + gc_r, gs_f + gs_r, d_bias, d_rate, d_skip)
```

```python
import jax
import jax.numpy as jnp
from jax import lax
from jax.sharding import PartitionSpec as P
from jax.experimental import pallas as pl
from jax.experimental.pallas import tpu as pltpu

D = 4096
ROWS = 256
HEADS = 4
STATE = 128
GROUPS = 16
SLICES = 32
F32 = jnp.float32
BF16 = jnp.bfloat16
VMEM = pltpu.VMEM


def call(kernel, outs, *args):
    shapes = tuple(jax.ShapeDtypeStruct(shape, kind) for shape, kind in outs)
    return pl.pallas_call(kernel, out_shape=shapes, name=kernel.__name__)(*args)


def iota(shape, dim):
    return lax.broadcasted_iota(jnp.int32, shape, dim)


def mm(left, right):
    return lax.dot_general(left, right, (((1,), (0,)), ((), ())), preferred_element_type=F32)


def mm_tn(left, right):
    return lax.dot_general(left, right, (((0,), (0,)), ((), ())), preferred_element_type=F32)


def mm_nt(left, right):
    return lax.dot_general(left, right, (((1,), (1,)), ((), ())), preferred_element_type=F32)


def pieces(value, count):
    parts = []
    rest = value
    for _ in range(count):
        part = rest.astype(BF16)
        parts.append(part)
        rest = rest - part.astype(F32)
    return parts


def exact(form, left, right, count, split_left):
    total = None
    for part in pieces(left if split_left else right, count):
        term = form(part, right) if split_left else form(left, part)
        total = term if total is None else total + term
    return total


def head_masks(rows):
    lane_head = iota((rows, 256), 1) // 64
    return [lane_head == h for h in range(HEADS)]


def by_head(values, masks):
    out = values[3]
    for h in range(3):
        out = jnp.where(masks[h], values[h], out)
    return out


def expand(cols, first, masks):
    wide = [jnp.broadcast_to(cols[:, first + h : first + h + 1], (ROWS, 256)) for h in range(HEADS)]
    return by_head(wide, masks)


def columns(rows):
    missing = 128 - rows.shape[0]
    return jnp.transpose(jnp.concatenate([rows, jnp.zeros((missing, ROWS), F32)], axis=0))


def inclusive_masks():
    before = iota((ROWS, ROWS), 0) <= iota((ROWS, ROWS), 1)
    after = iota((ROWS, ROWS), 0) >= iota((ROWS, ROWS), 1)
    return jnp.where(before, 1.0, 0.0).astype(BF16), jnp.where(after, 1.0, 0.0).astype(BF16)


def tokens_kernel(ids, table, scale, gain, cw, cb, wbc, swx, xf, xr, gf, gr, send, oht_ref):
    normed = (table[...] * scale[...] * gain[...]).astype(BF16).astype(F32)
    vocab = iota((16, ROWS), 0)
    hits = [jnp.where(ids[o : o + 1, :] == vocab, 1.0, 0.0) for o in range(8)]
    oht = jnp.concatenate(hits, axis=0).astype(BF16)
    oht_ref[...] = oht
    none = jnp.zeros((16, 256), F32)
    taps = [cw[k : k + 1, :] * normed for k in range(4)]
    fwd_rows = jnp.concatenate([taps[3], taps[2], taps[1], taps[0], none, none, none, none], axis=0)
    rev_rows = jnp.concatenate([none, none, none, taps[0], taps[1], taps[2], taps[3], none], axis=0)
    halves = []
    for rows, x_ref, slope_ref in ((fwd_rows, xf, gf), (rev_rows, xr, gr)):
        pre = exact(mm_tn, oht, rows, 3, False) + cb[...]
        gate = 1.0 / (1.0 + jnp.exp(-pre))
        slope_ref[...] = gate * (1.0 + pre * (1.0 - gate))
        half = (pre * gate).astype(BF16)
        x_ref[...] = half
        halves.append(half)
    for member, half in enumerate(halves):
        part = mm(half, wbc[...]).astype(BF16).reshape(GROUPS, 16, 256)
        send[:, 0:16, member * 256 : member * 256 + 256] = part
    own = iota((128, 256), 0) % 8 < 4
    steps = jnp.where(own, mm_nt(swx[...], halves[0]), mm_nt(swx[...], halves[1]))
    high, low = pieces(steps, 2)
    send[:, 16:24, 0:256] = high.reshape(GROUPS, 8, 256)
    send[:, 16:24, 256:512] = low.reshape(GROUPS, 8, 256)


def reduce_kernel(got, bc, raw):
    total = got[0].astype(F32)
    for k in range(1, GROUPS):
        total = total + got[k].astype(F32)
    half = total[0:16].astype(BF16)
    bc[...] = jnp.broadcast_to(half[None], (GROUPS, 16, 512))
    raw[...] = total[16:24, 0:256] + total[16:24, 256:512]


def states_kernel(bc, raw, bias, rate, xf, xr, dy, send, cols_ref, rows_ref):
    shifted = raw[...] + bias[...]
    step = jnp.maximum(shifted, 0.0) + jnp.log1p(jnp.exp(-jnp.abs(shifted)))
    slope = 1.0 / (1.0 + jnp.exp(-shifted))
    logdec = -step * jnp.exp(rate[...])
    before, after = inclusive_masks()
    fwd_row = iota((8, ROWS), 0) < 4
    prefix = exact(mm, logdec, before, 3, True)
    suffix = exact(mm, logdec, after, 3, True)
    cumul = jnp.where(fwd_row, prefix, suffix)
    fwd_one = iota((8, 1), 0) < 4
    ending = jnp.where(fwd_one, prefix[:, ROWS - 1 : ROWS], suffix[:, 0:1])
    closing = jnp.exp(ending - cumul)
    weight = closing * step
    grown = jnp.exp(cumul)
    rows_ref[...] = jnp.concatenate([cumul, step, weight, closing, slope, logdec], axis=0)
    cols = columns(jnp.concatenate([cumul, step, weight, grown], axis=0))
    cols_ref[...] = cols
    masks = head_masks(ROWS)
    dyf = dy[...].astype(F32)
    found = []
    for br, x in ((0, xf), (1, xr)):
        b = bc[:, br * 256 : br * 256 + 128]
        c = bc[:, br * 256 + 128 : br * 256 + 256]
        weighted = (expand(cols, 16 + 4 * br, masks) * x[...].astype(F32)).astype(BF16)
        final = mm_tn(b, weighted)
        turned = (expand(cols, 24 + 4 * br, masks) * dyf).astype(BF16)
        found.append((final, mm_tn(c, turned)))
    chains = (found[0][0], found[1][1], found[1][0], found[0][1])
    for ch, state in enumerate(chains):
        for hp in range(2):
            part = state[:, hp * 128 : hp * 128 + 128].astype(BF16).reshape(16, 8, 128)
            send[:, hp, ch * 8 : ch * 8 + 8, :] = part
    decay = jnp.exp(ending)
    left = iota((1, 128), 1) < 64
    row = iota((8, 128), 0)
    for hp in range(2):
        fd = jnp.where(left, decay[2 * hp : 2 * hp + 1], decay[2 * hp + 1 : 2 * hp + 2])
        rd = jnp.where(left, decay[4 + 2 * hp : 5 + 2 * hp], decay[5 + 2 * hp : 6 + 2 * hp])
        f_high = fd.astype(BF16).astype(F32)
        r_high = rd.astype(BF16).astype(F32)
        packed = jnp.where(row == 0, f_high, 0.0)
        packed = jnp.where(row == 1, fd - f_high, packed)
        packed = jnp.where(row == 2, r_high, packed)
        packed = jnp.where(row == 3, rd - r_high, packed)
        send[:, hp, 32:40, :] = jnp.broadcast_to(packed.astype(BF16)[None], (16, 8, 128))


def chain_kernel(got, out):
    decays = got[:, 32:40, :].astype(F32)
    fwd_decay = decays[:, 0:1, :] + decays[:, 1:2, :]
    rev_decay = decays[:, 2:3, :] + decays[:, 3:4, :]
    up_f = jnp.zeros((8, 128), F32)
    up_r = jnp.zeros((8, 128), F32)
    down_r = jnp.zeros((8, 128), F32)
    down_f = jnp.zeros((8, 128), F32)
    for i in range(SLICES):
        out[i, 0:16, :] = jnp.concatenate([up_f, up_r], axis=0).astype(BF16)
        here = got[i, 0:16, :].astype(F32)
        up_f = fwd_decay[i] * up_f + here[0:8]
        up_r = rev_decay[i] * up_r + here[8:16]
        j = SLICES - 1 - i
        out[j, 16:32, :] = jnp.concatenate([down_r, down_f], axis=0).astype(BF16)
        there = got[j, 16:32, :].astype(F32)
        down_r = rev_decay[j] * down_r + there[0:8]
        down_f = fwd_decay[j] * down_f + there[8:16]


def within_kernel(bc, cols_ref, rows_ref, xf, xr, dy, skip, y_ref, dxf, dxr, dbc, side, line):
    masks = head_masks(ROWS)
    t_at = iota((ROWS, ROWS), 0)
    s_at = iota((ROWS, ROWS), 1)
    lane = iota((ROWS, 128), 1)
    cols = cols_ref[...]
    dyh = dy[...]
    dyf = dyh.astype(F32)
    nothing = jnp.zeros((ROWS, 256), BF16)
    direct = skip[...] * dyf
    total = skip[...] * (xf[...].astype(F32) + xr[...].astype(F32))
    side_acc = jnp.zeros((ROWS, 128), F32)
    lines = []
    for br, x, dx_ref in ((0, xf, dxf), (1, xr, dxr)):
        xh = x[...]
        b = bc[:, br * 256 : br * 256 + 128]
        c = bc[:, br * 256 + 128 : br * 256 + 256]
        inner = mm_nt(c, b)
        causal = t_at >= s_at if br == 0 else t_at <= s_at
        dinner = jnp.zeros((ROWS, ROWS), F32)
        intra = []
        back = []
        for h in range(HEADS):
            at = 4 * br + h
            spread = cols[:, at : at + 1] - rows_ref[at : at + 1, :]
            decay = jnp.exp(jnp.where(causal, spread, -jnp.inf))
            step = rows_ref[8 + at : 9 + at, :]
            paced = decay * step
            mixing = (inner * paced).astype(BF16)
            intra.append(mm(mixing, xh))
            back.append(mm_tn(mixing, dyh))
            dmix = mm_nt(jnp.where(masks[h], dyh, nothing), xh)
            dinner = dinner + dmix * paced
            reach = dmix * decay * inner
            lines.append(jnp.sum(reach, axis=0, keepdims=True))
            flow = jnp.sum(reach * step, axis=1, keepdims=True)
            side_acc = jnp.where(lane == at, flow, side_acc)
        total = total + by_head(intra, masks)
        dx_ref[...] = direct + by_head(back, masks)
        dhalf = dinner.astype(BF16)
        dbc[:, br * 256 : br * 256 + 128] = mm_tn(dhalf, c)
        dbc[:, br * 256 + 128 : br * 256 + 256] = mm(dhalf, b)
    y_ref[...] = total
    side[...] = jnp.transpose(side_acc)[0:8]
    line[...] = jnp.concatenate(lines, axis=0)


def carried_kernel(
    got, bc, cols_ref, rows_ref, xf, xr, dy, y0, dxf0, dxr0, dbc0, side, line, rate,
    out, dxf, dxr, send, draw_ref, small,
):
    masks = head_masks(ROWS)
    cols = cols_ref[...]
    dyf = dy[...].astype(F32)

    def state(ch):
        halves = [
            got[:, hp, ch * 8 : ch * 8 + 8, :].astype(F32).reshape(STATE, 128) for hp in range(2)
        ]
        return jnp.concatenate(halves, axis=1)

    row_at = iota((8, 256), 0)
    lane_head = iota((8, 256), 1) // 64
    total = y0[...]
    dp = jnp.zeros((8, ROWS), F32)
    dw = jnp.zeros((8, ROWS), F32)
    d_end = jnp.zeros((8, 1), F32)
    for br, x, dx0, dx_ref, at_state, at_grad in ((0, xf, dxf0, dxf, 0, 3), (1, xr, dxr0, dxr, 2, 1)):
        start = state(at_state)
        ahead = state(at_grad)
        start_half = start.astype(BF16)
        ahead_half = ahead.astype(BF16)
        b = bc[:, br * 256 : br * 256 + 128]
        c = bc[:, br * 256 + 128 : br * 256 + 256]
        grown = expand(cols, 24 + 4 * br, masks)
        weight = expand(cols, 16 + 4 * br, masks)
        heads = jnp.where(lane_head + 4 * br == row_at, 1.0, 0.0).astype(BF16)
        carried = grown * mm(c, start_half)
        total = total + carried
        dp = dp + exact(mm_nt, heads, dyf * carried, 2, False)
        xv = x[...].astype(F32)
        toward = mm(b, ahead_half)
        dx_ref[...] = dx0[...] + weight * toward
        dw = dw + exact(mm_nt, heads, xv * toward, 2, False)
        dc = mm_nt((grown * dyf).astype(BF16), start_half)
        db = mm_nt((weight * xv).astype(BF16), ahead_half)
        at = br * 256
        send[:, :, at : at + 128] = (dbc0[:, at : at + 128] + db).astype(BF16).reshape(16, 16, 128)
        send[:, :, at + 128 : at + 256] = (
            (dbc0[:, at + 128 : at + 256] + dc).astype(BF16).reshape(16, 16, 128)
        )
        both = jnp.sum(start * ahead, axis=0, keepdims=True)
        spread = jnp.where(lane_head + 4 * br == row_at, both, 0.0)
        d_end = d_end + jnp.sum(spread, axis=1, keepdims=True)
    out[...] = total.astype(BF16)
    cumul = rows_ref[0:8]
    step = rows_ref[8:16]
    weight = rows_ref[16:24]
    closing = rows_ref[24:32]
    slope = rows_ref[32:40]
    logdec = rows_ref[40:48]
    at = iota((8, ROWS), 1)
    row = iota((8, ROWS), 0)
    last = at == jnp.where(row < 4, ROWS - 1, 0)
    pull = dw * weight
    ending = jnp.sum(jnp.where(last, cumul, 0.0), axis=1, keepdims=True)
    d_end = jnp.exp(ending) * d_end + jnp.sum(pull, axis=1, keepdims=True)
    dcumul = side[...] - step * line[...] + dp - pull + jnp.where(last, d_end, 0.0)
    before, after = inclusive_masks()
    prefix = exact(mm, dcumul, before, 3, True)
    suffix = exact(mm, dcumul, after, 3, True)
    dlog = jnp.where(row < 4, suffix, prefix)
    dstep = line[...] + dw * closing - dlog * jnp.exp(rate[...])
    draw = dstep * slope
    draw_ref[...] = draw.astype(BF16)
    d_bias = jnp.sum(draw, axis=1, keepdims=True)
    d_rate = jnp.sum(dlog * logdec, axis=1, keepdims=True)
    first = iota((1, 256), 1)
    bias_row = jnp.zeros((1, 256), F32)
    rate_row = jnp.zeros((1, 256), F32)
    for h in range(HEADS):
        bias_row = jnp.where(first == 64 * h, d_bias[h : h + 1] + d_bias[h + 4 : h + 5], bias_row)
        rate_row = jnp.where(first == 64 * h, d_rate[h : h + 1] + d_rate[h + 4 : h + 5], rate_row)
    skip_row = jnp.sum(dyf * (xf[...].astype(F32) + xr[...].astype(F32)), axis=0, keepdims=True)
    none = jnp.zeros((5, 256), F32)
    small[...] = jnp.concatenate([skip_row, bias_row, rate_row, none], axis=0)


def total_kernel(got, draw, send):
    total = got[0].astype(F32)
    for k in range(1, GROUPS):
        total = total + got[k].astype(F32)
    send[:, 0:16, :] = jnp.broadcast_to(total.astype(BF16)[None], (GROUPS, 16, 512))
    padded = jnp.concatenate([draw[...].astype(F32), jnp.zeros((8, 256), F32)], axis=1)
    send[:, 16:24, :] = jnp.broadcast_to(padded.astype(BF16)[None], (GROUPS, 8, 512))


def project_back_kernel(
    got, xf, xr, gf, gr, dxf, dxr, wbc, sw, oht, table, scale, gain, small,
    dpf, dpr, to_prev, to_next, grads, lines,
):
    dbc = got[:, 0:16, :].reshape(ROWS, 512)
    draw = got[:, 16:24, 0:256].astype(F32).reshape(128, 256).astype(BF16)
    pick_row = iota((128, 64), 0)
    pick_col = iota((128, 64), 1)
    wanted = pick_row // 8 * 4 + pick_row % 4
    normed = (table[...] * scale[...] * gain[...]).astype(BF16).astype(F32)
    taps = [jnp.zeros((1, 256), F32)] * 4
    bias_row = jnp.zeros((1, 256), F32)
    wide = jnp.zeros((256, 256), F32)
    thin = jnp.zeros((256, 64), F32)
    for br, x, slope, dx, out in ((0, xf, gf, dxf, dpf), (1, xr, gr, dxr, dpr)):
        mine = (wanted == pick_col) & ((pick_row % 8 < 4) == (br == 0))
        dstep = mm_tn(draw, jnp.where(mine, 1.0, 0.0).astype(BF16)).astype(BF16)
        half = dbc[:, br * 256 : br * 256 + 256]
        into = mm_nt(half, wbc[...]) + mm_nt(dstep, sw[...])
        whole = (dx[...] + into).astype(BF16).astype(F32)
        dpre = whole * slope[...]
        out[...] = dpre
        wide = wide + mm_tn(x[...], half)
        thin = thin + mm_tn(x[...], dstep)
        sums = exact(mm, oht[...], dpre, 2, False)
        for k in range(4):
            o = 3 - k if br == 0 else 3 + k
            part = jnp.sum(normed * sums[16 * o : 16 * o + 16], axis=0, keepdims=True)
            taps[k] = taps[k] + part
        bias_row = bias_row + jnp.sum(dpre, axis=0, keepdims=True)
    to_prev[...] = dpf[0:8]
    to_next[...] = dpr[ROWS - 8 : ROWS]
    grads[:, 0:256] = wide
    grads[:, 256:384] = jnp.concatenate([thin, jnp.zeros((256, 64), F32)], axis=1)
    lines[...] = jnp.concatenate(taps + [bias_row, small[0:3]], axis=0)


def normed_kernel(
    dpf, dpr, from_next, from_prev, cw, gain, table, oht, grads, lines,
    gn_ref, cross, send, ahead, behind,
):
    ahead[0:ROWS] = dpf[...]
    ahead[ROWS : ROWS + 8] = from_next[...]
    behind[0:8] = from_prev[...]
    behind[8 : ROWS + 8] = dpr[...]
    dn = jnp.zeros((ROWS, 256), F32)
    for k in range(4):
        dn = dn + cw[k : k + 1] * (ahead[k : k + ROWS] + behind[8 - k : 8 - k + ROWS])
    gn = dn.astype(BF16)
    gn_ref[...] = gn
    own = oht[48:64]
    sums = mm(own, gn)
    rated = exact(mm_tn, own, table[...] * gain[...], 3, False)
    ones = jnp.ones((8, 256), BF16)
    cross[...] = jnp.broadcast_to(
        exact(mm_nt, ones, gn.astype(F32) * rated, 3, False)[None], (GROUPS, 8, ROWS)
    )
    stacked = jnp.concatenate(
        [jnp.zeros((64, 256), F32), sums, lines[...], jnp.zeros((40, 256), F32)], axis=0
    )
    last = grads[:, 256:384] + jnp.transpose(stacked)
    send[:, 0:8, :] = grads[:, 0:128].astype(BF16).reshape(SLICES, 8, 128)
    send[:, 8:16, :] = grads[:, 128:256].astype(BF16).reshape(SLICES, 8, 128)
    send[:, 16:24, :] = last.astype(BF16).reshape(SLICES, 8, 128)


def embedded_kernel(got, gn, gain, table, scale, oht, out, counts):
    total = got[0]
    for k in range(1, GROUPS):
        total = total + got[k]
    cross = columns(total)[:, 0:1]
    own = oht[48:64]
    unit = scale[...]
    turned = exact(mm_tn, own, unit * gain[...], 3, False)
    shrunk = exact(mm_tn, own, table[...] * (unit * unit * unit / D), 3, False)
    out[...] = (turned * gn[...].astype(F32) - shrunk * cross).astype(BF16)
    counts[...] = exact(mm_nt, own, total, 3, False)


def gather_kernel(got, send):
    total = got[0].astype(F32)
    for k in range(1, SLICES):
        total = total + got[k].astype(F32)
    send[...] = jnp.broadcast_to(total.astype(BF16)[None], (SLICES, 24, 128))


def finish_kernel(got, counts, table, scale, gain, gt, gg, gcw, gcb, gwb, gwc, gsw, heads):
    gwb[...] = got[:, 0:8, :].astype(F32).reshape(256, 128)
    gwc[...] = got[:, 8:16, :].astype(F32).reshape(256, 128)
    last = got[:, 16:24, :].astype(F32).reshape(256, 128)
    gsw[...] = last[:, 0:64]
    rows = jnp.transpose(last)
    sums = rows[64:80]
    crossed = counts[0]
    for k in range(1, SLICES):
        crossed = crossed + counts[k]
    unit = scale[...]
    shrunk = table[...] * (unit * unit * unit / D) * crossed[:, 0:1]
    gt[...] = unit * gain[...] * sums - shrunk
    gg[...] = jnp.sum(table[...] * unit * sums, axis=0, keepdims=True)
    gcw[...] = rows[80:84]
    gcb[...] = rows[84:85]
    lane = iota((8, 256), 1)
    tail = rows[80:88]
    picked = iota((8, 128), 1)
    result = jnp.zeros((8, 128), F32)
    for h in range(HEADS):
        part = jnp.sum(jnp.where(lane // 64 == h, tail, 0.0), axis=1, keepdims=True)
        result = jnp.where(picked == h, part, result)
    heads[...] = result


def swap(value, axis):
    return lax.all_to_all(value, axis, 0, 0, tiled=True)


def local(
    token_ids,
    table,
    norm_gain,
    conv_weight,
    conv_bias,
    weight_b,
    weight_c,
    step_weight,
    step_bias,
    log_rate,
    skip_gain,
    out_grad,
):
    size = lax.axis_size("ctx")
    up = [(i, i + 1) for i in range(size - 1)]
    down = [(i + 1, i) for i in range(size - 1)]
    marked = token_ids + 1
    before = lax.ppermute(marked[-3:], "ctx", up)
    after = lax.ppermute(marked[:3], "ctx", down)
    squares = jnp.sum(table * table, axis=1)
    spread = jnp.broadcast_to(squares[None, None, :], (GROUPS, 1, 16))
    spread = jnp.pad(spread, ((0, 0), (0, 0), (0, 112)))
    square_sums = jnp.sum(swap(spread, "fsdp"), axis=(0, 1))[:16]
    scale = lax.rsqrt(square_sums / D + 1e-05)[:, None]
    reach = jnp.concatenate([before, marked, after]) - 1
    ids = jnp.stack([reach[o : o + ROWS] for o in range(7)] + [jnp.full((ROWS,), -1, jnp.int32)])
    gain = norm_gain[None]
    wbc = jnp.concatenate([weight_b, weight_c], axis=1)
    heads_first = jnp.transpose(step_weight).reshape(GROUPS, HEADS, 256)
    swx = jnp.concatenate([heads_first, heads_first], axis=1).reshape(128, 256)
    bias = jnp.tile(step_bias, 2)[:, None]
    rate = jnp.tile(log_rate, 2)[:, None]
    skip = jnp.repeat(skip_gain, 64)[None]

    square = ((ROWS, 256), F32)
    half_square = ((ROWS, 256), BF16)
    xf, xr, gf, gr, part, oht = call(
        tokens_kernel,
        (
            half_square,
            half_square,
            square,
            square,
            ((GROUPS, 24, 512), BF16),
            ((128, 256), BF16),
        ),
        ids, table, scale, gain, conv_weight, conv_bias[None], wbc, swx,
    )
    bc, raw = call(
        reduce_kernel, (((GROUPS, 16, 512), BF16), ((8, 256), F32)), swap(part, "fsdp")
    )
    bc = swap(bc, "fsdp").reshape(ROWS, 512)
    states, cols, rows = call(
        states_kernel,
        (((16, 2, 40, 128), BF16), ((ROWS, 128), F32), ((48, ROWS), F32)),
        bc, raw, bias, rate, xf, xr, out_grad,
    )
    arrived = swap(states.reshape(SLICES, 40, 128), "ctx")
    y0, dxf0, dxr0, dbc0, side, line = call(
        within_kernel,
        (square, square, square, ((ROWS, 512), F32), ((8, ROWS), F32), ((8, ROWS), F32)),
        bc, cols, rows, xf, xr, out_grad, skip,
    )
    (entering,) = call(chain_kernel, (((SLICES, 32, 128), BF16),), arrived)
    entering = swap(entering, "ctx").reshape(16, 2, 32, 128)
    mixer_out, dxf, dxr, dpart, draw, small = call(
        carried_kernel,
        (
            half_square,
            square,
            square,
            ((GROUPS, 16, 512), BF16),
            ((8, 256), BF16),
            ((8, 256), F32),
        ),
        entering, bc, cols, rows, xf, xr, out_grad, y0, dxf0, dxr0, dbc0, side, line, rate,
    )
    (totals,) = call(total_kernel, (((GROUPS, 24, 512), BF16),), swap(dpart, "fsdp"), draw)
    edge = ((8, 256), F32)
    dpf, dpr, to_prev, to_next, grads, lines = call(
        project_back_kernel,
        (square, square, edge, edge, ((256, 384), F32), edge),
        swap(totals, "fsdp"), xf, xr, gf, gr, dxf, dxr, wbc, step_weight, oht, table, scale, gain, small,
    )
    from_next = lax.ppermute(to_prev, "ctx", down)
    from_prev = lax.ppermute(to_next, "ctx", up)
    gn, cross, gsend = pl.pallas_call(
        normed_kernel,
        out_shape=(
            jax.ShapeDtypeStruct((ROWS, 256), BF16),
            jax.ShapeDtypeStruct((GROUPS, 8, ROWS), F32),
            jax.ShapeDtypeStruct((SLICES, 24, 128), BF16),
        ),
        scratch_shapes=[VMEM((ROWS + 8, 256), F32), VMEM((ROWS + 8, 256), F32)],
        name="normed_kernel",
    )(dpf, dpr, from_next, from_prev, conv_weight, gain, table, oht, grads, lines)
    grad_embedded, counts = call(
        embedded_kernel,
        (half_square, ((16, 8), F32)),
        swap(cross, "fsdp"), gn, gain, table, scale, oht,
    )
    (gathered,) = call(gather_kernel, (((SLICES, 24, 128), BF16),), swap(gsend, "ctx"))
    counts = jnp.broadcast_to(counts[None], (SLICES, 16, 8))
    outs = call(
        finish_kernel,
        (
            ((16, 256), F32),
            ((1, 256), F32),
            ((4, 256), F32),
            ((1, 256), F32),
            ((256, 128), F32),
            ((256, 128), F32),
            ((256, 64), F32),
            ((8, 128), F32),
        ),
        swap(gathered, "ctx"), swap(counts, "ctx"), table, scale, gain,
    )
    gt, gg, gcw, gcb, gwb, gwc, gsw, heads = outs
    return (
        mixer_out,
        grad_embedded,
        gt,
        gg[0],
        gcw,
        gcb[0],
        gwb,
        gwc,
        gsw,
        heads[6, :HEADS],
        heads[7, :HEADS],
        heads[5, :HEADS],
    )


def solution(mesh):
    return jax.shard_map(
        local,
        mesh=mesh,
        in_specs=(
            P("ctx"),
            P(None, "fsdp"),
            P("fsdp"),
            P(None, "fsdp"),
            P("fsdp"),
            P("fsdp", None),
            P("fsdp", None),
            P("fsdp", None),
            P("fsdp"),
            P("fsdp"),
            P("fsdp"),
            P("ctx", "fsdp"),
        ),
        out_specs=(
            P("ctx", "fsdp"),
            P("ctx", "fsdp"),
            P(None, "fsdp"),
            P("fsdp"),
            P(None, "fsdp"),
            P("fsdp"),
            P("fsdp", None),
            P("fsdp", None),
            P("fsdp", None),
            P("fsdp"),
            P("fsdp"),
            P("fsdp"),
        ),
        check_vma=False,
    )
```

```python
import jax
import jax.numpy as jnp
from jax import lax
from jax.sharding import PartitionSpec as P
from jax.experimental import pallas as pl
from jax.experimental.pallas import tpu as pltpu

D = 4096
ROWS = 256
HEADS = 4
STATE = 128
GROUPS = 16
SLICES = 32
F32 = jnp.float32
BF16 = jnp.bfloat16
VMEM = pltpu.VMEM


def call(kernel, outs, *args, final=(), scratch=()):
    shapes = tuple(
        jax.ShapeDtypeStruct(shape, kind) if i in final else VMEM(shape, kind)
        for i, (shape, kind) in enumerate(outs)
    )
    near = [pltpu.with_memory_space_constraint(arg, VMEM) for arg in args]
    return pl.pallas_call(
        kernel,
        out_shape=shapes,
        scratch_shapes=scratch,
        compiler_params=pltpu.CompilerParams(vmem_limit_bytes=24 << 20),
    )(*near)


def iota(shape, dim):
    return lax.broadcasted_iota(jnp.int32, shape, dim)


def mm(left, right):
    return lax.dot_general(left, right, (((1,), (0,)), ((), ())), preferred_element_type=F32)


def mm_tn(left, right):
    return lax.dot_general(left, right, (((0,), (0,)), ((), ())), preferred_element_type=F32)


def mm_nt(left, right):
    return lax.dot_general(left, right, (((1,), (1,)), ((), ())), preferred_element_type=F32)


def pieces(value, count):
    parts = []
    rest = value
    for _ in range(count):
        part = rest.astype(BF16)
        parts.append(part)
        rest = rest - part.astype(F32)
    return parts


def exact(form, left, right, count, split_left):
    total = None
    for part in pieces(left if split_left else right, count):
        term = form(part, right) if split_left else form(left, part)
        total = term if total is None else total + term
    return total


def head_masks(rows):
    lane_head = iota((rows, 256), 1) // 64
    return [lane_head == h for h in range(HEADS)]


def by_head(values, masks):
    out = values[3]
    for h in range(3):
        out = jnp.where(masks[h], values[h], out)
    return out


def expand(cols, first, masks):
    wide = [jnp.broadcast_to(cols[:, first + h : first + h + 1], (ROWS, 256)) for h in range(HEADS)]
    return by_head(wide, masks)


def columns(rows):
    missing = 128 - rows.shape[0]
    return jnp.transpose(jnp.concatenate([rows, jnp.zeros((missing, ROWS), F32)], axis=0))


def inclusive_masks():
    before = iota((ROWS, ROWS), 0) <= iota((ROWS, ROWS), 1)
    after = iota((ROWS, ROWS), 0) >= iota((ROWS, ROWS), 1)
    return jnp.where(before, 1.0, 0.0).astype(BF16), jnp.where(after, 1.0, 0.0).astype(BF16)


def squares_kernel(table, send):
    squares = jnp.concatenate([table[...] * table[...], jnp.zeros((112, 256), F32)], axis=0)
    sums = exact(mm_nt, jnp.ones((8, 256), BF16), squares, 3, False)
    send[...] = jnp.broadcast_to(sums[0:1][None], (GROUPS, 1, 128))


def tokens_kernel(
    ids, ids_prev, ids_next, got, table, gain, cw, cb, wbc, swx,
    xf, xr, gf, gr, send, oht_ref, scale,
):
    total = got[0]
    for k in range(1, GROUPS):
        total = total + got[k]
    unit = lax.rsqrt(total / D + 1e-05)
    spread = jnp.transpose(jnp.broadcast_to(unit, (128, 128)))[0:16]
    scale[...] = spread
    unit = spread[:, 0:1]
    normed = (table[...] * unit * gain[...]).astype(BF16).astype(F32)
    vocab = iota((16, ROWS), 0) + 1
    lane = iota((1, ROWS), 1)
    here = ids[...]
    hits = []
    for o in range(7):
        d = o - 3
        if d == 0:
            moved = here
        elif d > 0:
            ahead = pltpu.roll(ids_next[...], ROWS - d, 1)
            moved = jnp.where(lane < ROWS - d, pltpu.roll(here, ROWS - d, 1), ahead)
        else:
            moved = jnp.where(lane >= -d, pltpu.roll(here, -d, 1), pltpu.roll(ids_prev[...], -d, 1))
        hits.append(jnp.where(moved == vocab, 1.0, 0.0))
    hits.append(jnp.zeros((16, ROWS), F32))
    oht = jnp.concatenate(hits, axis=0).astype(BF16)
    oht_ref[...] = oht
    none = jnp.zeros((16, 256), F32)
    taps = [cw[k : k + 1, :] * normed for k in range(4)]
    fwd_rows = jnp.concatenate([taps[3], taps[2], taps[1], taps[0], none, none, none, none], axis=0)
    rev_rows = jnp.concatenate([none, none, none, taps[0], taps[1], taps[2], taps[3], none], axis=0)
    halves = []
    for rows, x_ref, slope_ref in ((fwd_rows, xf, gf), (rev_rows, xr, gr)):
        pre = exact(mm_tn, oht, rows, 3, False) + cb[...]
        gate = 1.0 / (1.0 + jnp.exp(-pre))
        slope_ref[...] = gate * (1.0 + pre * (1.0 - gate))
        half = (pre * gate).astype(BF16)
        x_ref[...] = half
        halves.append(half)
    for member, half in enumerate(halves):
        part = mm(half, wbc[...]).astype(BF16).reshape(GROUPS, 16, 256)
        send[:, 0:16, member * 256 : member * 256 + 256] = part
    own = iota((128, 256), 0) % 8 < 4
    steps = jnp.where(own, mm_nt(swx[...], halves[0]), mm_nt(swx[...], halves[1]))
    high, low = pieces(steps, 2)
    send[:, 16:24, 0:256] = high.reshape(GROUPS, 8, 256)
    send[:, 16:24, 256:512] = low.reshape(GROUPS, 8, 256)


def reduce_kernel(got, bc, raw):
    total = got[0].astype(F32)
    for k in range(1, GROUPS):
        total = total + got[k].astype(F32)
    half = total[0:16].astype(BF16)
    bc[...] = jnp.broadcast_to(half[None], (GROUPS, 16, 512))
    raw[...] = total[16:24, 0:256] + total[16:24, 256:512]


def steps_kernel(
    raw, bias, rate, xf, xr, dy,
    cols_ref, rows_ref, weight_ref, grown_ref, weighted_ref, turned_ref, packed_ref,
):
    shifted = raw[...] + bias[...]
    step = jnp.maximum(shifted, 0.0) + jnp.log1p(jnp.exp(-jnp.abs(shifted)))
    slope = 1.0 / (1.0 + jnp.exp(-shifted))
    logdec = -step * jnp.exp(rate[...])
    before, after = inclusive_masks()
    fwd_row = iota((8, ROWS), 0) < 4
    prefix = exact(mm, logdec, before, 3, True)
    suffix = exact(mm, logdec, after, 3, True)
    cumul = jnp.where(fwd_row, prefix, suffix)
    fwd_one = iota((8, 1), 0) < 4
    ending = jnp.where(fwd_one, prefix[:, ROWS - 1 : ROWS], suffix[:, 0:1])
    closing = jnp.exp(ending - cumul)
    weight = closing * step
    grown = jnp.exp(cumul)
    rows_ref[...] = jnp.concatenate([cumul, step, weight, closing, slope, logdec], axis=0)
    cols = columns(jnp.concatenate([cumul, step, weight, grown], axis=0))
    cols_ref[...] = cols
    masks = head_masks(ROWS)
    dyf = dy[...].astype(F32)
    for br, x in ((0, xf), (1, xr)):
        weight_wide = expand(cols, 16 + 4 * br, masks)
        grown_wide = expand(cols, 24 + 4 * br, masks)
        weight_ref[br] = weight_wide
        grown_ref[br] = grown_wide
        weighted_ref[br] = (weight_wide * x[...].astype(F32)).astype(BF16)
        turned_ref[br] = (grown_wide * dyf).astype(BF16)
    decay = jnp.exp(ending)
    left = iota((1, 128), 1) < 64
    row = iota((8, 128), 0)
    for hp in range(2):
        fd = jnp.where(left, decay[2 * hp : 2 * hp + 1], decay[2 * hp + 1 : 2 * hp + 2])
        rd = jnp.where(left, decay[4 + 2 * hp : 5 + 2 * hp], decay[5 + 2 * hp : 6 + 2 * hp])
        f_high = fd.astype(BF16).astype(F32)
        r_high = rd.astype(BF16).astype(F32)
        packed = jnp.where(row == 0, f_high, 0.0)
        packed = jnp.where(row == 1, fd - f_high, packed)
        packed = jnp.where(row == 2, r_high, packed)
        packed = jnp.where(row == 3, rd - r_high, packed)
        packed_ref[hp] = packed


def states_kernel(bc, weighted, turned, packed, send):
    found = []
    for br in range(2):
        b = bc[:, br * 256 : br * 256 + 128]
        c = bc[:, br * 256 + 128 : br * 256 + 256]
        found.append((mm_tn(b, weighted[br]), mm_tn(c, turned[br])))
    chains = (found[0][0], found[1][1], found[1][0], found[0][1])
    for ch, state in enumerate(chains):
        for hp in range(2):
            part = state[:, hp * 128 : hp * 128 + 128].astype(BF16).reshape(16, 8, 128)
            send[:, hp, ch * 8 : ch * 8 + 8, :] = part
    for hp in range(2):
        send[:, hp, 32:40, :] = jnp.broadcast_to(packed[hp].astype(BF16)[None], (16, 8, 128))


def chain_kernel(got, out):
    decays = got[:, 32:40, :].astype(F32)
    fwd_decay = decays[:, 0:1, :] + decays[:, 1:2, :]
    rev_decay = decays[:, 2:3, :] + decays[:, 3:4, :]
    up_f = jnp.zeros((8, 128), F32)
    up_r = jnp.zeros((8, 128), F32)
    down_r = jnp.zeros((8, 128), F32)
    down_f = jnp.zeros((8, 128), F32)
    for i in range(SLICES):
        out[i, 0:16, :] = jnp.concatenate([up_f, up_r], axis=0).astype(BF16)
        here = got[i, 0:16, :].astype(F32)
        up_f = fwd_decay[i] * up_f + here[0:8]
        up_r = rev_decay[i] * up_r + here[8:16]
        j = SLICES - 1 - i
        out[j, 16:32, :] = jnp.concatenate([down_r, down_f], axis=0).astype(BF16)
        there = got[j, 16:32, :].astype(F32)
        down_r = rev_decay[j] * down_r + there[0:8]
        down_f = fwd_decay[j] * down_f + there[8:16]


def within_kernel(bc, cols_ref, rows_ref, xf, xr, dy, skip, y_ref, dxf, dxr, dbc, side, line):
    masks = head_masks(ROWS)
    t_at = iota((ROWS, ROWS), 0)
    s_at = iota((ROWS, ROWS), 1)
    lane = iota((ROWS, 128), 1)
    cols = cols_ref[...]
    dyh = dy[...]
    dyf = dyh.astype(F32)
    nothing = jnp.zeros((ROWS, 256), BF16)
    direct = skip[...] * dyf
    total = skip[...] * (xf[...].astype(F32) + xr[...].astype(F32))
    side_acc = jnp.zeros((ROWS, 128), F32)
    lines = []
    for br, x, dx_ref in ((0, xf, dxf), (1, xr, dxr)):
        xh = x[...]
        b = bc[:, br * 256 : br * 256 + 128]
        c = bc[:, br * 256 + 128 : br * 256 + 256]
        inner = mm_nt(c, b)
        causal = t_at >= s_at if br == 0 else t_at <= s_at
        dinner = jnp.zeros((ROWS, ROWS), F32)
        intra = []
        back = []
        for h in range(HEADS):
            at = 4 * br + h
            spread = cols[:, at : at + 1] - rows_ref[at : at + 1, :]
            decay = jnp.exp(jnp.where(causal, spread, -jnp.inf))
            step = rows_ref[8 + at : 9 + at, :]
            paced = decay * step
            mixing = (inner * paced).astype(BF16)
            intra.append(mm(mixing, xh))
            back.append(mm_tn(mixing, dyh))
            dmix = mm_nt(jnp.where(masks[h], dyh, nothing), xh)
            dinner = dinner + dmix * paced
            reach = dmix * decay * inner
            lines.append(jnp.sum(reach, axis=0, keepdims=True))
            flow = jnp.sum(reach * step, axis=1, keepdims=True)
            side_acc = jnp.where(lane == at, flow, side_acc)
        total = total + by_head(intra, masks)
        dx_ref[...] = direct + by_head(back, masks)
        dhalf = dinner.astype(BF16)
        dbc[:, br * 256 : br * 256 + 128] = mm_tn(dhalf, c)
        dbc[:, br * 256 + 128 : br * 256 + 256] = mm(dhalf, b)
    y_ref[...] = total
    side[...] = jnp.transpose(side_acc)[0:8]
    line[...] = jnp.concatenate(lines, axis=0)


def carried_kernel(
    got, bc, weight_ref, grown_ref, weighted, turned, rows_ref, xf, xr, dy,
    y0, dxf0, dxr0, dbc0, side, line, rate,
    out, dxf, dxr, send, draw_ref, small,
):
    dyf = dy[...].astype(F32)

    def state(ch):
        halves = [
            got[:, hp, ch * 8 : ch * 8 + 8, :].astype(F32).reshape(STATE, 128) for hp in range(2)
        ]
        return jnp.concatenate(halves, axis=1)

    row_at = iota((8, 256), 0)
    lane_head = iota((8, 256), 1) // 64
    total = y0[...]
    dp = jnp.zeros((8, ROWS), F32)
    dw = jnp.zeros((8, ROWS), F32)
    d_end = jnp.zeros((8, 1), F32)
    for br, x, dx0, dx_ref, at_state, at_grad in ((0, xf, dxf0, dxf, 0, 3), (1, xr, dxr0, dxr, 2, 1)):
        start = state(at_state)
        ahead = state(at_grad)
        start_half = start.astype(BF16)
        ahead_half = ahead.astype(BF16)
        b = bc[:, br * 256 : br * 256 + 128]
        c = bc[:, br * 256 + 128 : br * 256 + 256]
        heads = jnp.where(lane_head + 4 * br == row_at, 1.0, 0.0).astype(BF16)
        carried = grown_ref[br] * mm(c, start_half)
        total = total + carried
        dp = dp + exact(mm_nt, heads, dyf * carried, 2, False)
        xv = x[...].astype(F32)
        toward = mm(b, ahead_half)
        dx_ref[...] = dx0[...] + weight_ref[br] * toward
        dw = dw + exact(mm_nt, heads, xv * toward, 2, False)
        dc = mm_nt(turned[br], start_half)
        db = mm_nt(weighted[br], ahead_half)
        at = br * 256
        send[:, :, at : at + 128] = (dbc0[:, at : at + 128] + db).astype(BF16).reshape(16, 16, 128)
        send[:, :, at + 128 : at + 256] = (
            (dbc0[:, at + 128 : at + 256] + dc).astype(BF16).reshape(16, 16, 128)
        )
        both = jnp.sum(start * ahead, axis=0, keepdims=True)
        spread = jnp.where(lane_head + 4 * br == row_at, both, 0.0)
        d_end = d_end + jnp.sum(spread, axis=1, keepdims=True)
    out[...] = total.astype(BF16)
    cumul = rows_ref[0:8]
    step = rows_ref[8:16]
    weight = rows_ref[16:24]
    closing = rows_ref[24:32]
    slope = rows_ref[32:40]
    logdec = rows_ref[40:48]
    at = iota((8, ROWS), 1)
    row = iota((8, ROWS), 0)
    last = at == jnp.where(row < 4, ROWS - 1, 0)
    pull = dw * weight
    ending = jnp.sum(jnp.where(last, cumul, 0.0), axis=1, keepdims=True)
    d_end = jnp.exp(ending) * d_end + jnp.sum(pull, axis=1, keepdims=True)
    dcumul = side[...] - step * line[...] + dp - pull + jnp.where(last, d_end, 0.0)
    before, after = inclusive_masks()
    prefix = exact(mm, dcumul, before, 3, True)
    suffix = exact(mm, dcumul, after, 3, True)
    dlog = jnp.where(row < 4, suffix, prefix)
    dstep = line[...] + dw * closing - dlog * jnp.exp(rate[...])
    draw = dstep * slope
    draw_ref[...] = draw.astype(BF16)
    d_bias = jnp.sum(draw, axis=1, keepdims=True)
    d_rate = jnp.sum(dlog * logdec, axis=1, keepdims=True)
    first = iota((1, 256), 1)
    bias_row = jnp.zeros((1, 256), F32)
    rate_row = jnp.zeros((1, 256), F32)
    for h in range(HEADS):
        bias_row = jnp.where(first == 64 * h, d_bias[h : h + 1] + d_bias[h + 4 : h + 5], bias_row)
        rate_row = jnp.where(first == 64 * h, d_rate[h : h + 1] + d_rate[h + 4 : h + 5], rate_row)
    skip_row = jnp.sum(dyf * (xf[...].astype(F32) + xr[...].astype(F32)), axis=0, keepdims=True)
    none = jnp.zeros((5, 256), F32)
    small[...] = jnp.concatenate([skip_row, bias_row, rate_row, none], axis=0)


def total_kernel(got, draw, send):
    total = got[0].astype(F32)
    for k in range(1, GROUPS):
        total = total + got[k].astype(F32)
    send[:, 0:16, :] = jnp.broadcast_to(total.astype(BF16)[None], (GROUPS, 16, 512))
    padded = jnp.concatenate([draw[...].astype(F32), jnp.zeros((8, 256), F32)], axis=1)
    send[:, 16:24, :] = jnp.broadcast_to(padded.astype(BF16)[None], (GROUPS, 8, 512))


def project_back_kernel(
    got, xf, xr, gf, gr, dxf, dxr, wbc, swt, oht, table, scale, gain, cw, small,
    dpf, dpr, to_prev, to_next, send, cpart,
):
    dbc = got[:, 0:16, :].reshape(ROWS, 512)
    draw = got[:, 16:24, 0:256].astype(F32).reshape(128, 256).astype(BF16)
    pick_row = iota((128, 64), 0)
    pick_col = iota((128, 64), 1)
    wanted = pick_row // 8 * 4 + pick_row % 4
    normed = (table[...] * scale[:, 0:1] * gain[...]).astype(BF16).astype(F32)
    taps = [jnp.zeros((1, 256), F32)] * 4
    bias_row = jnp.zeros((1, 256), F32)
    wide = jnp.zeros((256, 256), F32)
    thin = jnp.zeros((256, 64), F32)
    ids_sum = jnp.zeros((16, 256), F32)
    for br, x, slope, dx, out in ((0, xf, gf, dxf, dpf), (1, xr, gr, dxr, dpr)):
        mine = (wanted == pick_col) & ((pick_row % 8 < 4) == (br == 0))
        dstep = mm_tn(draw, jnp.where(mine, 1.0, 0.0).astype(BF16)).astype(BF16)
        half = dbc[:, br * 256 : br * 256 + 256]
        into = mm_nt(half, wbc[...]) + mm(dstep, swt[...])
        whole = (dx[...] + into).astype(BF16).astype(F32)
        dpre = whole * slope[...]
        out[...] = dpre
        wide = wide + mm_tn(x[...], half)
        thin = thin + mm_tn(x[...], dstep)
        sums = exact(mm, oht[...], dpre, 2, False)
        for k in range(4):
            o = 3 - k if br == 0 else 3 + k
            block = sums[16 * o : 16 * o + 16]
            ids_sum = ids_sum + cw[k : k + 1] * block
            part = jnp.sum(normed * block, axis=0, keepdims=True)
            taps[k] = taps[k] + part
        bias_row = bias_row + jnp.sum(dpre, axis=0, keepdims=True)
    to_prev[...] = dpf[0:8]
    to_next[...] = dpr[ROWS - 8 : ROWS]
    shared = table[...] * gain[...] * ids_sum
    placed = jnp.concatenate(
        [jnp.zeros((88, 256), F32), shared, jnp.zeros((24, 256), F32)], axis=0
    )
    cpart[...] = exact(mm_nt, jnp.ones((8, 256), BF16), placed, 3, False)[0:1]
    stacked = jnp.concatenate(
        [jnp.zeros((64, 256), F32), ids_sum] + taps + [bias_row, small[0:3], jnp.zeros((40, 256), F32)],
        axis=0,
    )
    last = jnp.concatenate([thin, jnp.zeros((256, 64), F32)], axis=1) + jnp.transpose(stacked)
    send[:, 0:8, :] = wide[:, 0:128].astype(BF16).reshape(SLICES, 8, 128)
    send[:, 8:16, :] = wide[:, 128:256].astype(BF16).reshape(SLICES, 8, 128)
    send[:, 16:24, :] = last.astype(BF16).reshape(SLICES, 8, 128)


def normed_kernel(
    dpf, dpr, from_next, from_prev, cw, gain, table, oht, cpart,
    gn_ref, cross, ahead, behind,
):
    ahead[0:ROWS] = dpf[...]
    ahead[ROWS : ROWS + 8] = from_next[...]
    behind[0:8] = from_prev[...]
    behind[8 : ROWS + 8] = dpr[...]
    dn = jnp.zeros((ROWS, 256), F32)
    for k in range(4):
        dn = dn + cw[k : k + 1] * (ahead[k : k + ROWS] + behind[8 - k : 8 - k + ROWS])
    gn = dn.astype(BF16)
    gn_ref[...] = gn
    rated = exact(mm_tn, oht[48:64], table[...] * gain[...], 3, False)
    ones = jnp.ones((8, 256), BF16)
    row = exact(mm_nt, ones, gn.astype(F32) * rated, 3, False)[0:1]
    row = jnp.concatenate([row, cpart[...]], axis=1)
    cross[...] = jnp.broadcast_to(row[None], (GROUPS, 1, 384))


def embedded_kernel(got, gn, gain, table, scale, oht, out):
    total = got[0]
    for k in range(1, GROUPS):
        total = total + got[k]
    cross = columns(jnp.broadcast_to(total[:, 0:256], (8, ROWS)))[:, 0:1]
    own = oht[48:64]
    unit = scale[:, 0:1]
    turned = exact(mm_tn, own, unit * gain[...], 3, False)
    shrunk = exact(mm_tn, own, table[...] * (unit * unit * unit / D), 3, False)
    out[...] = (turned * gn[...].astype(F32) - shrunk * cross).astype(BF16)


def gather_kernel(got, cross, send):
    total = got[0].astype(F32)
    for k in range(1, SLICES):
        total = total + got[k].astype(F32)
    here = cross[0]
    for k in range(1, GROUPS):
        here = here + cross[k]
    here = here[:, 256:384]
    high = here.astype(BF16).astype(F32)
    row = iota((24, 128), 0)
    total = total + jnp.where(row == 16, high, 0.0) + jnp.where(row == 17, here - high, 0.0)
    send[...] = jnp.broadcast_to(total.astype(BF16)[None], (SLICES, 24, 128))


def finish_kernel(got, table, scale, gain, gt, gg, gcw, gcb, gwb, gwc, gswt, gsb, glr, gsg):
    gwb[...] = got[:, 0:8, :].astype(F32).reshape(256, 128)
    gwc[...] = got[:, 8:16, :].astype(F32).reshape(256, 128)
    rows = jnp.transpose(got[:, 16:24, :].astype(F32).reshape(256, 128))
    gswt[...] = rows[0:64]
    sums = rows[64:80]
    crossed = jnp.sum(rows[88:104], axis=1, keepdims=True)
    unit = scale[:, 0:1]
    gt[...] = unit * gain[...] * sums - table[...] * (unit * unit * unit / D) * crossed
    gg[...] = jnp.sum(table[...] * unit * sums, axis=0, keepdims=True)
    gcw[...] = rows[80:84]
    gcb[...] = rows[84:85]
    lane = iota((8, 256), 1)
    tail = rows[80:88]
    picked = iota((8, 4), 1)
    result = jnp.zeros((8, 4), F32)
    for h in range(HEADS):
        part = jnp.sum(jnp.where(lane // 64 == h, tail, 0.0), axis=1, keepdims=True)
        result = jnp.where(picked == h, part, result)
    gsg[...] = result[5:6]
    gsb[...] = result[6:7]
    glr[...] = result[7:8]


def swap(value, axis):
    return lax.all_to_all(value, axis, 0, 0, tiled=True)


def shift(value, pairs):
    return lax.ppermute(value, "ctx", pairs)


def mixer(
    token_ids,
    table,
    norm_gain,
    conv_weight,
    conv_bias,
    weight_b,
    weight_c,
    step_weight,
    step_bias,
    log_rate,
    skip_gain,
    out_grad,
):
    size = lax.axis_size("ctx")
    up = [(i, i + 1) for i in range(size - 1)]
    down = [(i + 1, i) for i in range(size - 1)]
    edge = ((8, 256), F32)
    square = ((ROWS, 256), F32)
    half_square = ((ROWS, 256), BF16)
    (squares,) = call(squares_kernel, (((GROUPS, 1, 128), F32),), table)
    squares = swap(squares, "fsdp")
    marked = token_ids[None] + 1
    ids_prev = shift(marked, up)
    ids_next = shift(marked, down)
    gain = norm_gain[None]
    wbc = jnp.concatenate([weight_b, weight_c], axis=1)
    swt = jnp.transpose(step_weight)
    heads_first = swt.reshape(GROUPS, HEADS, 256)
    swx = jnp.concatenate([heads_first, heads_first], axis=1).reshape(128, 256)
    bias = jnp.tile(step_bias, 2)[:, None]
    rate = jnp.tile(log_rate, 2)[:, None]
    skip = jnp.repeat(skip_gain, 64)[None]

    xf, xr, gf, gr, part, oht, scale = call(
        tokens_kernel,
        (
            half_square,
            half_square,
            square,
            square,
            ((GROUPS, 24, 512), BF16),
            ((128, 256), BF16),
            ((16, 128), F32),
        ),
        marked, ids_prev, ids_next, squares, table, gain, conv_weight, conv_bias[None], wbc, swx,
    )
    bc, raw = call(reduce_kernel, (((GROUPS, 16, 512), BF16), ((8, 256), F32)), swap(part, "fsdp"))
    bc = swap(bc, "fsdp").reshape(ROWS, 512)
    pair = ((2, ROWS, 256), F32)
    half_pair = ((2, ROWS, 256), BF16)
    cols, rows, weight, grown, weighted, turned, packed = call(
        steps_kernel,
        (((ROWS, 128), F32), ((48, ROWS), F32), pair, pair, half_pair, half_pair, ((2, 8, 128), F32)),
        raw, bias, rate, xf, xr, out_grad,
    )
    (states,) = call(
        states_kernel, (((16, 2, 40, 128), BF16),), bc, weighted, turned, packed
    )
    arrived = swap(states.reshape(SLICES, 40, 128), "ctx")
    y0, dxf0, dxr0, dbc0, side, line = call(
        within_kernel,
        (square, square, square, ((ROWS, 512), F32), ((8, ROWS), F32), ((8, ROWS), F32)),
        bc, cols, rows, xf, xr, out_grad, skip,
    )
    (entering,) = call(chain_kernel, (((SLICES, 32, 128), BF16),), arrived)
    entering = swap(entering, "ctx").reshape(16, 2, 32, 128)
    mixer_out, dxf, dxr, dpart, draw, small = call(
        carried_kernel,
        (
            half_square,
            square,
            square,
            ((GROUPS, 16, 512), BF16),
            ((8, 256), BF16),
            edge,
        ),
        entering, bc, weight, grown, weighted, turned, rows, xf, xr, out_grad,
        y0, dxf0, dxr0, dbc0, side, line, rate,
        final=(0,),
    )
    (totals,) = call(total_kernel, (((GROUPS, 24, 512), BF16),), swap(dpart, "fsdp"), draw)
    dpf, dpr, to_prev, to_next, gsend, cpart = call(
        project_back_kernel,
        (square, square, edge, edge, ((SLICES, 24, 128), BF16), ((1, 128), F32)),
        swap(totals, "fsdp"), xf, xr, gf, gr, dxf, dxr, wbc, swt, oht, table, scale, gain,
        conv_weight, small,
    )
    from_next = shift(to_prev, down)
    from_prev = shift(to_next, up)
    reduced = swap(gsend, "ctx")
    gn, cross = call(
        normed_kernel,
        (half_square, ((GROUPS, 1, 384), F32)),
        dpf, dpr, from_next, from_prev, conv_weight, gain, table, oht, cpart,
        scratch=[VMEM((ROWS + 8, 256), F32), VMEM((ROWS + 8, 256), F32)],
    )
    crossed = swap(cross, "fsdp")
    (gathered,) = call(gather_kernel, (((SLICES, 24, 128), BF16),), reduced, crossed)
    (grad_embedded,) = call(
        embedded_kernel, (half_square,), crossed, gn, gain, table, scale, oht, final=(0,)
    )
    outs = call(
        finish_kernel,
        (
            ((16, 256), F32),
            ((1, 256), F32),
            ((4, 256), F32),
            ((1, 256), F32),
            ((256, 128), F32),
            ((256, 128), F32),
            ((64, 256), F32),
            ((1, 4), F32),
            ((1, 4), F32),
            ((1, 4), F32),
        ),
        swap(gathered, "ctx"), table, scale, gain,
        final=range(10),
    )
    gt, gg, gcw, gcb, gwb, gwc, gswt, gsb, glr, gsg = outs
    return (
        mixer_out,
        grad_embedded,
        gt,
        gg[0],
        gcw,
        gcb[0],
        gwb,
        gwc,
        jnp.transpose(gswt),
        gsb[0],
        glr[0],
        gsg[0],
    )


def solution(mesh):
    return jax.shard_map(
        mixer,
        mesh=mesh,
        in_specs=(
            P("ctx"),
            P(None, "fsdp"),
            P("fsdp"),
            P(None, "fsdp"),
            P("fsdp"),
            P("fsdp", None),
            P("fsdp", None),
            P("fsdp", None),
            P("fsdp"),
            P("fsdp"),
            P("fsdp"),
            P("ctx", "fsdp"),
        ),
        out_specs=(
            P("ctx", "fsdp"),
            P("ctx", "fsdp"),
            P(None, "fsdp"),
            P("fsdp"),
            P(None, "fsdp"),
            P("fsdp"),
            P("fsdp", None),
            P("fsdp", None),
            P("fsdp", None),
            P("fsdp"),
            P("fsdp"),
            P("fsdp"),
        ),
        check_vma=False,
    )
```

```python
import jax
import jax.numpy as jnp
from jax import lax
from jax.sharding import PartitionSpec as P
from jax.experimental import pallas as pl
from jax.experimental.pallas import tpu as pltpu

D = 4096
ROWS = 256
HEADS = 4
STATE = 128
GROUPS = 16
NEAR = 8
FAR = 4
CTX = ("zh", "zl", "xh")
BESIDE = ("zl", "xh")
F32 = jnp.float32
BF16 = jnp.bfloat16
VMEM = pltpu.VMEM


def call(kernel, outs, *args, final=(), scratch=()):
    shapes = tuple(
        jax.ShapeDtypeStruct(shape, kind) if i in final else VMEM(shape, kind)
        for i, (shape, kind) in enumerate(outs)
    )
    near = [pltpu.with_memory_space_constraint(arg, VMEM) for arg in args]
    return pl.pallas_call(
        kernel,
        out_shape=shapes,
        scratch_shapes=scratch,
        compiler_params=pltpu.CompilerParams(vmem_limit_bytes=24 << 20),
    )(*near)


def iota(shape, dim):
    return lax.broadcasted_iota(jnp.int32, shape, dim)


def mm(left, right):
    return lax.dot_general(left, right, (((1,), (0,)), ((), ())), preferred_element_type=F32)


def mm_tn(left, right):
    return lax.dot_general(left, right, (((0,), (0,)), ((), ())), preferred_element_type=F32)


def mm_nt(left, right):
    return lax.dot_general(left, right, (((1,), (1,)), ((), ())), preferred_element_type=F32)


def pieces(value, count):
    parts = []
    rest = value
    for _ in range(count):
        part = rest.astype(BF16)
        parts.append(part)
        rest = rest - part.astype(F32)
    return parts


def exact(form, left, right, count, split_left):
    total = None
    for part in pieces(left if split_left else right, count):
        term = form(part, right) if split_left else form(left, part)
        total = term if total is None else total + term
    return total


def head_masks(rows):
    lane_head = iota((rows, 256), 1) // 64
    return [lane_head == h for h in range(HEADS)]


def by_head(values, masks):
    out = values[3]
    for h in range(3):
        out = jnp.where(masks[h], values[h], out)
    return out


def expand(cols, first, masks):
    wide = [jnp.broadcast_to(cols[:, first + h : first + h + 1], (ROWS, 256)) for h in range(HEADS)]
    return by_head(wide, masks)


def columns(rows):
    missing = 128 - rows.shape[0]
    return jnp.transpose(jnp.concatenate([rows, jnp.zeros((missing, ROWS), F32)], axis=0))


def inclusive_masks():
    before = iota((ROWS, ROWS), 0) <= iota((ROWS, ROWS), 1)
    after = iota((ROWS, ROWS), 0) >= iota((ROWS, ROWS), 1)
    return jnp.where(before, 1.0, 0.0).astype(BF16), jnp.where(after, 1.0, 0.0).astype(BF16)


def squares_kernel(table, send):
    squares = jnp.concatenate([table[...] * table[...], jnp.zeros((112, 256), F32)], axis=0)
    sums = exact(mm_nt, jnp.ones((8, 256), BF16), squares, 3, False)
    send[...] = jnp.broadcast_to(sums[0:1][None], (GROUPS, 1, 128))


def tokens_kernel(
    ids, ids_prev, ids_next, got, table, gain, cw, cb, wb, wc, swt,
    xf, xr, gf, gr, send, oht_ref, scale,
):
    total = got[0]
    for k in range(1, GROUPS):
        total = total + got[k]
    unit = lax.rsqrt(total / D + 1e-05)
    spread = jnp.transpose(jnp.broadcast_to(unit, (128, 128)))[0:16]
    scale[...] = spread
    unit = spread[:, 0:1]
    normed = (table[...] * unit * gain[...]).astype(BF16).astype(F32)
    vocab = iota((16, ROWS), 0) + 1
    lane = iota((1, ROWS), 1)
    here = ids[...]
    hits = []
    for o in range(7):
        d = o - 3
        if d == 0:
            moved = here
        elif d > 0:
            ahead = pltpu.roll(ids_next[...], ROWS - d, 1)
            moved = jnp.where(lane < ROWS - d, pltpu.roll(here, ROWS - d, 1), ahead)
        else:
            moved = jnp.where(lane >= -d, pltpu.roll(here, -d, 1), pltpu.roll(ids_prev[...], -d, 1))
        hits.append(jnp.where(moved == vocab, 1.0, 0.0))
    hits.append(jnp.zeros((16, ROWS), F32))
    oht = jnp.concatenate(hits, axis=0).astype(BF16)
    oht_ref[...] = oht
    none = jnp.zeros((16, 256), F32)
    taps = [cw[k : k + 1, :] * normed for k in range(4)]
    fwd_rows = jnp.concatenate([taps[3], taps[2], taps[1], taps[0], none, none, none, none], axis=0)
    rev_rows = jnp.concatenate([none, none, none, taps[0], taps[1], taps[2], taps[3], none], axis=0)
    halves = []
    for rows, x_ref, slope_ref in ((fwd_rows, xf, gf), (rev_rows, xr, gr)):
        pre = exact(mm_tn, oht, rows, 3, False) + cb[...]
        gate = 1.0 / (1.0 + jnp.exp(-pre))
        slope_ref[...] = gate * (1.0 + pre * (1.0 - gate))
        half = (pre * gate).astype(BF16)
        x_ref[...] = half
        halves.append(half)
    for member, half in enumerate(halves):
        for side, weight in ((0, wb), (128, wc)):
            at = member * 256 + side
            part = mm(half, weight[...]).astype(BF16).reshape(GROUPS, 16, 128)
            send[:, 0:16, at : at + 128] = part
    own = iota((128, 256), 0) % 8 < 4
    place = iota((128, 64), 0)
    chosen = jnp.where(place // 8 * 4 + place % 4 == iota((128, 64), 1), 1.0, 0.0).astype(BF16)
    swx = mm(chosen, swt[...]).astype(BF16)
    steps = jnp.where(own, mm_nt(swx, halves[0]), mm_nt(swx, halves[1]))
    high, low = pieces(steps, 2)
    send[:, 16:24, 0:256] = high.reshape(GROUPS, 8, 256)
    send[:, 16:24, 256:512] = low.reshape(GROUPS, 8, 256)


def reduce_kernel(got, bc, raw):
    total = got[0].astype(F32)
    for k in range(1, GROUPS):
        total = total + got[k].astype(F32)
    half = total[0:16].astype(BF16)
    bc[...] = jnp.broadcast_to(half[None], (GROUPS, 16, 512))
    raw[...] = total[16:24, 0:256] + total[16:24, 256:512]


def steps_kernel(
    raw, bias, rate, xf, xr, dy,
    cols_ref, rows_ref, weighted_ref, turned_ref, packed_ref,
):
    shifted = raw[...] + bias[...]
    step = jnp.maximum(shifted, 0.0) + jnp.log1p(jnp.exp(-jnp.abs(shifted)))
    slope = 1.0 / (1.0 + jnp.exp(-shifted))
    logdec = -step * jnp.exp(rate[...])
    before, after = inclusive_masks()
    fwd_row = iota((8, ROWS), 0) < 4
    prefix = exact(mm, logdec, before, 3, True)
    suffix = exact(mm, logdec, after, 3, True)
    cumul = jnp.where(fwd_row, prefix, suffix)
    fwd_one = iota((8, 1), 0) < 4
    ending = jnp.where(fwd_one, prefix[:, ROWS - 1 : ROWS], suffix[:, 0:1])
    closing = jnp.exp(ending - cumul)
    weight = closing * step
    grown = jnp.exp(cumul)
    rows_ref[...] = jnp.concatenate([cumul, step, weight, closing, slope, logdec], axis=0)
    cols = columns(jnp.concatenate([cumul, step, weight, grown], axis=0))
    cols_ref[...] = cols
    masks = head_masks(ROWS)
    dyf = dy[...].astype(F32)
    for br, x in ((0, xf), (1, xr)):
        weight_wide = expand(cols, 16 + 4 * br, masks)
        grown_wide = expand(cols, 24 + 4 * br, masks)
        weighted_ref[br] = (weight_wide * x[...].astype(F32)).astype(BF16)
        turned_ref[br] = (grown_wide * dyf).astype(BF16)
    decay = jnp.exp(ending)
    lane_head = iota((1, 256), 1) // 64
    fwd_decay = jnp.zeros((1, 256), F32)
    rev_decay = jnp.zeros((1, 256), F32)
    for h in range(HEADS):
        fwd_decay = jnp.where(lane_head == h, decay[h : h + 1], fwd_decay)
        rev_decay = jnp.where(lane_head == h, decay[h + 4 : h + 5], rev_decay)
    packed_ref[...] = split_decays(fwd_decay, rev_decay)


def split_decays(fwd_decay, rev_decay):
    row = iota((8, 256), 0)
    f_high = fwd_decay.astype(BF16).astype(F32)
    r_high = rev_decay.astype(BF16).astype(F32)
    packed = jnp.where(row == 0, f_high, 0.0)
    packed = jnp.where(row == 1, fwd_decay - f_high, packed)
    packed = jnp.where(row == 2, r_high, packed)
    return jnp.where(row == 3, rev_decay - r_high, packed)


def join_decays(packed):
    rows = packed.astype(F32)
    return rows[0:1] + rows[1:2], rows[2:3] + rows[3:4]


def states_kernel(bc, weighted, turned, packed, send):
    found = []
    for br in range(2):
        b = bc[:, br * 256 : br * 256 + 128]
        c = bc[:, br * 256 + 128 : br * 256 + 256]
        found.append((mm_tn(b, weighted[br]), mm_tn(c, turned[br])))
    chains = (found[0][0], found[1][1], found[1][0], found[0][1])
    for ch, state in enumerate(chains):
        send[:, ch * 16 : ch * 16 + 16, :] = state.astype(BF16).reshape(NEAR, 16, 256)
    send[:, 64:72, :] = jnp.broadcast_to(packed[...].astype(BF16)[None], (NEAR, 8, 256))


def advance(state, decay_first, decay_second, piece):
    return decay_first * state[0] + piece[0:16], decay_second * state[1] + piece[16:32]


def group_kernel(got, send):
    nothing = jnp.zeros((16, 256), F32)
    up = (nothing, nothing)
    down = (nothing, nothing)
    fwd_all = jnp.ones((1, 256), F32)
    rev_all = jnp.ones((1, 256), F32)
    for i in range(NEAR):
        fwd_decay, rev_decay = join_decays(got[i, 64:72, :])
        fwd_all = fwd_all * fwd_decay
        rev_all = rev_all * rev_decay
        up = advance(up, fwd_decay, rev_decay, got[i, 0:32, :].astype(F32))
        j = NEAR - 1 - i
        fwd_decay, rev_decay = join_decays(got[j, 64:72, :])
        down = advance(down, rev_decay, fwd_decay, got[j, 32:64, :].astype(F32))
    totals = jnp.concatenate([up[0], up[1], down[0], down[1], split_decays(fwd_all, rev_all)], axis=0)
    send[...] = jnp.broadcast_to(totals.astype(BF16)[None], (FAR, 72, 256))


def chain_kernel(got, far, group, out):
    here = group[...]
    nothing = jnp.zeros((16, 256), F32)
    up = (nothing, nothing)
    down = (nothing, nothing)
    for g in range(FAR):
        fwd_decay, rev_decay = join_decays(far[g, 64:72, :])
        moved = advance(up, fwd_decay, rev_decay, far[g, 0:32, :].astype(F32))
        up = tuple(jnp.where(here > g, new, old) for new, old in zip(moved, up))
        k = FAR - 1 - g
        fwd_decay, rev_decay = join_decays(far[k, 64:72, :])
        moved = advance(down, rev_decay, fwd_decay, far[k, 32:64, :].astype(F32))
        down = tuple(jnp.where(here < k, new, old) for new, old in zip(moved, down))
    for i in range(NEAR):
        out[i, 0:16, :] = up[0].astype(BF16)
        out[i, 16:32, :] = up[1].astype(BF16)
        fwd_decay, rev_decay = join_decays(got[i, 64:72, :])
        up = advance(up, fwd_decay, rev_decay, got[i, 0:32, :].astype(F32))
        j = NEAR - 1 - i
        out[j, 32:48, :] = down[0].astype(BF16)
        out[j, 48:64, :] = down[1].astype(BF16)
        fwd_decay, rev_decay = join_decays(got[j, 64:72, :])
        down = advance(down, rev_decay, fwd_decay, got[j, 32:64, :].astype(F32))


def within_kernel(bc, cols_ref, rows_ref, xf, xr, dy, skip, y_ref, dxf, dxr, dbc, side, line):
    masks = head_masks(ROWS)
    t_at = iota((ROWS, ROWS), 0)
    s_at = iota((ROWS, ROWS), 1)
    lane = iota((ROWS, 128), 1)
    cols = cols_ref[...]
    dyh = dy[...]
    dyf = dyh.astype(F32)
    nothing = jnp.zeros((ROWS, 256), BF16)
    direct = skip[...] * dyf
    total = skip[...] * (xf[...].astype(F32) + xr[...].astype(F32))
    side_acc = jnp.zeros((ROWS, 128), F32)
    lines = []
    for br, x, dx_ref in ((0, xf, dxf), (1, xr, dxr)):
        xh = x[...]
        b = bc[:, br * 256 : br * 256 + 128]
        c = bc[:, br * 256 + 128 : br * 256 + 256]
        inner = mm_nt(c, b)
        causal = t_at >= s_at if br == 0 else t_at <= s_at
        dinner = jnp.zeros((ROWS, ROWS), F32)
        intra = []
        back = []
        for h in range(HEADS):
            at = 4 * br + h
            spread = cols[:, at : at + 1] - rows_ref[at : at + 1, :]
            decay = jnp.exp(jnp.where(causal, spread, -jnp.inf))
            step = rows_ref[8 + at : 9 + at, :]
            paced = decay * step
            mixing = (inner * paced).astype(BF16)
            intra.append(mm(mixing, xh))
            back.append(mm_tn(mixing, dyh))
            dmix = mm_nt(jnp.where(masks[h], dyh, nothing), xh)
            dinner = dinner + dmix * paced
            reach = dmix * decay * inner
            lines.append(jnp.sum(reach, axis=0, keepdims=True))
            flow = jnp.sum(reach * step, axis=1, keepdims=True)
            side_acc = jnp.where(lane == at, flow, side_acc)
        total = total + by_head(intra, masks)
        dx_ref[...] = direct + by_head(back, masks)
        dhalf = dinner.astype(BF16)
        dbc[:, br * 256 : br * 256 + 128] = mm_tn(dhalf, c)
        dbc[:, br * 256 + 128 : br * 256 + 256] = mm(dhalf, b)
    y_ref[...] = total
    side[...] = jnp.transpose(side_acc)[0:8]
    line[...] = jnp.concatenate(lines, axis=0)


def carried_kernel(
    got, bc, cols_ref, weighted, turned, rows_ref, xf, xr, dy,
    y0, dxf0, dxr0, dbc0, side, line, rate,
    out, dxf, dxr, send, draw_ref, small,
):
    dyf = dy[...].astype(F32)

    masks = head_masks(ROWS)
    cols = cols_ref[...]

    def state(ch):
        return got[:, ch * 16 : ch * 16 + 16, :].reshape(STATE, 256)

    row_at = iota((8, 256), 0)
    lane_head = iota((8, 256), 1) // 64
    total = y0[...]
    dp = jnp.zeros((8, ROWS), F32)
    dw = jnp.zeros((8, ROWS), F32)
    d_end = jnp.zeros((8, 1), F32)
    for br, x, dx0, dx_ref, at_state, at_grad in ((0, xf, dxf0, dxf, 0, 3), (1, xr, dxr0, dxr, 2, 1)):
        start_half = state(at_state)
        ahead_half = state(at_grad)
        b = bc[:, br * 256 : br * 256 + 128]
        c = bc[:, br * 256 + 128 : br * 256 + 256]
        heads = jnp.where(lane_head + 4 * br == row_at, 1.0, 0.0).astype(BF16)
        carried = expand(cols, 24 + 4 * br, masks) * mm(c, start_half)
        total = total + carried
        dp = dp + exact(mm_nt, heads, dyf * carried, 2, False)
        xv = x[...].astype(F32)
        toward = mm(b, ahead_half)
        dx_ref[...] = dx0[...] + expand(cols, 16 + 4 * br, masks) * toward
        dw = dw + exact(mm_nt, heads, xv * toward, 2, False)
        dc = mm_nt(turned[br], start_half)
        db = mm_nt(weighted[br], ahead_half)
        at = br * 256
        send[:, :, at : at + 128] = (dbc0[:, at : at + 128] + db).astype(BF16).reshape(16, 16, 128)
        send[:, :, at + 128 : at + 256] = (
            (dbc0[:, at + 128 : at + 256] + dc).astype(BF16).reshape(16, 16, 128)
        )
        both = jnp.sum(start_half.astype(F32) * ahead_half.astype(F32), axis=0, keepdims=True)
        spread = jnp.where(lane_head + 4 * br == row_at, both, 0.0)
        d_end = d_end + jnp.sum(spread, axis=1, keepdims=True)
    out[...] = total.astype(BF16)
    cumul = rows_ref[0:8]
    step = rows_ref[8:16]
    weight = rows_ref[16:24]
    closing = rows_ref[24:32]
    slope = rows_ref[32:40]
    logdec = rows_ref[40:48]
    at = iota((8, ROWS), 1)
    row = iota((8, ROWS), 0)
    last = at == jnp.where(row < 4, ROWS - 1, 0)
    pull = dw * weight
    ending = jnp.sum(jnp.where(last, cumul, 0.0), axis=1, keepdims=True)
    d_end = jnp.exp(ending) * d_end + jnp.sum(pull, axis=1, keepdims=True)
    dcumul = side[...] - step * line[...] + dp - pull + jnp.where(last, d_end, 0.0)
    before, after = inclusive_masks()
    prefix = exact(mm, dcumul, before, 3, True)
    suffix = exact(mm, dcumul, after, 3, True)
    dlog = jnp.where(row < 4, suffix, prefix)
    dstep = line[...] + dw * closing - dlog * jnp.exp(rate[...])
    draw = dstep * slope
    draw_ref[...] = draw.astype(BF16)
    d_bias = jnp.sum(draw, axis=1, keepdims=True)
    d_rate = jnp.sum(dlog * logdec, axis=1, keepdims=True)
    first = iota((1, 256), 1)
    bias_row = jnp.zeros((1, 256), F32)
    rate_row = jnp.zeros((1, 256), F32)
    for h in range(HEADS):
        bias_row = jnp.where(first == 64 * h, d_bias[h : h + 1] + d_bias[h + 4 : h + 5], bias_row)
        rate_row = jnp.where(first == 64 * h, d_rate[h : h + 1] + d_rate[h + 4 : h + 5], rate_row)
    skip_row = jnp.sum(dyf * (xf[...].astype(F32) + xr[...].astype(F32)), axis=0, keepdims=True)
    none = jnp.zeros((5, 256), F32)
    small[...] = jnp.concatenate([skip_row, bias_row, rate_row, none], axis=0)


def total_kernel(got, draw, send):
    total = got[0].astype(F32)
    for k in range(1, GROUPS):
        total = total + got[k].astype(F32)
    send[:, 0:16, :] = jnp.broadcast_to(total.astype(BF16)[None], (GROUPS, 16, 512))
    padded = jnp.concatenate([draw[...].astype(F32), jnp.zeros((8, 256), F32)], axis=1)
    send[:, 16:24, :] = jnp.broadcast_to(padded.astype(BF16)[None], (GROUPS, 8, 512))


def project_back_kernel(
    got, xf, xr, gf, gr, dxf, dxr, wb, wc, swt, oht, table, scale, gain, cw, small,
    dpf, dpr, to_prev, to_next, send, cpart,
):
    dbc = got[:, 0:16, :].reshape(ROWS, 512)
    draw = got[:, 16:24, 0:256].astype(F32).reshape(128, 256).astype(BF16)
    pick_row = iota((128, 64), 0)
    pick_col = iota((128, 64), 1)
    wanted = pick_row // 8 * 4 + pick_row % 4
    normed = (table[...] * scale[:, 0:1] * gain[...]).astype(BF16).astype(F32)
    taps = [jnp.zeros((1, 256), F32)] * 4
    bias_row = jnp.zeros((1, 256), F32)
    wide = jnp.zeros((256, 256), F32)
    thin = jnp.zeros((256, 64), F32)
    ids_sum = jnp.zeros((16, 256), F32)
    for br, x, slope, dx, out in ((0, xf, gf, dxf, dpf), (1, xr, gr, dxr, dpr)):
        mine = (wanted == pick_col) & ((pick_row % 8 < 4) == (br == 0))
        dstep = mm_tn(draw, jnp.where(mine, 1.0, 0.0).astype(BF16)).astype(BF16)
        half = dbc[:, br * 256 : br * 256 + 256]
        into = mm_nt(half[:, 0:128], wb[...]) + mm_nt(half[:, 128:256], wc[...])
        into = into + mm(dstep, swt[...])
        whole = (dx[...] + into).astype(BF16).astype(F32)
        dpre = whole * slope[...]
        out[...] = dpre
        wide = wide + mm_tn(x[...], half)
        thin = thin + mm_tn(x[...], dstep)
        sums = exact(mm, oht[...], dpre, 2, False)
        for k in range(4):
            o = 3 - k if br == 0 else 3 + k
            block = sums[16 * o : 16 * o + 16]
            ids_sum = ids_sum + cw[k : k + 1] * block
            part = jnp.sum(normed * block, axis=0, keepdims=True)
            taps[k] = taps[k] + part
        bias_row = bias_row + jnp.sum(dpre, axis=0, keepdims=True)
    to_prev[...] = dpf[0:8]
    to_next[...] = dpr[ROWS - 8 : ROWS]
    shared = table[...] * gain[...] * ids_sum
    placed = jnp.concatenate(
        [jnp.zeros((88, 256), F32), shared, jnp.zeros((24, 256), F32)], axis=0
    )
    cpart[...] = exact(mm_nt, jnp.ones((8, 256), BF16), placed, 3, False)[0:1]
    stacked = jnp.concatenate(
        [jnp.zeros((64, 256), F32), ids_sum] + taps + [bias_row, small[0:3], jnp.zeros((40, 256), F32)],
        axis=0,
    )
    last = jnp.concatenate([thin, jnp.zeros((256, 64), F32)], axis=1) + jnp.transpose(stacked)
    send[:, 0:32, :] = wide[:, 0:128].astype(BF16).reshape(NEAR, 32, 128)
    send[:, 32:64, :] = wide[:, 128:256].astype(BF16).reshape(NEAR, 32, 128)
    send[:, 64:96, :] = last.astype(BF16).reshape(NEAR, 32, 128)


def normed_kernel(
    dpf, dpr, from_next, from_prev, cw, gain, table, oht, cpart,
    gn_ref, cross, ahead, behind,
):
    ahead[0:ROWS] = dpf[...]
    ahead[ROWS : ROWS + 8] = from_next[...]
    behind[0:8] = from_prev[...]
    behind[8 : ROWS + 8] = dpr[...]
    dn = jnp.zeros((ROWS, 256), F32)
    for k in range(4):
        dn = dn + cw[k : k + 1] * (ahead[k : k + ROWS] + behind[8 - k : 8 - k + ROWS])
    gn = dn.astype(BF16)
    gn_ref[...] = gn
    rated = exact(mm_tn, oht[48:64], table[...] * gain[...], 3, False)
    ones = jnp.ones((8, 256), BF16)
    row = exact(mm_nt, ones, gn.astype(F32) * rated, 3, False)[0:1]
    row = jnp.concatenate([row, cpart[...]], axis=1)
    cross[...] = jnp.broadcast_to(row[None], (GROUPS, 1, 384))


def embedded_kernel(got, gn, gain, table, scale, oht, out):
    total = got[0]
    for k in range(1, GROUPS):
        total = total + got[k]
    cross = columns(jnp.broadcast_to(total[:, 0:256], (8, ROWS)))[:, 0:1]
    own = oht[48:64]
    unit = scale[:, 0:1]
    turned = exact(mm_tn, own, unit * gain[...], 3, False)
    shrunk = exact(mm_tn, own, table[...] * (unit * unit * unit / D), 3, False)
    out[...] = (turned * gn[...].astype(F32) - shrunk * cross).astype(BF16)


def near_kernel(got, cross, send):
    total = got[0].astype(F32)
    for k in range(1, NEAR):
        total = total + got[k].astype(F32)
    here = cross[0]
    for k in range(1, GROUPS):
        here = here + cross[k]
    here = here[:, 256:384]
    high = here.astype(BF16).astype(F32)
    row = iota((96, 128), 0)
    total = total + jnp.where(row == 64, high, 0.0) + jnp.where(row == 65, here - high, 0.0)
    send[...] = jnp.broadcast_to(total.astype(BF16)[None], (FAR, 96, 128))


def far_kernel(got, send):
    total = got[0].astype(F32)
    for k in range(1, FAR):
        total = total + got[k].astype(F32)
    send[...] = jnp.broadcast_to(total.astype(BF16)[None], (NEAR, 96, 128))


def finish_kernel(got, table, scale, gain, gt, gg, gcw, gcb, gwb, gwc, gswt, gsb, glr, gsg):
    gwb[...] = got[:, 0:32, :].astype(F32).reshape(256, 128)
    gwc[...] = got[:, 32:64, :].astype(F32).reshape(256, 128)
    rows = jnp.transpose(got[:, 64:96, :].astype(F32).reshape(256, 128))
    gswt[...] = rows[0:64]
    sums = rows[64:80]
    crossed = jnp.sum(rows[88:104], axis=1, keepdims=True)
    unit = scale[:, 0:1]
    gt[...] = unit * gain[...] * sums - table[...] * (unit * unit * unit / D) * crossed
    gg[...] = jnp.sum(table[...] * unit * sums, axis=0, keepdims=True)
    gcw[...] = rows[80:84]
    gcb[...] = rows[84:85]
    lane = iota((8, 256), 1)
    tail = rows[80:88]
    picked = iota((8, 4), 1)
    result = jnp.zeros((8, 4), F32)
    for h in range(HEADS):
        part = jnp.sum(jnp.where(lane // 64 == h, tail, 0.0), axis=1, keepdims=True)
        result = jnp.where(picked == h, part, result)
    gsg[...] = result[5:6]
    gsb[...] = result[6:7]
    glr[...] = result[7:8]


def swap(value, axis):
    return lax.all_to_all(value, axis, 0, 0, tiled=True)


def shift(value, pairs):
    return lax.ppermute(value, CTX, pairs)


def mixer(
    token_ids,
    table,
    norm_gain,
    conv_weight,
    conv_bias,
    weight_b,
    weight_c,
    step_weight,
    step_bias,
    log_rate,
    skip_gain,
    out_grad,
):
    size = lax.axis_size(CTX)
    up = [(i, i + 1) for i in range(size - 1)]
    down = [(i + 1, i) for i in range(size - 1)]
    edge = ((8, 256), F32)
    square = ((ROWS, 256), F32)
    half_square = ((ROWS, 256), BF16)
    (squares,) = call(squares_kernel, (((GROUPS, 1, 128), F32),), table)
    squares = swap(squares, "fsdp")
    marked = token_ids[None] + 1
    ids_prev = shift(marked, up)
    ids_next = shift(marked, down)
    gain = norm_gain[None]
    group = lax.axis_index("zh").reshape(1, 1)
    swt = jnp.transpose(step_weight)
    bias = jnp.tile(step_bias, 2)[:, None]
    rate = jnp.tile(log_rate, 2)[:, None]
    skip = jnp.repeat(skip_gain, 64)[None]

    xf, xr, gf, gr, part, oht, scale = call(
        tokens_kernel,
        (
            half_square,
            half_square,
            square,
            square,
            ((GROUPS, 24, 512), BF16),
            ((128, 256), BF16),
            ((16, 128), F32),
        ),
        marked, ids_prev, ids_next, squares, table, gain, conv_weight, conv_bias[None],
        weight_b, weight_c, swt,
    )
    bc, raw = call(reduce_kernel, (((GROUPS, 16, 512), BF16), ((8, 256), F32)), swap(part, "fsdp"))
    bc = swap(bc, "fsdp").reshape(ROWS, 512)
    half_pair = ((2, ROWS, 256), BF16)
    cols, rows, weighted, turned, packed = call(
        steps_kernel,
        (((ROWS, 128), F32), ((48, ROWS), F32), half_pair, half_pair, edge),
        raw, bias, rate, xf, xr, out_grad,
    )
    (states,) = call(
        states_kernel, (((NEAR, 72, 256), BF16),), bc, weighted, turned, packed
    )
    arrived = swap(states, BESIDE)
    y0, dxf0, dxr0, dbc0, side, line = call(
        within_kernel,
        (square, square, square, ((ROWS, 512), F32), ((8, ROWS), F32), ((8, ROWS), F32)),
        bc, cols, rows, xf, xr, out_grad, skip,
    )
    (groups,) = call(group_kernel, (((FAR, 72, 256), BF16),), arrived)
    groups = swap(groups, "zh")
    (entering,) = call(chain_kernel, (((NEAR, 64, 256), BF16),), arrived, groups, group)
    entering = swap(entering, BESIDE)
    mixer_out, dxf, dxr, dpart, draw, small = call(
        carried_kernel,
        (
            half_square,
            square,
            square,
            ((GROUPS, 16, 512), BF16),
            ((8, 256), BF16),
            edge,
        ),
        entering, bc, cols, weighted, turned, rows, xf, xr, out_grad,
        y0, dxf0, dxr0, dbc0, side, line, rate,
        final=(0,),
    )
    (totals,) = call(total_kernel, (((GROUPS, 24, 512), BF16),), swap(dpart, "fsdp"), draw)
    dpf, dpr, to_prev, to_next, gsend, cpart = call(
        project_back_kernel,
        (square, square, edge, edge, ((NEAR, 96, 128), BF16), ((1, 128), F32)),
        swap(totals, "fsdp"), xf, xr, gf, gr, dxf, dxr, weight_b,
        weight_c, swt, oht, table, scale, gain, conv_weight, small,
    )
    from_next = shift(to_prev, down)
    from_prev = shift(to_next, up)
    reduced = swap(gsend, BESIDE)
    gn, cross = call(
        normed_kernel,
        (half_square, ((GROUPS, 1, 384), F32)),
        dpf, dpr, from_next, from_prev, conv_weight, gain, table, oht, cpart,
        scratch=[VMEM((ROWS + 8, 256), F32), VMEM((ROWS + 8, 256), F32)],
    )
    crossed = swap(cross, "fsdp")
    (summed,) = call(near_kernel, (((FAR, 96, 128), BF16),), reduced, crossed)
    summed = swap(summed, "zh")
    (gathered,) = call(far_kernel, (((NEAR, 96, 128), BF16),), summed)
    (grad_embedded,) = call(
        embedded_kernel, (half_square,), crossed, gn, gain, table, scale, oht, final=(0,)
    )
    outs = call(
        finish_kernel,
        (
            ((16, 256), F32),
            ((1, 256), F32),
            ((4, 256), F32),
            ((1, 256), F32),
            ((256, 128), F32),
            ((256, 128), F32),
            ((64, 256), F32),
            ((1, 4), F32),
            ((1, 4), F32),
            ((1, 4), F32),
        ),
        swap(gathered, BESIDE), table, scale, gain,
        final=range(10),
    )
    gt, gg, gcw, gcb, gwb, gwc, gswt, gsb, glr, gsg = outs
    return (
        mixer_out,
        grad_embedded,
        gt,
        gg[0],
        gcw,
        gcb[0],
        gwb,
        gwc,
        jnp.transpose(gswt),
        gsb[0],
        glr[0],
        gsg[0],
    )


def solution(mesh):
    devices = mesh.devices.reshape(mesh.shape["fsdp"], FAR, 4, 2)
    mesh = jax.sharding.Mesh(devices, ("fsdp",) + CTX)
    return jax.shard_map(
        mixer,
        mesh=mesh,
        in_specs=(
            P(CTX),
            P(None, "fsdp"),
            P("fsdp"),
            P(None, "fsdp"),
            P("fsdp"),
            P("fsdp", None),
            P("fsdp", None),
            P("fsdp", None),
            P("fsdp"),
            P("fsdp"),
            P("fsdp"),
            P(CTX, "fsdp"),
        ),
        out_specs=(
            P(CTX, "fsdp"),
            P(CTX, "fsdp"),
            P(None, "fsdp"),
            P("fsdp"),
            P(None, "fsdp"),
            P("fsdp"),
            P("fsdp", None),
            P("fsdp", None),
            P("fsdp", None),
            P("fsdp"),
            P("fsdp"),
            P("fsdp"),
        ),
        check_vma=False,
    )
```

```python
import jax
import jax.numpy as jnp
from jax import lax
from jax.sharding import PartitionSpec as P
from jax.experimental import pallas as pl
from jax.experimental.pallas import tpu as pltpu

D = 4096
ROWS = 256
HEADS = 4
STATE = 128
GROUPS = 16
NEAR = 8
FAR = 4
CTX = ("zh", "zl", "xh")
BESIDE = ("zl", "xh")
F32 = jnp.float32
BF16 = jnp.bfloat16
VMEM = pltpu.VMEM


def call(kernel, outs, *args, final=(), scratch=(), near=True):
    shapes = tuple(
        jax.ShapeDtypeStruct(shape, kind) if i in final else VMEM(shape, kind)
        for i, (shape, kind) in enumerate(outs)
    )
    space = VMEM if near else pltpu.HBM
    args = [pltpu.with_memory_space_constraint(arg, space) for arg in args]
    return pl.pallas_call(
        kernel,
        out_shape=shapes,
        scratch_shapes=scratch,
        compiler_params=pltpu.CompilerParams(vmem_limit_bytes=24 << 20),
    )(*args)


def iota(shape, dim):
    return lax.broadcasted_iota(jnp.int32, shape, dim)


def mm(left, right):
    return lax.dot_general(left, right, (((1,), (0,)), ((), ())), preferred_element_type=F32)


def mm_tn(left, right):
    return lax.dot_general(left, right, (((0,), (0,)), ((), ())), preferred_element_type=F32)


def mm_nt(left, right):
    return lax.dot_general(left, right, (((1,), (1,)), ((), ())), preferred_element_type=F32)


def pieces(value, count):
    parts = []
    rest = value
    for _ in range(count):
        part = rest.astype(BF16)
        parts.append(part)
        rest = rest - part.astype(F32)
    return parts


def exact(form, left, right, count, split_left):
    total = None
    for part in pieces(left if split_left else right, count):
        term = form(part, right) if split_left else form(left, part)
        total = term if total is None else total + term
    return total


def head_masks(rows):
    lane_head = iota((rows, 256), 1) // 64
    return [lane_head == h for h in range(HEADS)]


def by_head(values, masks):
    out = values[3]
    for h in range(3):
        out = jnp.where(masks[h], values[h], out)
    return out


def expand(cols, first, masks):
    wide = [jnp.broadcast_to(cols[:, first + h : first + h + 1], (ROWS, 256)) for h in range(HEADS)]
    return by_head(wide, masks)


def columns(rows):
    missing = 128 - rows.shape[0]
    return jnp.transpose(jnp.concatenate([rows, jnp.zeros((missing, ROWS), F32)], axis=0))


def inclusive_masks():
    before = iota((ROWS, ROWS), 0) <= iota((ROWS, ROWS), 1)
    after = iota((ROWS, ROWS), 0) >= iota((ROWS, ROWS), 1)
    return jnp.where(before, 1.0, 0.0).astype(BF16), jnp.where(after, 1.0, 0.0).astype(BF16)


def squares_kernel(table, send):
    squares = jnp.concatenate([table[...] * table[...], jnp.zeros((112, 256), F32)], axis=0)
    sums = exact(mm_nt, jnp.ones((8, 256), BF16), squares, 3, False)
    send[...] = jnp.broadcast_to(sums[0:1][None], (GROUPS, 1, 128))


def fetch_kernel(
    table, gain, cw, cb, wb, wc, swt, step_bias, log_rate, skip_gain, dy,
    table_v, gain_v, cw_v, cb_v, wb_v, wc_v, swt_v, swx, bias, rate, skip, dy_v,
):
    table_v[...] = table[...]
    gain_v[...] = gain[...]
    cw_v[...] = cw[...]
    cb_v[...] = cb[...]
    wb_v[...] = wb[...]
    wc_v[...] = wc[...]
    swt_v[...] = swt[...]
    dy_v[...] = dy[...]
    place = iota((128, 64), 0)
    chosen = jnp.where(place // 8 * 4 + place % 4 == iota((128, 64), 1), 1.0, 0.0).astype(BF16)
    swx[...] = mm(chosen, swt[...]).astype(BF16)
    own = iota((8, HEADS), 0) % HEADS == iota((8, HEADS), 1)
    for source, column in ((step_bias, bias), (log_rate, rate)):
        column[...] = jnp.sum(jnp.where(own, source[...], 0.0), axis=1, keepdims=True)
    lane_head = iota((1, 256), 1) // 64
    row = jnp.zeros((1, 256), F32)
    for h in range(HEADS):
        row = jnp.where(lane_head == h, skip_gain[:, h : h + 1], row)
    skip[...] = row


def tokens_kernel(
    ids, ids_prev, ids_next, place, got, table, gain, cw, cb, wb, wc, swx,
    xf, xr, gf, gr, send, oht_ref, scale,
):
    total = got[0]
    for k in range(1, GROUPS):
        total = total + got[k]
    unit = lax.rsqrt(total / D + 1e-05)
    spread = jnp.transpose(jnp.broadcast_to(unit, (128, 128)))[0:16]
    scale[...] = spread
    unit = spread[:, 0:1]
    normed = (table[...] * unit * gain[...]).astype(BF16).astype(F32)
    vocab = iota((16, ROWS), 0)
    lane = iota((1, ROWS), 1)
    here = ids[...]
    following = jnp.where(place[...] == FAR * NEAR - 1, -1, ids_next[...])
    preceding = jnp.where(place[...] == 0, -1, ids_prev[...])
    hits = []
    for o in range(7):
        d = o - 3
        if d == 0:
            moved = here
        elif d > 0:
            ahead = pltpu.roll(following, ROWS - d, 1)
            moved = jnp.where(lane < ROWS - d, pltpu.roll(here, ROWS - d, 1), ahead)
        else:
            moved = jnp.where(lane >= -d, pltpu.roll(here, -d, 1), pltpu.roll(preceding, -d, 1))
        hits.append(jnp.where(moved == vocab, 1.0, 0.0))
    hits.append(jnp.zeros((16, ROWS), F32))
    oht = jnp.concatenate(hits, axis=0).astype(BF16)
    oht_ref[...] = oht
    none = jnp.zeros((16, 256), F32)
    taps = [cw[k : k + 1, :] * normed for k in range(4)]
    fwd_rows = jnp.concatenate([taps[3], taps[2], taps[1], taps[0], none, none, none, none], axis=0)
    rev_rows = jnp.concatenate([none, none, none, taps[0], taps[1], taps[2], taps[3], none], axis=0)
    halves = []
    for rows, x_ref, slope_ref in ((fwd_rows, xf, gf), (rev_rows, xr, gr)):
        pre = exact(mm_tn, oht, rows, 3, False) + cb[...]
        gate = 1.0 / (1.0 + jnp.exp(-pre))
        slope_ref[...] = gate * (1.0 + pre * (1.0 - gate))
        half = (pre * gate).astype(BF16)
        x_ref[...] = half
        halves.append(half)
    for member, half in enumerate(halves):
        for side, weight in ((0, wb), (128, wc)):
            at = member * 256 + side
            part = mm(half, weight[...]).astype(BF16).reshape(GROUPS, 16, 128)
            send[:, 0:16, at : at + 128] = part
    own = iota((128, 256), 0) % 8 < 4
    steps = jnp.where(own, mm_nt(swx[...], halves[0]), mm_nt(swx[...], halves[1]))
    high, low = pieces(steps, 2)
    send[:, 16:24, 0:256] = high.reshape(GROUPS, 8, 256)
    send[:, 16:24, 256:512] = low.reshape(GROUPS, 8, 256)


def reduce_kernel(got, bc, raw):
    total = got[0].astype(F32)
    for k in range(1, GROUPS):
        total = total + got[k].astype(F32)
    half = total[0:16].astype(BF16)
    bc[...] = jnp.broadcast_to(half[None], (GROUPS, 16, 512))
    raw[...] = total[16:24, 0:256] + total[16:24, 256:512]


def steps_kernel(
    raw, bias, rate, xf, xr, dy,
    cols_ref, rows_ref, weighted_ref, turned_ref, packed_ref,
):
    shifted = raw[...] + bias[...]
    step = jnp.maximum(shifted, 0.0) + jnp.log1p(jnp.exp(-jnp.abs(shifted)))
    slope = 1.0 / (1.0 + jnp.exp(-shifted))
    logdec = -step * jnp.exp(rate[...])
    before, after = inclusive_masks()
    fwd_row = iota((8, ROWS), 0) < 4
    prefix = exact(mm, logdec, before, 3, True)
    suffix = exact(mm, logdec, after, 3, True)
    cumul = jnp.where(fwd_row, prefix, suffix)
    fwd_one = iota((8, 1), 0) < 4
    ending = jnp.where(fwd_one, prefix[:, ROWS - 1 : ROWS], suffix[:, 0:1])
    closing = jnp.exp(ending - cumul)
    weight = closing * step
    grown = jnp.exp(cumul)
    rows_ref[...] = jnp.concatenate([cumul, step, weight, closing, slope, logdec], axis=0)
    cols = columns(jnp.concatenate([cumul, step, weight, grown], axis=0))
    cols_ref[...] = cols
    masks = head_masks(ROWS)
    dyf = dy[...].astype(F32)
    for br, x in ((0, xf), (1, xr)):
        weight_wide = expand(cols, 16 + 4 * br, masks)
        grown_wide = expand(cols, 24 + 4 * br, masks)
        weighted_ref[br] = (weight_wide * x[...].astype(F32)).astype(BF16)
        turned_ref[br] = (grown_wide * dyf).astype(BF16)
    decay = jnp.exp(ending)
    lane_head = iota((1, 256), 1) // 64
    fwd_decay = jnp.zeros((1, 256), F32)
    rev_decay = jnp.zeros((1, 256), F32)
    for h in range(HEADS):
        fwd_decay = jnp.where(lane_head == h, decay[h : h + 1], fwd_decay)
        rev_decay = jnp.where(lane_head == h, decay[h + 4 : h + 5], rev_decay)
    packed_ref[...] = split_decays(fwd_decay, rev_decay)


def split_decays(fwd_decay, rev_decay):
    row = iota((8, 256), 0)
    f_high = fwd_decay.astype(BF16).astype(F32)
    r_high = rev_decay.astype(BF16).astype(F32)
    packed = jnp.where(row == 0, f_high, 0.0)
    packed = jnp.where(row == 1, fwd_decay - f_high, packed)
    packed = jnp.where(row == 2, r_high, packed)
    return jnp.where(row == 3, rev_decay - r_high, packed)


def join_decays(packed):
    rows = packed.astype(F32)
    return rows[0:1] + rows[1:2], rows[2:3] + rows[3:4]


def states_kernel(bc, weighted, turned, packed, send):
    found = []
    for br in range(2):
        b = bc[:, br * 256 : br * 256 + 128]
        c = bc[:, br * 256 + 128 : br * 256 + 256]
        found.append((mm_tn(b, weighted[br]), mm_tn(c, turned[br])))
    chains = (found[0][0], found[1][1], found[1][0], found[0][1])
    for ch, state in enumerate(chains):
        send[:, ch * 16 : ch * 16 + 16, :] = state.astype(BF16).reshape(NEAR, 16, 256)
    send[:, 64:72, :] = jnp.broadcast_to(packed[...].astype(BF16)[None], (NEAR, 8, 256))


def advance(state, decay_first, decay_second, piece):
    return decay_first * state[0] + piece[0:16], decay_second * state[1] + piece[16:32]


def group_kernel(got, send):
    nothing = jnp.zeros((16, 256), F32)
    up = (nothing, nothing)
    down = (nothing, nothing)
    fwd_all = jnp.ones((1, 256), F32)
    rev_all = jnp.ones((1, 256), F32)
    for i in range(NEAR):
        fwd_decay, rev_decay = join_decays(got[i, 64:72, :])
        fwd_all = fwd_all * fwd_decay
        rev_all = rev_all * rev_decay
        up = advance(up, fwd_decay, rev_decay, got[i, 0:32, :].astype(F32))
        j = NEAR - 1 - i
        fwd_decay, rev_decay = join_decays(got[j, 64:72, :])
        down = advance(down, rev_decay, fwd_decay, got[j, 32:64, :].astype(F32))
    totals = jnp.concatenate([up[0], up[1], down[0], down[1], split_decays(fwd_all, rev_all)], axis=0)
    send[...] = jnp.broadcast_to(totals.astype(BF16)[None], (FAR, 72, 256))


def chain_kernel(got, far, place, out):
    here = place[...] // NEAR
    nothing = jnp.zeros((16, 256), F32)
    up = (nothing, nothing)
    down = (nothing, nothing)
    for g in range(FAR):
        fwd_decay, rev_decay = join_decays(far[g, 64:72, :])
        moved = advance(up, fwd_decay, rev_decay, far[g, 0:32, :].astype(F32))
        up = tuple(jnp.where(here > g, new, old) for new, old in zip(moved, up))
        k = FAR - 1 - g
        fwd_decay, rev_decay = join_decays(far[k, 64:72, :])
        moved = advance(down, rev_decay, fwd_decay, far[k, 32:64, :].astype(F32))
        down = tuple(jnp.where(here < k, new, old) for new, old in zip(moved, down))
    for i in range(NEAR):
        out[i, 0:16, :] = up[0].astype(BF16)
        out[i, 16:32, :] = up[1].astype(BF16)
        fwd_decay, rev_decay = join_decays(got[i, 64:72, :])
        up = advance(up, fwd_decay, rev_decay, got[i, 0:32, :].astype(F32))
        j = NEAR - 1 - i
        out[j, 32:48, :] = down[0].astype(BF16)
        out[j, 48:64, :] = down[1].astype(BF16)
        fwd_decay, rev_decay = join_decays(got[j, 64:72, :])
        down = advance(down, rev_decay, fwd_decay, got[j, 32:64, :].astype(F32))


def within_kernel(bc, cols_ref, rows_ref, xf, xr, dy, skip, y_ref, dxf, dxr, dbc, side, line):
    masks = head_masks(ROWS)
    t_at = iota((ROWS, ROWS), 0)
    s_at = iota((ROWS, ROWS), 1)
    lane = iota((ROWS, 128), 1)
    cols = cols_ref[...]
    dyh = dy[...]
    dyf = dyh.astype(F32)
    nothing = jnp.zeros((ROWS, 256), BF16)
    direct = skip[...] * dyf
    total = skip[...] * (xf[...].astype(F32) + xr[...].astype(F32))
    side_acc = jnp.zeros((ROWS, 128), F32)
    lines = []
    for br, x, dx_ref in ((0, xf, dxf), (1, xr, dxr)):
        xh = x[...]
        b = bc[:, br * 256 : br * 256 + 128]
        c = bc[:, br * 256 + 128 : br * 256 + 256]
        inner = mm_nt(c, b)
        causal = t_at >= s_at if br == 0 else t_at <= s_at
        dinner = jnp.zeros((ROWS, ROWS), F32)
        intra = []
        back = []
        for h in range(HEADS):
            at = 4 * br + h
            spread = cols[:, at : at + 1] - rows_ref[at : at + 1, :]
            decay = jnp.exp(jnp.where(causal, spread, -jnp.inf))
            step = rows_ref[8 + at : 9 + at, :]
            paced = decay * step
            mixing = (inner * paced).astype(BF16)
            intra.append(mm(mixing, xh))
            back.append(mm_tn(mixing, dyh))
            dmix = mm_nt(jnp.where(masks[h], dyh, nothing), xh)
            dinner = dinner + dmix * paced
            reach = dmix * decay * inner
            lines.append(jnp.sum(reach, axis=0, keepdims=True))
            flow = jnp.sum(reach * step, axis=1, keepdims=True)
            side_acc = jnp.where(lane == at, flow, side_acc)
        total = total + by_head(intra, masks)
        dx_ref[...] = direct + by_head(back, masks)
        dhalf = dinner.astype(BF16)
        dbc[:, br * 256 : br * 256 + 128] = mm_tn(dhalf, c).astype(BF16)
        dbc[:, br * 256 + 128 : br * 256 + 256] = mm(dhalf, b).astype(BF16)
    y_ref[...] = total
    side[...] = jnp.transpose(side_acc)[0:8]
    line[...] = jnp.concatenate(lines, axis=0)


def carried_kernel(
    got, bc, cols_ref, weighted, turned, rows_ref, xf, xr, dy,
    y0, dxf0, dxr0, dbc0, side, line, rate,
    out, dxf, dxr, send, draw_ref, small,
):
    dyf = dy[...].astype(F32)

    masks = head_masks(ROWS)
    cols = cols_ref[...]

    def state(ch):
        return got[:, ch * 16 : ch * 16 + 16, :].reshape(STATE, 256)

    row_at = iota((8, 256), 0)
    lane_head = iota((8, 256), 1) // 64
    total = y0[...]
    dp = jnp.zeros((8, ROWS), F32)
    dw = jnp.zeros((8, ROWS), F32)
    d_end = jnp.zeros((8, 1), F32)
    for br, x, dx0, dx_ref, at_state, at_grad in ((0, xf, dxf0, dxf, 0, 3), (1, xr, dxr0, dxr, 2, 1)):
        start_half = state(at_state)
        ahead_half = state(at_grad)
        b = bc[:, br * 256 : br * 256 + 128]
        c = bc[:, br * 256 + 128 : br * 256 + 256]
        heads = jnp.where(lane_head + 4 * br == row_at, 1.0, 0.0).astype(BF16)
        carried = expand(cols, 24 + 4 * br, masks) * mm(c, start_half)
        total = total + carried
        dp = dp + exact(mm_nt, heads, dyf * carried, 2, False)
        xv = x[...].astype(F32)
        toward = mm(b, ahead_half)
        dx_ref[...] = dx0[...] + expand(cols, 16 + 4 * br, masks) * toward
        dw = dw + exact(mm_nt, heads, xv * toward, 2, False)
        dc = mm_nt(turned[br], start_half)
        db = mm_nt(weighted[br], ahead_half)
        at = br * 256
        send[:, :, at : at + 128] = (dbc0[:, at : at + 128] + db).astype(BF16).reshape(16, 16, 128)
        send[:, :, at + 128 : at + 256] = (
            (dbc0[:, at + 128 : at + 256] + dc).astype(BF16).reshape(16, 16, 128)
        )
        both = jnp.sum(start_half.astype(F32) * ahead_half.astype(F32), axis=0, keepdims=True)
        spread = jnp.where(lane_head + 4 * br == row_at, both, 0.0)
        d_end = d_end + jnp.sum(spread, axis=1, keepdims=True)
    out[...] = total.astype(BF16)
    cumul = rows_ref[0:8]
    step = rows_ref[8:16]
    weight = rows_ref[16:24]
    closing = rows_ref[24:32]
    slope = rows_ref[32:40]
    logdec = rows_ref[40:48]
    at = iota((8, ROWS), 1)
    row = iota((8, ROWS), 0)
    last = at == jnp.where(row < 4, ROWS - 1, 0)
    pull = dw * weight
    ending = jnp.sum(jnp.where(last, cumul, 0.0), axis=1, keepdims=True)
    d_end = jnp.exp(ending) * d_end + jnp.sum(pull, axis=1, keepdims=True)
    dcumul = side[...] - step * line[...] + dp - pull + jnp.where(last, d_end, 0.0)
    before, after = inclusive_masks()
    prefix = exact(mm, dcumul, before, 3, True)
    suffix = exact(mm, dcumul, after, 3, True)
    dlog = jnp.where(row < 4, suffix, prefix)
    dstep = line[...] + dw * closing - dlog * jnp.exp(rate[...])
    draw = dstep * slope
    draw_ref[...] = draw.astype(BF16)
    d_bias = jnp.sum(draw, axis=1, keepdims=True)
    d_rate = jnp.sum(dlog * logdec, axis=1, keepdims=True)
    first = iota((1, 256), 1)
    bias_row = jnp.zeros((1, 256), F32)
    rate_row = jnp.zeros((1, 256), F32)
    for h in range(HEADS):
        bias_row = jnp.where(first == 64 * h, d_bias[h : h + 1] + d_bias[h + 4 : h + 5], bias_row)
        rate_row = jnp.where(first == 64 * h, d_rate[h : h + 1] + d_rate[h + 4 : h + 5], rate_row)
    skip_row = jnp.sum(dyf * (xf[...].astype(F32) + xr[...].astype(F32)), axis=0, keepdims=True)
    none = jnp.zeros((5, 256), F32)
    small[...] = jnp.concatenate([skip_row, bias_row, rate_row, none], axis=0)


def total_kernel(got, draw, send):
    total = got[0].astype(F32)
    for k in range(1, GROUPS):
        total = total + got[k].astype(F32)
    send[:, 0:16, :] = jnp.broadcast_to(total.astype(BF16)[None], (GROUPS, 16, 512))
    padded = jnp.concatenate([draw[...].astype(F32), jnp.zeros((8, 256), F32)], axis=1)
    send[:, 16:24, :] = jnp.broadcast_to(padded.astype(BF16)[None], (GROUPS, 8, 512))


def split_row(value, rows):
    row = iota((rows, 128), 0) % 32
    high = value.astype(BF16).astype(F32)
    return jnp.where(row == 0, high, 0.0) + jnp.where(row == 1, value - high, 0.0)


def project_back_kernel(
    got, xf, xr, gf, gr, dxf, dxr, wb, wc, swt, oht, table, scale, gain, cw, small,
    dpf, dpr, to_prev, to_next, send,
):
    dbc = got[:, 0:16, :].reshape(ROWS, 512)
    draw = got[:, 16:24, 0:256].astype(F32).reshape(128, 256).astype(BF16)
    pick_row = iota((128, 64), 0)
    pick_col = iota((128, 64), 1)
    wanted = pick_row // 8 * 4 + pick_row % 4
    normed = (table[...] * scale[:, 0:1] * gain[...]).astype(BF16).astype(F32)
    taps = [jnp.zeros((1, 256), F32)] * 4
    bias_row = jnp.zeros((1, 256), F32)
    wide = jnp.zeros((256, 256), F32)
    thin = jnp.zeros((256, 64), F32)
    ids_sum = jnp.zeros((16, 256), F32)
    for br, x, slope, dx, out in ((0, xf, gf, dxf, dpf), (1, xr, gr, dxr, dpr)):
        mine = (wanted == pick_col) & ((pick_row % 8 < 4) == (br == 0))
        dstep = mm_tn(draw, jnp.where(mine, 1.0, 0.0).astype(BF16)).astype(BF16)
        half = dbc[:, br * 256 : br * 256 + 256]
        into = mm_nt(half[:, 0:128], wb[...]) + mm_nt(half[:, 128:256], wc[...])
        into = into + mm(dstep, swt[...])
        whole = (dx[...] + into).astype(BF16).astype(F32)
        dpre = whole * slope[...]
        out[...] = dpre
        wide = wide + mm_tn(x[...], half)
        thin = thin + mm_tn(x[...], dstep)
        sums = exact(mm, oht[...], dpre, 2, False)
        for k in range(4):
            o = 3 - k if br == 0 else 3 + k
            block = sums[16 * o : 16 * o + 16]
            ids_sum = ids_sum + cw[k : k + 1] * block
            part = jnp.sum(normed * block, axis=0, keepdims=True)
            taps[k] = taps[k] + part
        bias_row = bias_row + jnp.sum(dpre, axis=0, keepdims=True)
    to_prev[...] = dpf[0:8]
    to_next[...] = dpr[ROWS - 8 : ROWS]
    shared = table[...] * gain[...] * ids_sum
    placed = jnp.concatenate(
        [jnp.zeros((88, 256), F32), shared, jnp.zeros((24, 256), F32)], axis=0
    )
    crossed = exact(mm_nt, jnp.ones((8, 256), BF16), placed, 3, False)[0:1]
    stacked = jnp.concatenate(
        [jnp.zeros((64, 256), F32), ids_sum] + taps + [bias_row, small[0:3], jnp.zeros((40, 256), F32)],
        axis=0,
    )
    last = jnp.concatenate([thin, jnp.zeros((256, 64), F32)], axis=1) + jnp.transpose(stacked)
    last = last + split_row(crossed, 256)
    send[:, 0:32, :] = wide[:, 0:128].astype(BF16).reshape(NEAR, 32, 128)
    send[:, 32:64, :] = wide[:, 128:256].astype(BF16).reshape(NEAR, 32, 128)
    send[:, 64:96, :] = last.astype(BF16).reshape(NEAR, 32, 128)


def ahead_kernel(dpf, from_next, cw, part, ahead):
    ahead[0:ROWS] = dpf[...]
    ahead[ROWS : ROWS + 8] = from_next[...]
    total = cw[0:1] * ahead[0:ROWS]
    for k in range(1, 4):
        total = total + cw[k : k + 1] * ahead[k : k + ROWS]
    part[...] = total


def normed_kernel(part, dpr, from_prev, cw, gain, table, oht, gn_ref, cross, behind):
    behind[0:8] = from_prev[...]
    behind[8 : ROWS + 8] = dpr[...]
    dn = part[...]
    for k in range(4):
        dn = dn + cw[k : k + 1] * behind[8 - k : 8 - k + ROWS]
    gn = dn.astype(BF16)
    gn_ref[...] = gn
    rated = exact(mm_tn, oht[48:64], table[...] * gain[...], 3, False)
    ones = jnp.ones((8, 256), BF16)
    cross[...] = exact(mm_nt, ones, gn.astype(F32) * rated, 3, False)[0:1]


def embedded_kernel(got, gn, gain, table, scale, oht, out):
    total = got[0]
    for k in range(1, GROUPS):
        total = total + got[k]
    cross = columns(jnp.broadcast_to(total[:, 0:256], (8, ROWS)))[:, 0:1]
    own = oht[48:64]
    unit = scale[:, 0:1]
    turned = exact(mm_tn, own, unit * gain[...], 3, False)
    shrunk = exact(mm_tn, own, table[...] * (unit * unit * unit / D), 3, False)
    out[...] = (turned * gn[...].astype(F32) - shrunk * cross).astype(BF16)


def near_kernel(got, send):
    total = got[0].astype(F32)
    for k in range(1, NEAR):
        total = total + got[k].astype(F32)
    last = total[64:96]
    lane = iota((32, 128), 1)
    crossed = jnp.where((lane >= 88) & (lane < 104), last, 0.0)
    last = last - crossed + split_row(jnp.sum(crossed, axis=0, keepdims=True), 32)
    total = jnp.concatenate([total[0:64], last], axis=0)
    send[...] = jnp.broadcast_to(total.astype(BF16)[None], (FAR, 96, 128))


def far_kernel(got, cross, send, payload):
    total = got[0].astype(F32)
    for k in range(1, FAR):
        total = total + got[k].astype(F32)
    send[...] = jnp.broadcast_to(total.astype(BF16)[None], (NEAR, 96, 128))
    lane = iota((1, 128), 1)
    both = total[64:65] + total[65:66]
    crossed = jnp.where((lane >= 88) & (lane < 104), both, 0.0)
    row = jnp.concatenate([cross[...], crossed], axis=1)
    payload[...] = jnp.broadcast_to(row[None], (GROUPS, 1, 384))


def finish_kernel(got, cross, table, scale, gain, gt, gg, gcw, gcb, gwb, gwc, gswt, gsb, glr, gsg):
    gwb[...] = got[:, 0:32, :].astype(F32).reshape(256, 128)
    gwc[...] = got[:, 32:64, :].astype(F32).reshape(256, 128)
    rows = jnp.transpose(got[:, 64:96, :].astype(F32).reshape(256, 128))
    gswt[...] = rows[0:64]
    sums = rows[64:80]
    here = cross[0]
    for k in range(1, GROUPS):
        here = here + cross[k]
    crossed = jnp.transpose(jnp.broadcast_to(here[:, 256:384], (128, 128)))[88:104, 0:1]
    unit = scale[:, 0:1]
    gt[...] = unit * gain[...] * sums - table[...] * (unit * unit * unit / D) * crossed
    gg[...] = jnp.sum(table[...] * unit * sums, axis=0, keepdims=True)
    gcw[...] = rows[80:84]
    gcb[...] = rows[84:85]
    lane = iota((8, 256), 1)
    tail = rows[80:88]
    picked = iota((8, 4), 1)
    result = jnp.zeros((8, 4), F32)
    for h in range(HEADS):
        part = jnp.sum(jnp.where(lane // 64 == h, tail, 0.0), axis=1, keepdims=True)
        result = jnp.where(picked == h, part, result)
    gsg[...] = result[5:6]
    gsb[...] = result[6:7]
    glr[...] = result[7:8]


def swap(value, axis):
    return lax.all_to_all(value, axis, 0, 0, tiled=True)


def shift(value, pairs):
    return lax.ppermute(value, CTX, pairs)


def mixer(
    token_ids,
    table,
    norm_gain,
    conv_weight,
    conv_bias,
    weight_b,
    weight_c,
    step_weight,
    step_bias,
    log_rate,
    skip_gain,
    out_grad,
):
    size = lax.axis_size(CTX)
    up = [(i, i + 1) for i in range(size - 1)]
    down = [(i + 1, i) for i in range(size - 1)]
    edge = ((8, 256), F32)
    square = ((ROWS, 256), F32)
    half_square = ((ROWS, 256), BF16)
    (squares,) = call(squares_kernel, (((GROUPS, 1, 128), F32),), table, near=False)
    squares = swap(squares, "fsdp")
    ids = token_ids[None]
    ids_prev = shift(ids, up)
    ids_next = shift(ids, down)
    place = lax.axis_index(CTX).reshape(1, 1)
    table, gain, cw, cb, wb, wc, swt, swx, bias, rate, skip, dy = call(
        fetch_kernel,
        (
            ((16, 256), F32),
            ((1, 256), F32),
            ((4, 256), F32),
            ((1, 256), F32),
            ((256, 128), BF16),
            ((256, 128), BF16),
            ((64, 256), BF16),
            ((128, 256), BF16),
            ((8, 1), F32),
            ((8, 1), F32),
            ((1, 256), F32),
            half_square,
        ),
        table, norm_gain[None], conv_weight, conv_bias[None], weight_b, weight_c,
        jnp.transpose(step_weight), step_bias[None], log_rate[None], skip_gain[None], out_grad,
        near=False,
    )
    xf, xr, gf, gr, part, oht, scale = call(
        tokens_kernel,
        (
            half_square,
            half_square,
            square,
            square,
            ((GROUPS, 24, 512), BF16),
            ((128, 256), BF16),
            ((16, 128), F32),
        ),
        ids, ids_prev, ids_next, place, squares, table, gain, cw, cb, wb, wc, swx,
    )
    bc, raw = call(reduce_kernel, (((GROUPS, 16, 512), BF16), ((8, 256), F32)), swap(part, "fsdp"))
    bc = swap(bc, "fsdp").reshape(ROWS, 512)
    half_pair = ((2, ROWS, 256), BF16)
    cols, rows, weighted, turned, packed = call(
        steps_kernel,
        (((ROWS, 128), F32), ((48, ROWS), F32), half_pair, half_pair, edge),
        raw, bias, rate, xf, xr, dy,
    )
    (states,) = call(
        states_kernel, (((NEAR, 72, 256), BF16),), bc, weighted, turned, packed
    )
    arrived = swap(states, BESIDE)
    y0, dxf0, dxr0, dbc0, side, line = call(
        within_kernel,
        (square, square, square, ((ROWS, 512), BF16), edge, edge),
        bc, cols, rows, xf, xr, dy, skip,
    )
    (groups,) = call(group_kernel, (((FAR, 72, 256), BF16),), arrived)
    groups = swap(groups, "zh")
    (entering,) = call(chain_kernel, (((NEAR, 64, 256), BF16),), arrived, groups, place)
    entering = swap(entering, BESIDE)
    mixer_out, dxf, dxr, dpart, draw, small = call(
        carried_kernel,
        (
            half_square,
            square,
            square,
            ((GROUPS, 16, 512), BF16),
            ((8, 256), BF16),
            edge,
        ),
        entering, bc, cols, weighted, turned, rows, xf, xr, dy,
        y0, dxf0, dxr0, dbc0, side, line, rate,
        final=(0,),
    )
    (totals,) = call(total_kernel, (((GROUPS, 24, 512), BF16),), swap(dpart, "fsdp"), draw)
    dpf, dpr, to_prev, to_next, gsend = call(
        project_back_kernel,
        (square, square, edge, edge, ((NEAR, 96, 128), BF16)),
        swap(totals, "fsdp"), xf, xr, gf, gr, dxf, dxr, wb,
        wc, swt, oht, table, scale, gain, cw, small,
    )
    from_next = shift(to_prev, down)
    from_prev = shift(to_next, up)
    reduced = swap(gsend, BESIDE)
    (ahead,) = call(
        ahead_kernel, (square,), dpf, from_next, cw, scratch=[VMEM((ROWS + 8, 256), F32)]
    )
    gn, cross = call(
        normed_kernel,
        (half_square, ((1, 256), F32)),
        ahead, dpr, from_prev, cw, gain, table, oht,
        scratch=[VMEM((ROWS + 8, 256), F32)],
    )
    (summed,) = call(near_kernel, (((FAR, 96, 128), BF16),), reduced)
    summed = swap(summed, "zh")
    gathered, payload = call(
        far_kernel, (((NEAR, 96, 128), BF16), ((GROUPS, 1, 384), F32)), summed, cross
    )
    crossed = swap(payload, "fsdp")
    (grad_embedded,) = call(
        embedded_kernel, (half_square,), crossed, gn, gain, table, scale, oht, final=(0,)
    )
    outs = call(
        finish_kernel,
        (
            ((16, 256), F32),
            ((1, 256), F32),
            ((4, 256), F32),
            ((1, 256), F32),
            ((256, 128), F32),
            ((256, 128), F32),
            ((64, 256), F32),
            ((1, 4), F32),
            ((1, 4), F32),
            ((1, 4), F32),
        ),
        swap(gathered, BESIDE), crossed, table, scale, gain,
        final=range(10),
    )
    gt, gg, gcw, gcb, gwb, gwc, gswt, gsb, glr, gsg = outs
    return (
        mixer_out,
        grad_embedded,
        gt,
        gg[0],
        gcw,
        gcb[0],
        gwb,
        gwc,
        jnp.transpose(gswt),
        gsb[0],
        glr[0],
        gsg[0],
    )


def solution(mesh):
    devices = mesh.devices.reshape(mesh.shape["fsdp"], FAR, 4, 2)
    mesh = jax.sharding.Mesh(devices, ("fsdp",) + CTX)
    return jax.shard_map(
        mixer,
        mesh=mesh,
        in_specs=(
            P(CTX),
            P(None, "fsdp"),
            P("fsdp"),
            P(None, "fsdp"),
            P("fsdp"),
            P("fsdp", None),
            P("fsdp", None),
            P("fsdp", None),
            P("fsdp"),
            P("fsdp"),
            P("fsdp"),
            P(CTX, "fsdp"),
        ),
        out_specs=(
            P(CTX, "fsdp"),
            P(CTX, "fsdp"),
            P(None, "fsdp"),
            P("fsdp"),
            P(None, "fsdp"),
            P("fsdp"),
            P("fsdp", None),
            P("fsdp", None),
            P("fsdp", None),
            P("fsdp"),
            P("fsdp"),
            P("fsdp"),
        ),
        check_vma=False,
    )
```

```python
import jax
import jax.numpy as jnp
from jax import lax
from jax.sharding import PartitionSpec as P
from jax.experimental import pallas as pl
from jax.experimental.pallas import tpu as pltpu

D = 4096
ROWS = 256
HEADS = 4
STATE = 128
GROUPS = 16
NEAR = 8
FAR = 4
CTX = ("zh", "zl", "xh")
BESIDE = ("zl", "xh")
F32 = jnp.float32
BF16 = jnp.bfloat16
VMEM = pltpu.VMEM


def call(kernel, outs, *args, final=(), scratch=(), near=True):
    shapes = tuple(
        jax.ShapeDtypeStruct(shape, kind) if i in final else VMEM(shape, kind)
        for i, (shape, kind) in enumerate(outs)
    )
    space = VMEM if near else pltpu.HBM
    args = [pltpu.with_memory_space_constraint(arg, space) for arg in args]
    return pl.pallas_call(
        kernel,
        out_shape=shapes,
        scratch_shapes=scratch,
        compiler_params=pltpu.CompilerParams(vmem_limit_bytes=24 << 20),
    )(*args)


def iota(shape, dim):
    return lax.broadcasted_iota(jnp.int32, shape, dim)


def mm(left, right):
    return lax.dot_general(left, right, (((1,), (0,)), ((), ())), preferred_element_type=F32)


def mm_tn(left, right):
    return lax.dot_general(left, right, (((0,), (0,)), ((), ())), preferred_element_type=F32)


def mm_nt(left, right):
    return lax.dot_general(left, right, (((1,), (1,)), ((), ())), preferred_element_type=F32)


def pieces(value, count):
    parts = []
    rest = value
    for _ in range(count):
        part = rest.astype(BF16)
        parts.append(part)
        rest = rest - part.astype(F32)
    return parts


def exact(form, left, right, count, split_left):
    total = None
    for part in pieces(left if split_left else right, count):
        term = form(part, right) if split_left else form(left, part)
        total = term if total is None else total + term
    return total


def head_masks(rows):
    lane_head = iota((rows, 256), 1) // 64
    return [lane_head == h for h in range(HEADS)]


def by_head(values, masks):
    out = values[3]
    for h in range(3):
        out = jnp.where(masks[h], values[h], out)
    return out


def expand(cols, first, masks):
    wide = [jnp.broadcast_to(cols[:, first + h : first + h + 1], (ROWS, 256)) for h in range(HEADS)]
    return by_head(wide, masks)


def columns(rows):
    missing = 128 - rows.shape[0]
    return jnp.transpose(jnp.concatenate([rows, jnp.zeros((missing, ROWS), F32)], axis=0))


def inclusive_masks():
    before = iota((ROWS, ROWS), 0) <= iota((ROWS, ROWS), 1)
    after = iota((ROWS, ROWS), 0) >= iota((ROWS, ROWS), 1)
    return jnp.where(before, 1.0, 0.0).astype(BF16), jnp.where(after, 1.0, 0.0).astype(BF16)


def squares_kernel(table, ids, send, ids_v):
    ids_v[...] = ids[...]
    squares = jnp.concatenate([table[...] * table[...], jnp.zeros((112, 256), F32)], axis=0)
    sums = exact(mm_nt, jnp.ones((8, 256), BF16), squares, 3, False)
    send[...] = jnp.broadcast_to(sums[0:1][None], (GROUPS, 1, 128))


def fetch_kernel(
    table, gain, cw, cb, wb, wc, swt, step_bias, log_rate, skip_gain, dy,
    table_v, gain_v, cw_v, cb_v, wb_v, wc_v, swt_v, swx, bias, rate, skip, dy_v,
):
    table_v[...] = table[...]
    gain_v[...] = gain[...]
    cw_v[...] = cw[...]
    cb_v[...] = cb[...]
    wb_v[...] = wb[...]
    wc_v[...] = wc[...]
    swt_v[...] = swt[...]
    dy_v[...] = dy[...]
    place = iota((128, 64), 0)
    chosen = jnp.where(place // 8 * 4 + place % 4 == iota((128, 64), 1), 1.0, 0.0).astype(BF16)
    swx[...] = mm(chosen, swt[...]).astype(BF16)
    own = iota((8, HEADS), 0) % HEADS == iota((8, HEADS), 1)
    for source, column in ((step_bias, bias), (log_rate, rate)):
        column[...] = jnp.sum(jnp.where(own, source[...], 0.0), axis=1, keepdims=True)
    lane_head = iota((1, 256), 1) // 64
    row = jnp.zeros((1, 256), F32)
    for h in range(HEADS):
        row = jnp.where(lane_head == h, skip_gain[:, h : h + 1], row)
    skip[...] = row


def tokens_kernel(
    ids, ids_pair, ids_side, place, got, table, gain, cw, cb, wb, wc, swx,
    xf, xr, gf, gr, send, oht_ref, scale,
):
    total = got[0]
    for k in range(1, GROUPS):
        total = total + got[k]
    unit = lax.rsqrt(total / D + 1e-05)
    spread = jnp.transpose(jnp.broadcast_to(unit, (128, 128)))[0:16]
    scale[...] = spread
    unit = spread[:, 0:1]
    normed = (table[...] * unit * gain[...]).astype(BF16).astype(F32)
    vocab = iota((16, ROWS), 0)
    lane = iota((1, ROWS), 1)
    here = ids[...]
    even = place[...] % 2 == 0
    following = jnp.where(even, ids_pair[...], ids_side[...])
    following = jnp.where(place[...] == FAR * NEAR - 1, -1, following)
    preceding = jnp.where(even, ids_side[...], ids_pair[...])
    preceding = jnp.where(place[...] == 0, -1, preceding)
    hits = []
    for o in range(7):
        d = o - 3
        if d == 0:
            moved = here
        elif d > 0:
            ahead = pltpu.roll(following, ROWS - d, 1)
            moved = jnp.where(lane < ROWS - d, pltpu.roll(here, ROWS - d, 1), ahead)
        else:
            moved = jnp.where(lane >= -d, pltpu.roll(here, -d, 1), pltpu.roll(preceding, -d, 1))
        hits.append(jnp.where(moved == vocab, 1.0, 0.0))
    hits.append(jnp.zeros((16, ROWS), F32))
    oht = jnp.concatenate(hits, axis=0).astype(BF16)
    oht_ref[...] = oht
    none = jnp.zeros((16, 256), F32)
    taps = [cw[k : k + 1, :] * normed for k in range(4)]
    fwd_rows = jnp.concatenate([taps[3], taps[2], taps[1], taps[0], none, none, none, none], axis=0)
    rev_rows = jnp.concatenate([none, none, none, taps[0], taps[1], taps[2], taps[3], none], axis=0)
    halves = []
    for rows, x_ref, slope_ref in ((fwd_rows, xf, gf), (rev_rows, xr, gr)):
        pre = exact(mm_tn, oht, rows, 3, False) + cb[...]
        gate = 1.0 / (1.0 + jnp.exp(-pre))
        slope_ref[...] = gate * (1.0 + pre * (1.0 - gate))
        half = (pre * gate).astype(BF16)
        x_ref[...] = half
        halves.append(half)
    for member, half in enumerate(halves):
        for side, weight in ((0, wb), (128, wc)):
            at = member * 256 + side
            part = mm(half, weight[...]).astype(BF16).reshape(GROUPS, 16, 128)
            send[:, 0:16, at : at + 128] = part
    own = iota((128, 256), 0) % 8 < 4
    steps = jnp.where(own, mm_nt(swx[...], halves[0]), mm_nt(swx[...], halves[1]))
    high, low = pieces(steps, 2)
    send[:, 16:24, 0:256] = high.reshape(GROUPS, 8, 256)
    send[:, 16:24, 256:512] = low.reshape(GROUPS, 8, 256)


def reduce_kernel(got, bc, raw):
    total = got[0].astype(F32)
    for k in range(1, GROUPS):
        total = total + got[k].astype(F32)
    half = total[0:16].astype(BF16)
    bc[...] = jnp.broadcast_to(half[None], (GROUPS, 16, 512))
    raw[...] = total[16:24, 0:256] + total[16:24, 256:512]


def steps_kernel(
    raw, bias, rate, xf, xr, dy,
    cols_ref, rows_ref, weighted_ref, turned_ref, packed_ref,
):
    shifted = raw[...] + bias[...]
    step = jnp.maximum(shifted, 0.0) + jnp.log1p(jnp.exp(-jnp.abs(shifted)))
    slope = 1.0 / (1.0 + jnp.exp(-shifted))
    logdec = -step * jnp.exp(rate[...])
    before, after = inclusive_masks()
    fwd_row = iota((8, ROWS), 0) < 4
    prefix = exact(mm, logdec, before, 3, True)
    suffix = exact(mm, logdec, after, 3, True)
    cumul = jnp.where(fwd_row, prefix, suffix)
    fwd_one = iota((8, 1), 0) < 4
    ending = jnp.where(fwd_one, prefix[:, ROWS - 1 : ROWS], suffix[:, 0:1])
    closing = jnp.exp(ending - cumul)
    weight = closing * step
    grown = jnp.exp(cumul)
    rows_ref[...] = jnp.concatenate([cumul, step, weight, closing, slope, logdec], axis=0)
    cols = columns(jnp.concatenate([cumul, step, weight, grown], axis=0))
    cols_ref[...] = cols
    masks = head_masks(ROWS)
    dyf = dy[...].astype(F32)
    for br, x in ((0, xf), (1, xr)):
        weight_wide = expand(cols, 16 + 4 * br, masks)
        grown_wide = expand(cols, 24 + 4 * br, masks)
        weighted_ref[br] = (weight_wide * x[...].astype(F32)).astype(BF16)
        turned_ref[br] = (grown_wide * dyf).astype(BF16)
    decay = jnp.exp(ending)
    lane_head = iota((1, 256), 1) // 64
    fwd_decay = jnp.zeros((1, 256), F32)
    rev_decay = jnp.zeros((1, 256), F32)
    for h in range(HEADS):
        fwd_decay = jnp.where(lane_head == h, decay[h : h + 1], fwd_decay)
        rev_decay = jnp.where(lane_head == h, decay[h + 4 : h + 5], rev_decay)
    packed_ref[...] = split_decays(fwd_decay, rev_decay)


def split_decays(fwd_decay, rev_decay):
    row = iota((8, 256), 0)
    f_high = fwd_decay.astype(BF16).astype(F32)
    r_high = rev_decay.astype(BF16).astype(F32)
    packed = jnp.where(row == 0, f_high, 0.0)
    packed = jnp.where(row == 1, fwd_decay - f_high, packed)
    packed = jnp.where(row == 2, r_high, packed)
    return jnp.where(row == 3, rev_decay - r_high, packed)


def join_decays(packed):
    rows = packed.astype(F32)
    return rows[0:1] + rows[1:2], rows[2:3] + rows[3:4]


def states_kernel(bc, weighted, turned, packed, send):
    found = []
    for br in range(2):
        b = bc[:, br * 256 : br * 256 + 128]
        c = bc[:, br * 256 + 128 : br * 256 + 256]
        found.append((mm_tn(b, weighted[br]), mm_tn(c, turned[br])))
    chains = (found[0][0], found[1][1], found[1][0], found[0][1])
    for ch, state in enumerate(chains):
        send[:, ch * 16 : ch * 16 + 16, :] = state.astype(BF16).reshape(NEAR, 16, 256)
    send[:, 64:72, :] = jnp.broadcast_to(packed[...].astype(BF16)[None], (NEAR, 8, 256))


def advance(state, decay_first, decay_second, piece):
    return decay_first * state[0] + piece[0:16], decay_second * state[1] + piece[16:32]


def group_kernel(got, send):
    nothing = jnp.zeros((16, 256), F32)
    up = (nothing, nothing)
    down = (nothing, nothing)
    fwd_all = jnp.ones((1, 256), F32)
    rev_all = jnp.ones((1, 256), F32)
    for i in range(NEAR):
        fwd_decay, rev_decay = join_decays(got[i, 64:72, :])
        fwd_all = fwd_all * fwd_decay
        rev_all = rev_all * rev_decay
        up = advance(up, fwd_decay, rev_decay, got[i, 0:32, :].astype(F32))
        j = NEAR - 1 - i
        fwd_decay, rev_decay = join_decays(got[j, 64:72, :])
        down = advance(down, rev_decay, fwd_decay, got[j, 32:64, :].astype(F32))
    totals = jnp.concatenate([up[0], up[1], down[0], down[1], split_decays(fwd_all, rev_all)], axis=0)
    send[...] = jnp.broadcast_to(totals.astype(BF16)[None], (FAR, 72, 256))


def chain_kernel(got, far, place, out):
    here = place[...] // NEAR
    nothing = jnp.zeros((16, 256), F32)
    up = (nothing, nothing)
    down = (nothing, nothing)
    for g in range(FAR):
        fwd_decay, rev_decay = join_decays(far[g, 64:72, :])
        moved = advance(up, fwd_decay, rev_decay, far[g, 0:32, :].astype(F32))
        up = tuple(jnp.where(here > g, new, old) for new, old in zip(moved, up))
        k = FAR - 1 - g
        fwd_decay, rev_decay = join_decays(far[k, 64:72, :])
        moved = advance(down, rev_decay, fwd_decay, far[k, 32:64, :].astype(F32))
        down = tuple(jnp.where(here < k, new, old) for new, old in zip(moved, down))
    for i in range(NEAR):
        out[i, 0:16, :] = up[0].astype(BF16)
        out[i, 16:32, :] = up[1].astype(BF16)
        fwd_decay, rev_decay = join_decays(got[i, 64:72, :])
        up = advance(up, fwd_decay, rev_decay, got[i, 0:32, :].astype(F32))
        j = NEAR - 1 - i
        out[j, 32:48, :] = down[0].astype(BF16)
        out[j, 48:64, :] = down[1].astype(BF16)
        fwd_decay, rev_decay = join_decays(got[j, 64:72, :])
        down = advance(down, rev_decay, fwd_decay, got[j, 32:64, :].astype(F32))


def within_kernel(bc, cols_ref, rows_ref, xf, xr, dy, skip, y_ref, dxf, dxr, dbc, side, line):
    masks = head_masks(ROWS)
    t_at = iota((ROWS, ROWS), 0)
    s_at = iota((ROWS, ROWS), 1)
    lane = iota((ROWS, 128), 1)
    cols = cols_ref[...]
    dyh = dy[...]
    dyf = dyh.astype(F32)
    nothing = jnp.zeros((ROWS, 256), BF16)
    direct = skip[...] * dyf
    total = skip[...] * (xf[...].astype(F32) + xr[...].astype(F32))
    side_acc = jnp.zeros((ROWS, 128), F32)
    lines = []
    for br, x, dx_ref in ((0, xf, dxf), (1, xr, dxr)):
        xh = x[...]
        b = bc[:, br * 256 : br * 256 + 128]
        c = bc[:, br * 256 + 128 : br * 256 + 256]
        inner = mm_nt(c, b)
        causal = t_at >= s_at if br == 0 else t_at <= s_at
        dinner = jnp.zeros((ROWS, ROWS), F32)
        intra = []
        back = []
        for h in range(HEADS):
            at = 4 * br + h
            spread = cols[:, at : at + 1] - rows_ref[at : at + 1, :]
            decay = jnp.exp(jnp.where(causal, spread, -jnp.inf))
            step = rows_ref[8 + at : 9 + at, :]
            paced = decay * step
            mixing = (inner * paced).astype(BF16)
            intra.append(mm(mixing, xh))
            back.append(mm_tn(mixing, dyh))
            dmix = mm_nt(jnp.where(masks[h], dyh, nothing), xh)
            dinner = dinner + dmix * paced
            reach = dmix * decay * inner
            lines.append(jnp.sum(reach, axis=0, keepdims=True))
            flow = jnp.sum(reach * step, axis=1, keepdims=True)
            side_acc = jnp.where(lane == at, flow, side_acc)
        total = total + by_head(intra, masks)
        dx_ref[...] = direct + by_head(back, masks)
        dhalf = dinner.astype(BF16)
        dbc[:, br * 256 : br * 256 + 128] = mm_tn(dhalf, c).astype(BF16)
        dbc[:, br * 256 + 128 : br * 256 + 256] = mm(dhalf, b).astype(BF16)
    y_ref[...] = total
    side[...] = jnp.transpose(side_acc)[0:8]
    line[...] = jnp.concatenate(lines, axis=0)


def state(got, ch):
    return got[:, ch * 16 : ch * 16 + 16, :].reshape(STATE, 256)


def partials_kernel(got, weighted, turned, dbc0, send):
    for br, at_state, at_grad in ((0, 0, 3), (1, 2, 1)):
        dc = mm_nt(turned[br], state(got, at_state))
        db = mm_nt(weighted[br], state(got, at_grad))
        at = br * 256
        part = dbc0[:, at : at + 256].astype(F32) + jnp.concatenate([db, dc], axis=1)
        send[:, :, at : at + 256] = part.astype(BF16).reshape(16, 16, 256)


def carried_kernel(
    got, bc, cols_ref, rows_ref, xf, xr, dy, y0, dxf0, dxr0, side, line, rate,
    out, dxf, dxr, draw_ref, small,
):
    dyf = dy[...].astype(F32)

    masks = head_masks(ROWS)
    cols = cols_ref[...]

    row_at = iota((8, 256), 0)
    lane_head = iota((8, 256), 1) // 64
    total = y0[...]
    dp = jnp.zeros((8, ROWS), F32)
    dw = jnp.zeros((8, ROWS), F32)
    d_end = jnp.zeros((8, 1), F32)
    for br, x, dx0, dx_ref, at_state, at_grad in ((0, xf, dxf0, dxf, 0, 3), (1, xr, dxr0, dxr, 2, 1)):
        start_half = state(got, at_state)
        ahead_half = state(got, at_grad)
        b = bc[:, br * 256 : br * 256 + 128]
        c = bc[:, br * 256 + 128 : br * 256 + 256]
        heads = jnp.where(lane_head + 4 * br == row_at, 1.0, 0.0).astype(BF16)
        carried = expand(cols, 24 + 4 * br, masks) * mm(c, start_half)
        total = total + carried
        dp = dp + exact(mm_nt, heads, dyf * carried, 2, False)
        xv = x[...].astype(F32)
        toward = mm(b, ahead_half)
        dx_ref[...] = dx0[...] + expand(cols, 16 + 4 * br, masks) * toward
        dw = dw + exact(mm_nt, heads, xv * toward, 2, False)
        both = jnp.sum(start_half.astype(F32) * ahead_half.astype(F32), axis=0, keepdims=True)
        spread = jnp.where(lane_head + 4 * br == row_at, both, 0.0)
        d_end = d_end + jnp.sum(spread, axis=1, keepdims=True)
    out[...] = total.astype(BF16)
    cumul = rows_ref[0:8]
    step = rows_ref[8:16]
    weight = rows_ref[16:24]
    closing = rows_ref[24:32]
    slope = rows_ref[32:40]
    logdec = rows_ref[40:48]
    at = iota((8, ROWS), 1)
    row = iota((8, ROWS), 0)
    last = at == jnp.where(row < 4, ROWS - 1, 0)
    pull = dw * weight
    ending = jnp.sum(jnp.where(last, cumul, 0.0), axis=1, keepdims=True)
    d_end = jnp.exp(ending) * d_end + jnp.sum(pull, axis=1, keepdims=True)
    dcumul = side[...] - step * line[...] + dp - pull + jnp.where(last, d_end, 0.0)
    before, after = inclusive_masks()
    prefix = exact(mm, dcumul, before, 3, True)
    suffix = exact(mm, dcumul, after, 3, True)
    dlog = jnp.where(row < 4, suffix, prefix)
    dstep = line[...] + dw * closing - dlog * jnp.exp(rate[...])
    draw = dstep * slope
    draw_ref[...] = draw.astype(BF16)
    d_bias = jnp.sum(draw, axis=1, keepdims=True)
    d_rate = jnp.sum(dlog * logdec, axis=1, keepdims=True)
    first = iota((1, 256), 1)
    bias_row = jnp.zeros((1, 256), F32)
    rate_row = jnp.zeros((1, 256), F32)
    for h in range(HEADS):
        bias_row = jnp.where(first == 64 * h, d_bias[h : h + 1] + d_bias[h + 4 : h + 5], bias_row)
        rate_row = jnp.where(first == 64 * h, d_rate[h : h + 1] + d_rate[h + 4 : h + 5], rate_row)
    skip_row = jnp.sum(dyf * (xf[...].astype(F32) + xr[...].astype(F32)), axis=0, keepdims=True)
    none = jnp.zeros((5, 256), F32)
    small[...] = jnp.concatenate([skip_row, bias_row, rate_row, none], axis=0)


def total_kernel(got, draw, send):
    total = got[0].astype(F32)
    for k in range(1, GROUPS):
        total = total + got[k].astype(F32)
    send[:, 0:16, :] = jnp.broadcast_to(total.astype(BF16)[None], (GROUPS, 16, 512))
    padded = jnp.concatenate([draw[...].astype(F32), jnp.zeros((8, 256), F32)], axis=1)
    send[:, 16:24, :] = jnp.broadcast_to(padded.astype(BF16)[None], (GROUPS, 8, 512))


def split_row(value, rows):
    row = iota((rows, 128), 0) % 32
    high = value.astype(BF16).astype(F32)
    return jnp.where(row == 0, high, 0.0) + jnp.where(row == 1, value - high, 0.0)


def project_back_kernel(
    got, xf, xr, gf, gr, dxf, dxr, wb, wc, swt, oht, table, scale, gain, cw, small,
    dpf, dpr, to_prev, to_next, send,
):
    dbc = got[:, 0:16, :].reshape(ROWS, 512)
    draw = got[:, 16:24, 0:256].astype(F32).reshape(128, 256).astype(BF16)
    pick_row = iota((128, 64), 0)
    pick_col = iota((128, 64), 1)
    wanted = pick_row // 8 * 4 + pick_row % 4
    normed = (table[...] * scale[:, 0:1] * gain[...]).astype(BF16).astype(F32)
    taps = [jnp.zeros((1, 256), F32)] * 4
    bias_row = jnp.zeros((1, 256), F32)
    wide = jnp.zeros((256, 256), F32)
    thin = jnp.zeros((256, 64), F32)
    ids_sum = jnp.zeros((16, 256), F32)
    for br, x, slope, dx, out in ((0, xf, gf, dxf, dpf), (1, xr, gr, dxr, dpr)):
        mine = (wanted == pick_col) & ((pick_row % 8 < 4) == (br == 0))
        dstep = mm_tn(draw, jnp.where(mine, 1.0, 0.0).astype(BF16)).astype(BF16)
        half = dbc[:, br * 256 : br * 256 + 256]
        into = mm_nt(half[:, 0:128], wb[...]) + mm_nt(half[:, 128:256], wc[...])
        into = into + mm(dstep, swt[...])
        whole = (dx[...] + into).astype(BF16).astype(F32)
        dpre = whole * slope[...]
        out[...] = dpre
        wide = wide + mm_tn(x[...], half)
        thin = thin + mm_tn(x[...], dstep)
        sums = exact(mm, oht[...], dpre, 2, False)
        for k in range(4):
            o = 3 - k if br == 0 else 3 + k
            block = sums[16 * o : 16 * o + 16]
            ids_sum = ids_sum + cw[k : k + 1] * block
            part = jnp.sum(normed * block, axis=0, keepdims=True)
            taps[k] = taps[k] + part
        bias_row = bias_row + jnp.sum(dpre, axis=0, keepdims=True)
    to_prev[...] = dpf[0:8]
    to_next[...] = dpr[ROWS - 8 : ROWS]
    shared = table[...] * gain[...] * ids_sum
    placed = jnp.concatenate(
        [jnp.zeros((88, 256), F32), shared, jnp.zeros((24, 256), F32)], axis=0
    )
    crossed = exact(mm_nt, jnp.ones((8, 256), BF16), placed, 3, False)[0:1]
    stacked = jnp.concatenate(
        [jnp.zeros((64, 256), F32), ids_sum] + taps + [bias_row, small[0:3], jnp.zeros((40, 256), F32)],
        axis=0,
    )
    last = jnp.concatenate([thin, jnp.zeros((256, 64), F32)], axis=1) + jnp.transpose(stacked)
    last = last + split_row(crossed, 256)
    send[:, 0:32, :] = wide[:, 0:128].astype(BF16).reshape(NEAR, 32, 128)
    send[:, 32:64, :] = wide[:, 128:256].astype(BF16).reshape(NEAR, 32, 128)
    send[:, 64:96, :] = last.astype(BF16).reshape(NEAR, 32, 128)


def ahead_kernel(dpf, from_next, cw, part, ahead):
    ahead[0:ROWS] = dpf[...]
    ahead[ROWS : ROWS + 8] = from_next[...]
    total = cw[0:1] * ahead[0:ROWS]
    for k in range(1, 4):
        total = total + cw[k : k + 1] * ahead[k : k + ROWS]
    part[...] = total


def normed_kernel(part, dpr, from_prev, cw, gain, table, oht, gn_ref, cross, behind):
    behind[0:8] = from_prev[...]
    behind[8 : ROWS + 8] = dpr[...]
    dn = part[...]
    for k in range(4):
        dn = dn + cw[k : k + 1] * behind[8 - k : 8 - k + ROWS]
    gn = dn.astype(BF16)
    gn_ref[...] = gn
    rated = exact(mm_tn, oht[48:64], table[...] * gain[...], 3, False)
    ones = jnp.ones((8, 256), BF16)
    cross[...] = exact(mm_nt, ones, gn.astype(F32) * rated, 3, False)[0:1]


def embedded_kernel(got, gn, gain, table, scale, oht, out):
    total = got[0]
    for k in range(1, GROUPS):
        total = total + got[k]
    cross = columns(jnp.broadcast_to(total[:, 0:256], (8, ROWS)))[:, 0:1]
    own = oht[48:64]
    unit = scale[:, 0:1]
    turned = exact(mm_tn, own, unit * gain[...], 3, False)
    shrunk = exact(mm_tn, own, table[...] * (unit * unit * unit / D), 3, False)
    out[...] = (turned * gn[...].astype(F32) - shrunk * cross).astype(BF16)


def near_kernel(got, send):
    total = got[0].astype(F32)
    for k in range(1, NEAR):
        total = total + got[k].astype(F32)
    last = total[64:96]
    lane = iota((32, 128), 1)
    crossed = jnp.where((lane >= 88) & (lane < 104), last, 0.0)
    last = last - crossed + split_row(jnp.sum(crossed, axis=0, keepdims=True), 32)
    total = jnp.concatenate([total[0:64], last], axis=0)
    send[...] = jnp.broadcast_to(total.astype(BF16)[None], (FAR, 96, 128))


def far_kernel(got, cross, send, payload):
    total = got[0].astype(F32)
    for k in range(1, FAR):
        total = total + got[k].astype(F32)
    send[...] = jnp.broadcast_to(total.astype(BF16)[None], (NEAR, 96, 128))
    lane = iota((1, 128), 1)
    both = total[64:65] + total[65:66]
    crossed = jnp.where((lane >= 88) & (lane < 104), both, 0.0)
    row = jnp.concatenate([cross[...], crossed], axis=1)
    payload[...] = jnp.broadcast_to(row[None], (GROUPS, 1, 384))


def finish_kernel(got, cross, table, scale, gain, gt, gg, gcw, gcb, gwb, gwc, gswt, gsb, glr, gsg):
    gwb[...] = got[:, 0:32, :].astype(F32).reshape(256, 128)
    gwc[...] = got[:, 32:64, :].astype(F32).reshape(256, 128)
    rows = jnp.transpose(got[:, 64:96, :].astype(F32).reshape(256, 128))
    gswt[...] = rows[0:64]
    sums = rows[64:80]
    here = cross[0]
    for k in range(1, GROUPS):
        here = here + cross[k]
    crossed = jnp.transpose(jnp.broadcast_to(here[:, 256:384], (128, 128)))[88:104, 0:1]
    unit = scale[:, 0:1]
    gt[...] = unit * gain[...] * sums - table[...] * (unit * unit * unit / D) * crossed
    gg[...] = jnp.sum(table[...] * unit * sums, axis=0, keepdims=True)
    gcw[...] = rows[80:84]
    gcb[...] = rows[84:85]
    lane = iota((8, 256), 1)
    tail = rows[80:88]
    picked = iota((8, 4), 1)
    result = jnp.zeros((8, 4), F32)
    for h in range(HEADS):
        part = jnp.sum(jnp.where(lane // 64 == h, tail, 0.0), axis=1, keepdims=True)
        result = jnp.where(picked == h, part, result)
    gsg[...] = result[5:6]
    gsb[...] = result[6:7]
    glr[...] = result[7:8]


def swap(value, axis):
    return lax.all_to_all(value, axis, 0, 0, tiled=True)


def shift(value, pairs):
    return lax.ppermute(value, CTX, pairs)


def mixer(
    token_ids,
    table,
    norm_gain,
    conv_weight,
    conv_bias,
    weight_b,
    weight_c,
    step_weight,
    step_bias,
    log_rate,
    skip_gain,
    out_grad,
):
    size = lax.axis_size(CTX)
    up = [(i, i + 1) for i in range(size - 1)]
    down = [(i + 1, i) for i in range(size - 1)]
    within = [(i, i ^ 1) for i in range(size)]
    across = [pair for i in range(1, size - 1, 2) for pair in ((i, i + 1), (i + 1, i))]
    edge = ((8, 256), F32)
    square = ((ROWS, 256), F32)
    half_square = ((ROWS, 256), BF16)
    squares, ids = call(
        squares_kernel,
        (((GROUPS, 1, 128), F32), ((1, ROWS), jnp.int32)),
        table, token_ids[None],
        near=False,
    )
    squares = swap(squares, "fsdp")
    ids_pair = shift(ids, within)
    ids_side = shift(ids, across)
    place = lax.axis_index(CTX).reshape(1, 1)
    table, gain, cw, cb, wb, wc, swt, swx, bias, rate, skip, dy = call(
        fetch_kernel,
        (
            ((16, 256), F32),
            ((1, 256), F32),
            ((4, 256), F32),
            ((1, 256), F32),
            ((256, 128), BF16),
            ((256, 128), BF16),
            ((64, 256), BF16),
            ((128, 256), BF16),
            ((8, 1), F32),
            ((8, 1), F32),
            ((1, 256), F32),
            half_square,
        ),
        table, norm_gain[None], conv_weight, conv_bias[None], weight_b, weight_c,
        jnp.transpose(step_weight), step_bias[None], log_rate[None], skip_gain[None], out_grad,
        near=False,
    )
    xf, xr, gf, gr, part, oht, scale = call(
        tokens_kernel,
        (
            half_square,
            half_square,
            square,
            square,
            ((GROUPS, 24, 512), BF16),
            ((128, 256), BF16),
            ((16, 128), F32),
        ),
        ids, ids_pair, ids_side, place, squares, table, gain, cw, cb, wb, wc, swx,
    )
    bc, raw = call(reduce_kernel, (((GROUPS, 16, 512), BF16), ((8, 256), F32)), swap(part, "fsdp"))
    bc = swap(bc, "fsdp").reshape(ROWS, 512)
    half_pair = ((2, ROWS, 256), BF16)
    cols, rows, weighted, turned, packed = call(
        steps_kernel,
        (((ROWS, 128), F32), ((48, ROWS), F32), half_pair, half_pair, edge),
        raw, bias, rate, xf, xr, dy,
    )
    (states,) = call(
        states_kernel, (((NEAR, 72, 256), BF16),), bc, weighted, turned, packed
    )
    arrived = swap(states, BESIDE)
    y0, dxf0, dxr0, dbc0, side, line = call(
        within_kernel,
        (square, square, square, ((ROWS, 512), BF16), edge, edge),
        bc, cols, rows, xf, xr, dy, skip,
    )
    (groups,) = call(group_kernel, (((FAR, 72, 256), BF16),), arrived)
    groups = swap(groups, "zh")
    (entering,) = call(chain_kernel, (((NEAR, 64, 256), BF16),), arrived, groups, place)
    entering = swap(entering, BESIDE)
    (dpart,) = call(
        partials_kernel, (((GROUPS, 16, 512), BF16),), entering, weighted, turned, dbc0
    )
    mixer_out, dxf, dxr, draw, small = call(
        carried_kernel,
        (half_square, square, square, ((8, 256), BF16), edge),
        entering, bc, cols, rows, xf, xr, dy, y0, dxf0, dxr0, side, line, rate,
        final=(0,),
    )
    (totals,) = call(total_kernel, (((GROUPS, 24, 512), BF16),), swap(dpart, "fsdp"), draw)
    dpf, dpr, to_prev, to_next, gsend = call(
        project_back_kernel,
        (square, square, edge, edge, ((NEAR, 96, 128), BF16)),
        swap(totals, "fsdp"), xf, xr, gf, gr, dxf, dxr, wb,
        wc, swt, oht, table, scale, gain, cw, small,
    )
    from_next = shift(to_prev, down)
    from_prev = shift(to_next, up)
    reduced = swap(gsend, BESIDE)
    (ahead,) = call(
        ahead_kernel, (square,), dpf, from_next, cw, scratch=[VMEM((ROWS + 8, 256), F32)]
    )
    gn, cross = call(
        normed_kernel,
        (half_square, ((1, 256), F32)),
        ahead, dpr, from_prev, cw, gain, table, oht,
        scratch=[VMEM((ROWS + 8, 256), F32)],
    )
    (summed,) = call(near_kernel, (((FAR, 96, 128), BF16),), reduced)
    summed = swap(summed, "zh")
    gathered, payload = call(
        far_kernel, (((NEAR, 96, 128), BF16), ((GROUPS, 1, 384), F32)), summed, cross
    )
    crossed = swap(payload, "fsdp")
    (grad_embedded,) = call(
        embedded_kernel, (half_square,), crossed, gn, gain, table, scale, oht, final=(0,)
    )
    outs = call(
        finish_kernel,
        (
            ((16, 256), F32),
            ((1, 256), F32),
            ((4, 256), F32),
            ((1, 256), F32),
            ((256, 128), F32),
            ((256, 128), F32),
            ((64, 256), F32),
            ((1, 4), F32),
            ((1, 4), F32),
            ((1, 4), F32),
        ),
        swap(gathered, BESIDE), crossed, table, scale, gain,
        final=range(10),
    )
    gt, gg, gcw, gcb, gwb, gwc, gswt, gsb, glr, gsg = outs
    return (
        mixer_out,
        grad_embedded,
        gt,
        gg[0],
        gcw,
        gcb[0],
        gwb,
        gwc,
        jnp.transpose(gswt),
        gsb[0],
        glr[0],
        gsg[0],
    )


def solution(mesh):
    devices = mesh.devices.reshape(mesh.shape["fsdp"], FAR, 4, 2)
    mesh = jax.sharding.Mesh(devices, ("fsdp",) + CTX)
    return jax.shard_map(
        mixer,
        mesh=mesh,
        in_specs=(
            P(CTX),
            P(None, "fsdp"),
            P("fsdp"),
            P(None, "fsdp"),
            P("fsdp"),
            P("fsdp", None),
            P("fsdp", None),
            P("fsdp", None),
            P("fsdp"),
            P("fsdp"),
            P("fsdp"),
            P(CTX, "fsdp"),
        ),
        out_specs=(
            P(CTX, "fsdp"),
            P(CTX, "fsdp"),
            P(None, "fsdp"),
            P("fsdp"),
            P(None, "fsdp"),
            P("fsdp"),
            P("fsdp", None),
            P("fsdp", None),
            P("fsdp", None),
            P("fsdp"),
            P("fsdp"),
            P("fsdp"),
        ),
        check_vma=False,
    )
```

```python
import jax
import jax.numpy as jnp
from jax import lax
from jax.sharding import PartitionSpec as P
from jax.experimental import pallas as pl
from jax.experimental.pallas import tpu as pltpu

D = 4096
ROWS = 256
HEADS = 4
STATE = 128
GROUPS = 16
NEAR = 8
FAR = 4
CTX = ("zh", "zl", "xh")
BESIDE = ("zl", "xh")
F32 = jnp.float32
BF16 = jnp.bfloat16
VMEM = pltpu.VMEM


def call(kernel, outs, *args, final=(), scratch=(), near=True):
    shapes = tuple(
        jax.ShapeDtypeStruct(shape, kind) if i in final else VMEM(shape, kind)
        for i, (shape, kind) in enumerate(outs)
    )
    space = VMEM if near else pltpu.HBM
    args = [pltpu.with_memory_space_constraint(arg, space) for arg in args]
    return pl.pallas_call(
        kernel,
        out_shape=shapes,
        scratch_shapes=scratch,
        compiler_params=pltpu.CompilerParams(vmem_limit_bytes=24 << 20),
    )(*args)


def iota(shape, dim):
    return lax.broadcasted_iota(jnp.int32, shape, dim)


def mm(left, right):
    return lax.dot_general(left, right, (((1,), (0,)), ((), ())), preferred_element_type=F32)


def mm_tn(left, right):
    return lax.dot_general(left, right, (((0,), (0,)), ((), ())), preferred_element_type=F32)


def mm_nt(left, right):
    return lax.dot_general(left, right, (((1,), (1,)), ((), ())), preferred_element_type=F32)


def pieces(value, count):
    parts = []
    rest = value
    for _ in range(count):
        part = rest.astype(BF16)
        parts.append(part)
        rest = rest - part.astype(F32)
    return parts


def exact(form, left, right, count, split_left):
    total = None
    for part in pieces(left if split_left else right, count):
        term = form(part, right) if split_left else form(left, part)
        total = term if total is None else total + term
    return total


def head_masks(rows):
    lane_head = iota((rows, 256), 1) // 64
    return [lane_head == h for h in range(HEADS)]


def by_head(values, masks):
    out = values[3]
    for h in range(3):
        out = jnp.where(masks[h], values[h], out)
    return out


def expand(cols, first, masks):
    wide = [jnp.broadcast_to(cols[:, first + h : first + h + 1], (ROWS, 256)) for h in range(HEADS)]
    return by_head(wide, masks)


def columns(rows):
    missing = 128 - rows.shape[0]
    return jnp.transpose(jnp.concatenate([rows, jnp.zeros((missing, ROWS), F32)], axis=0))


def inclusive_masks():
    before = iota((ROWS, ROWS), 0) <= iota((ROWS, ROWS), 1)
    after = iota((ROWS, ROWS), 0) >= iota((ROWS, ROWS), 1)
    return jnp.where(before, 1.0, 0.0).astype(BF16), jnp.where(after, 1.0, 0.0).astype(BF16)


def squares_kernel(table, ids, send, ids_v):
    ids_v[...] = ids[...]
    squares = jnp.concatenate([table[...] * table[...], jnp.zeros((112, 256), F32)], axis=0)
    sums = exact(mm_nt, jnp.ones((8, 256), BF16), squares, 3, False)
    send[...] = jnp.broadcast_to(sums[0:1][None], (GROUPS, 1, 128))


def fetch_kernel(
    table, gain, cw, cb, wb, wc, swt, step_bias, log_rate, skip_gain, dy,
    table_v, gain_v, cw_v, cb_v, wb_v, wc_v, swt_v, swx, bias, rate, skip, dy_v,
):
    table_v[...] = table[...]
    gain_v[...] = gain[...]
    cw_v[...] = cw[...]
    cb_v[...] = cb[...]
    wb_v[...] = wb[...]
    wc_v[...] = wc[...]
    swt_v[...] = swt[...]
    dy_v[...] = dy[...]
    place = iota((128, 64), 0)
    chosen = jnp.where(place // 8 * 4 + place % 4 == iota((128, 64), 1), 1.0, 0.0).astype(BF16)
    swx[...] = mm(chosen, swt[...]).astype(BF16)
    own = iota((8, HEADS), 0) % HEADS == iota((8, HEADS), 1)
    for source, column in ((step_bias, bias), (log_rate, rate)):
        column[...] = jnp.sum(jnp.where(own, source[...], 0.0), axis=1, keepdims=True)
    lane_head = iota((1, 256), 1) // 64
    row = jnp.zeros((1, 256), F32)
    for h in range(HEADS):
        row = jnp.where(lane_head == h, skip_gain[:, h : h + 1], row)
    skip[...] = row


def tokens_kernel(
    ids, ids_pair, ids_side, place, got, table, gain, cw, cb, wb, wc, swx,
    xf, xr, gf, gr, send, oht_ref, scale,
):
    total = got[0]
    for k in range(1, GROUPS):
        total = total + got[k]
    unit = lax.rsqrt(total / D + 1e-05)
    spread = jnp.transpose(jnp.broadcast_to(unit, (128, 128)))[0:16]
    scale[...] = spread
    unit = spread[:, 0:1]
    normed = (table[...] * unit * gain[...]).astype(BF16).astype(F32)
    vocab = iota((16, ROWS), 0)
    lane = iota((1, ROWS), 1)
    here = ids[...]
    even = place[...] % 2 == 0
    following = jnp.where(even, ids_pair[...], ids_side[...])
    following = jnp.where(place[...] == FAR * NEAR - 1, -1, following)
    preceding = jnp.where(even, ids_side[...], ids_pair[...])
    preceding = jnp.where(place[...] == 0, -1, preceding)
    hits = []
    for o in range(7):
        d = o - 3
        if d == 0:
            moved = here
        elif d > 0:
            ahead = pltpu.roll(following, ROWS - d, 1)
            moved = jnp.where(lane < ROWS - d, pltpu.roll(here, ROWS - d, 1), ahead)
        else:
            moved = jnp.where(lane >= -d, pltpu.roll(here, -d, 1), pltpu.roll(preceding, -d, 1))
        hits.append(jnp.where(moved == vocab, 1.0, 0.0))
    hits.append(jnp.zeros((16, ROWS), F32))
    oht = jnp.concatenate(hits, axis=0).astype(BF16)
    oht_ref[...] = oht
    none = jnp.zeros((16, 256), F32)
    taps = [cw[k : k + 1, :] * normed for k in range(4)]
    fwd_rows = jnp.concatenate([taps[3], taps[2], taps[1], taps[0], none, none, none, none], axis=0)
    rev_rows = jnp.concatenate([none, none, none, taps[0], taps[1], taps[2], taps[3], none], axis=0)
    halves = []
    for rows, x_ref, slope_ref in ((fwd_rows, xf, gf), (rev_rows, xr, gr)):
        pre = exact(mm_tn, oht, rows, 3, False) + cb[...]
        gate = 1.0 / (1.0 + jnp.exp(-pre))
        slope_ref[...] = (gate * (1.0 + pre * (1.0 - gate))).astype(BF16)
        half = (pre * gate).astype(BF16)
        x_ref[...] = half
        halves.append(half)
    for member, half in enumerate(halves):
        for side, weight in ((0, wb), (128, wc)):
            at = member * 256 + side
            part = mm(half, weight[...]).astype(BF16).reshape(GROUPS, 16, 128)
            send[:, 0:16, at : at + 128] = part
    own = iota((128, 256), 0) % 8 < 4
    steps = jnp.where(own, mm_nt(swx[...], halves[0]), mm_nt(swx[...], halves[1]))
    high, low = pieces(steps, 2)
    send[:, 16:24, 0:256] = high.reshape(GROUPS, 8, 256)
    send[:, 16:24, 256:512] = low.reshape(GROUPS, 8, 256)


def reduce_kernel(got, bc, raw):
    total = got[0].astype(F32)
    for k in range(1, GROUPS):
        total = total + got[k].astype(F32)
    half = total[0:16].astype(BF16)
    bc[...] = jnp.broadcast_to(half[None], (GROUPS, 16, 512))
    raw[...] = total[16:24, 0:256] + total[16:24, 256:512]


def steps_kernel(
    raw, bias, rate, xf, xr, dy,
    cols_ref, rows_ref, weighted_ref, turned_ref, packed_ref,
):
    shifted = raw[...] + bias[...]
    step = jnp.maximum(shifted, 0.0) + jnp.log1p(jnp.exp(-jnp.abs(shifted)))
    slope = 1.0 / (1.0 + jnp.exp(-shifted))
    logdec = -step * jnp.exp(rate[...])
    before, after = inclusive_masks()
    fwd_row = iota((8, ROWS), 0) < 4
    prefix = exact(mm, logdec, before, 3, True)
    suffix = exact(mm, logdec, after, 3, True)
    cumul = jnp.where(fwd_row, prefix, suffix)
    fwd_one = iota((8, 1), 0) < 4
    ending = jnp.where(fwd_one, prefix[:, ROWS - 1 : ROWS], suffix[:, 0:1])
    closing = jnp.exp(ending - cumul)
    weight = closing * step
    grown = jnp.exp(cumul)
    rows_ref[...] = jnp.concatenate([cumul, step, weight, closing, slope, logdec], axis=0)
    cols = columns(jnp.concatenate([cumul, step, weight, grown], axis=0))
    cols_ref[...] = cols
    masks = head_masks(ROWS)
    dyf = dy[...].astype(F32)
    for br, x in ((0, xf), (1, xr)):
        weight_wide = expand(cols, 16 + 4 * br, masks)
        grown_wide = expand(cols, 24 + 4 * br, masks)
        weighted_ref[br] = (weight_wide * x[...].astype(F32)).astype(BF16)
        turned_ref[br] = (grown_wide * dyf).astype(BF16)
    decay = jnp.exp(ending)
    lane_head = iota((1, 256), 1) // 64
    fwd_decay = jnp.zeros((1, 256), F32)
    rev_decay = jnp.zeros((1, 256), F32)
    for h in range(HEADS):
        fwd_decay = jnp.where(lane_head == h, decay[h : h + 1], fwd_decay)
        rev_decay = jnp.where(lane_head == h, decay[h + 4 : h + 5], rev_decay)
    packed_ref[...] = split_decays(fwd_decay, rev_decay)


def split_decays(fwd_decay, rev_decay):
    row = iota((8, 256), 0)
    f_high = fwd_decay.astype(BF16).astype(F32)
    r_high = rev_decay.astype(BF16).astype(F32)
    packed = jnp.where(row == 0, f_high, 0.0)
    packed = jnp.where(row == 1, fwd_decay - f_high, packed)
    packed = jnp.where(row == 2, r_high, packed)
    return jnp.where(row == 3, rev_decay - r_high, packed)


def join_decays(packed):
    rows = packed.astype(F32)
    return rows[0:1] + rows[1:2], rows[2:3] + rows[3:4]


def states_kernel(bc, weighted, turned, packed, send):
    found = []
    for br in range(2):
        b = bc[:, br * 256 : br * 256 + 128]
        c = bc[:, br * 256 + 128 : br * 256 + 256]
        found.append((mm_tn(b, weighted[br]), mm_tn(c, turned[br])))
    chains = (found[0][0], found[1][1], found[1][0], found[0][1])
    for ch, state in enumerate(chains):
        send[:, ch * 16 : ch * 16 + 16, :] = state.astype(BF16).reshape(NEAR, 16, 256)
    send[:, 64:72, :] = jnp.broadcast_to(packed[...].astype(BF16)[None], (NEAR, 8, 256))


def advance(state, decay_first, decay_second, piece):
    return decay_first * state[0] + piece[0:16], decay_second * state[1] + piece[16:32]


def group_kernel(got, place, send):
    here = place[...] // NEAR
    nothing = jnp.zeros((16, 256), F32)
    up = (nothing, nothing)
    down = (nothing, nothing)
    fwd_all = jnp.ones((1, 256), F32)
    rev_all = jnp.ones((1, 256), F32)
    for i in range(NEAR):
        fwd_decay, rev_decay = join_decays(got[i, 64:72, :])
        fwd_all = fwd_all * fwd_decay
        rev_all = rev_all * rev_decay
        up = advance(up, fwd_decay, rev_decay, got[i, 0:32, :].astype(F32))
        j = NEAR - 1 - i
        fwd_decay, rev_decay = join_decays(got[j, 64:72, :])
        down = advance(down, rev_decay, fwd_decay, got[j, 32:64, :].astype(F32))
    upward = jnp.concatenate(up, axis=0)
    downward = jnp.concatenate(down, axis=0)
    decays = split_decays(fwd_all, rev_all).astype(BF16)
    for g in range(FAR):
        send[g, 0:32, :] = jnp.where(here < g, upward, downward).astype(BF16)
        send[g, 32:40, :] = decays


def chain_kernel(got, far, place, out):
    here = place[...] // NEAR
    nothing = jnp.zeros((16, 256), F32)
    up = (nothing, nothing)
    down = (nothing, nothing)
    for g in range(FAR):
        fwd_decay, rev_decay = join_decays(far[g, 32:40, :])
        moved = advance(up, fwd_decay, rev_decay, far[g, 0:32, :].astype(F32))
        up = tuple(jnp.where(here > g, new, old) for new, old in zip(moved, up))
        k = FAR - 1 - g
        fwd_decay, rev_decay = join_decays(far[k, 32:40, :])
        moved = advance(down, rev_decay, fwd_decay, far[k, 0:32, :].astype(F32))
        down = tuple(jnp.where(here < k, new, old) for new, old in zip(moved, down))
    for i in range(NEAR):
        out[i, 0:16, :] = up[0].astype(BF16)
        out[i, 16:32, :] = up[1].astype(BF16)
        fwd_decay, rev_decay = join_decays(got[i, 64:72, :])
        up = advance(up, fwd_decay, rev_decay, got[i, 0:32, :].astype(F32))
        j = NEAR - 1 - i
        out[j, 32:48, :] = down[0].astype(BF16)
        out[j, 48:64, :] = down[1].astype(BF16)
        fwd_decay, rev_decay = join_decays(got[j, 64:72, :])
        down = advance(down, rev_decay, fwd_decay, got[j, 32:64, :].astype(F32))


def within_kernel(bc, cols_ref, rows_ref, xf, xr, dy, skip, y_ref, dxf, dxr, dbc, side, line):
    masks = head_masks(ROWS)
    t_at = iota((ROWS, ROWS), 0)
    s_at = iota((ROWS, ROWS), 1)
    lane = iota((ROWS, 128), 1)
    cols = cols_ref[...]
    dyh = dy[...]
    dyf = dyh.astype(F32)
    nothing = jnp.zeros((ROWS, 256), BF16)
    direct = skip[...] * dyf
    total = skip[...] * (xf[...].astype(F32) + xr[...].astype(F32))
    side_acc = jnp.zeros((ROWS, 128), F32)
    lines = []
    for br, x, dx_ref in ((0, xf, dxf), (1, xr, dxr)):
        xh = x[...]
        b = bc[:, br * 256 : br * 256 + 128]
        c = bc[:, br * 256 + 128 : br * 256 + 256]
        inner = mm_nt(c, b)
        causal = t_at >= s_at if br == 0 else t_at <= s_at
        dinner = jnp.zeros((ROWS, ROWS), F32)
        intra = []
        back = []
        for h in range(HEADS):
            at = 4 * br + h
            spread = cols[:, at : at + 1] - rows_ref[at : at + 1, :]
            decay = jnp.exp(jnp.where(causal, spread, -jnp.inf))
            step = rows_ref[8 + at : 9 + at, :]
            paced = decay * step
            mixing = (inner * paced).astype(BF16)
            intra.append(mm(mixing, xh))
            back.append(mm_tn(mixing, dyh))
            dmix = mm_nt(jnp.where(masks[h], dyh, nothing), xh)
            dinner = dinner + dmix * paced
            reach = dmix * decay * inner
            lines.append(jnp.sum(reach, axis=0, keepdims=True))
            flow = jnp.sum(reach * step, axis=1, keepdims=True)
            side_acc = jnp.where(lane == at, flow, side_acc)
        total = total + by_head(intra, masks)
        dx_ref[...] = direct + by_head(back, masks)
        dhalf = dinner.astype(BF16)
        dbc[:, br * 256 : br * 256 + 128] = mm_tn(dhalf, c).astype(BF16)
        dbc[:, br * 256 + 128 : br * 256 + 256] = mm(dhalf, b).astype(BF16)
    y_ref[...] = total
    side[...] = jnp.transpose(side_acc)[0:8]
    line[...] = jnp.concatenate(lines, axis=0)


def state(got, ch):
    return got[:, ch * 16 : ch * 16 + 16, :].reshape(STATE, 256)


def partials_kernel(got, weighted, turned, dbc0, send):
    for br, at_state, at_grad in ((0, 0, 3), (1, 2, 1)):
        dc = mm_nt(turned[br], state(got, at_state))
        db = mm_nt(weighted[br], state(got, at_grad))
        at = br * 256
        part = dbc0[:, at : at + 256].astype(F32) + jnp.concatenate([db, dc], axis=1)
        send[:, :, at : at + 256] = part.astype(BF16).reshape(16, 16, 256)


def carried_kernel(
    got, bc, cols_ref, rows_ref, xf, xr, dy, y0, dxf0, dxr0, side, line, rate,
    out, dxf, dxr, draw_ref, small,
):
    dyf = dy[...].astype(F32)

    masks = head_masks(ROWS)
    cols = cols_ref[...]

    row_at = iota((8, 256), 0)
    lane_head = iota((8, 256), 1) // 64
    total = y0[...]
    dp = jnp.zeros((8, ROWS), F32)
    dw = jnp.zeros((8, ROWS), F32)
    d_end = jnp.zeros((8, 1), F32)
    for br, x, dx0, dx_ref, at_state, at_grad in ((0, xf, dxf0, dxf, 0, 3), (1, xr, dxr0, dxr, 2, 1)):
        start_half = state(got, at_state)
        ahead_half = state(got, at_grad)
        b = bc[:, br * 256 : br * 256 + 128]
        c = bc[:, br * 256 + 128 : br * 256 + 256]
        heads = jnp.where(lane_head + 4 * br == row_at, 1.0, 0.0).astype(BF16)
        carried = expand(cols, 24 + 4 * br, masks) * mm(c, start_half)
        total = total + carried
        dp = dp + exact(mm_nt, heads, dyf * carried, 2, False)
        xv = x[...].astype(F32)
        toward = mm(b, ahead_half)
        dx_ref[...] = dx0[...] + expand(cols, 16 + 4 * br, masks) * toward
        dw = dw + exact(mm_nt, heads, xv * toward, 2, False)
        both = jnp.sum(start_half.astype(F32) * ahead_half.astype(F32), axis=0, keepdims=True)
        spread = jnp.where(lane_head + 4 * br == row_at, both, 0.0)
        d_end = d_end + jnp.sum(spread, axis=1, keepdims=True)
    out[...] = total.astype(BF16)
    cumul = rows_ref[0:8]
    step = rows_ref[8:16]
    weight = rows_ref[16:24]
    closing = rows_ref[24:32]
    slope = rows_ref[32:40]
    logdec = rows_ref[40:48]
    at = iota((8, ROWS), 1)
    row = iota((8, ROWS), 0)
    last = at == jnp.where(row < 4, ROWS - 1, 0)
    pull = dw * weight
    ending = jnp.sum(jnp.where(last, cumul, 0.0), axis=1, keepdims=True)
    d_end = jnp.exp(ending) * d_end + jnp.sum(pull, axis=1, keepdims=True)
    dcumul = side[...] - step * line[...] + dp - pull + jnp.where(last, d_end, 0.0)
    before, after = inclusive_masks()
    prefix = exact(mm, dcumul, before, 3, True)
    suffix = exact(mm, dcumul, after, 3, True)
    dlog = jnp.where(row < 4, suffix, prefix)
    dstep = line[...] + dw * closing - dlog * jnp.exp(rate[...])
    draw = dstep * slope
    draw_ref[...] = draw.astype(BF16)
    d_bias = jnp.sum(draw, axis=1, keepdims=True)
    d_rate = jnp.sum(dlog * logdec, axis=1, keepdims=True)
    first = iota((1, 256), 1)
    bias_row = jnp.zeros((1, 256), F32)
    rate_row = jnp.zeros((1, 256), F32)
    for h in range(HEADS):
        bias_row = jnp.where(first == 64 * h, d_bias[h : h + 1] + d_bias[h + 4 : h + 5], bias_row)
        rate_row = jnp.where(first == 64 * h, d_rate[h : h + 1] + d_rate[h + 4 : h + 5], rate_row)
    skip_row = jnp.sum(dyf * (xf[...].astype(F32) + xr[...].astype(F32)), axis=0, keepdims=True)
    none = jnp.zeros((5, 256), F32)
    small[...] = jnp.concatenate([skip_row, bias_row, rate_row, none], axis=0)


def total_kernel(got, draw, send):
    total = got[0].astype(F32)
    for k in range(1, GROUPS):
        total = total + got[k].astype(F32)
    half = total.astype(BF16)
    send[:, 0:16, :] = jnp.broadcast_to(half[None, :, 0:256], (GROUPS, 16, 256))
    send[:, 16:32, :] = jnp.broadcast_to(half[None, :, 256:512], (GROUPS, 16, 256))
    send[:, 32:40, :] = jnp.broadcast_to(draw[...][None], (GROUPS, 8, 256))


def split_row(value, rows):
    row = iota((rows, 128), 0) % 32
    high = value.astype(BF16).astype(F32)
    return jnp.where(row == 0, high, 0.0) + jnp.where(row == 1, value - high, 0.0)


def project_back_kernel(
    got, xf, xr, gf, gr, dxf, dxr, wb, wc, swt, oht, table, scale, gain, cw, small,
    place, dpf, dpr, to_pair, to_side, send,
):
    draw = got[:, 32:40, :].astype(F32).reshape(128, 256).astype(BF16)
    pick_row = iota((128, 64), 0)
    pick_col = iota((128, 64), 1)
    wanted = pick_row // 8 * 4 + pick_row % 4
    normed = (table[...] * scale[:, 0:1] * gain[...]).astype(BF16).astype(F32)
    taps = [jnp.zeros((1, 256), F32)] * 4
    bias_row = jnp.zeros((1, 256), F32)
    wide = jnp.zeros((256, 256), F32)
    thin = jnp.zeros((256, 64), F32)
    ids_sum = jnp.zeros((16, 256), F32)
    for br, x, slope, dx, out in ((0, xf, gf, dxf, dpf), (1, xr, gr, dxr, dpr)):
        mine = (wanted == pick_col) & ((pick_row % 8 < 4) == (br == 0))
        dstep = mm_tn(draw, jnp.where(mine, 1.0, 0.0).astype(BF16)).astype(BF16)
        half = got[:, br * 16 : br * 16 + 16, :].reshape(ROWS, 256)
        into = mm_nt(half[:, 0:128], wb[...]) + mm_nt(half[:, 128:256], wc[...])
        into = into + mm(dstep, swt[...])
        whole = (dx[...] + into).astype(BF16).astype(F32)
        dpre = whole * slope[...].astype(F32)
        out[...] = dpre
        wide = wide + mm_tn(x[...], half)
        thin = thin + mm_tn(x[...], dstep)
        sums = exact(mm, oht[...], dpre, 2, False)
        for k in range(4):
            o = 3 - k if br == 0 else 3 + k
            block = sums[16 * o : 16 * o + 16]
            ids_sum = ids_sum + cw[k : k + 1] * block
            part = jnp.sum(normed * block, axis=0, keepdims=True)
            taps[k] = taps[k] + part
        bias_row = bias_row + jnp.sum(dpre, axis=0, keepdims=True)
    even = place[...] % 2 == 0
    to_pair[...] = jnp.where(even, dpr[ROWS - 8 : ROWS], dpf[0:8])
    to_side[...] = jnp.where(even, dpf[0:8], dpr[ROWS - 8 : ROWS])
    shared = table[...] * gain[...] * ids_sum
    placed = jnp.concatenate(
        [jnp.zeros((88, 256), F32), shared, jnp.zeros((24, 256), F32)], axis=0
    )
    crossed = exact(mm_nt, jnp.ones((8, 256), BF16), placed, 3, False)[0:1]
    stacked = jnp.concatenate(
        [jnp.zeros((64, 256), F32), ids_sum] + taps + [bias_row, small[0:3], jnp.zeros((40, 256), F32)],
        axis=0,
    )
    last = jnp.concatenate([thin, jnp.zeros((256, 64), F32)], axis=1) + jnp.transpose(stacked)
    last = last + split_row(crossed, 256)
    send[:, 0:32, :] = wide[:, 0:128].astype(BF16).reshape(NEAR, 32, 128)
    send[:, 32:64, :] = wide[:, 128:256].astype(BF16).reshape(NEAR, 32, 128)
    send[:, 64:96, :] = last.astype(BF16).reshape(NEAR, 32, 128)


def catch_kernel(edge, caught):
    caught[...] = edge[...]


def normed_kernel(
    dpf, dpr, from_pair, from_side, place, cw, gain, table, oht,
    gn_ref, cross, ahead, behind,
):
    even = place[...] % 2 == 0
    ahead[0:ROWS] = dpf[...]
    ahead[ROWS : ROWS + 8] = jnp.where(even, from_pair[...], from_side[...])
    behind[0:8] = jnp.where(even, from_side[...], from_pair[...])
    behind[8 : ROWS + 8] = dpr[...]
    dn = jnp.zeros((ROWS, 256), F32)
    for k in range(4):
        dn = dn + cw[k : k + 1] * (ahead[k : k + ROWS] + behind[8 - k : 8 - k + ROWS])
    gn = dn.astype(BF16)
    gn_ref[...] = gn
    rated = exact(mm_tn, oht[48:64], table[...] * gain[...], 3, False)
    ones = jnp.ones((8, 256), BF16)
    cross[...] = exact(mm_nt, ones, gn.astype(F32) * rated, 3, False)[0:1]


def embedded_kernel(got, gn, gain, table, scale, oht, out):
    total = got[0]
    for k in range(1, GROUPS):
        total = total + got[k]
    cross = columns(jnp.broadcast_to(total[:, 0:256], (8, ROWS)))[:, 0:1]
    own = oht[48:64]
    unit = scale[:, 0:1]
    turned = exact(mm_tn, own, unit * gain[...], 3, False)
    shrunk = exact(mm_tn, own, table[...] * (unit * unit * unit / D), 3, False)
    out[...] = (turned * gn[...].astype(F32) - shrunk * cross).astype(BF16)


def near_kernel(got, send):
    total = got[0].astype(F32)
    for k in range(1, NEAR):
        total = total + got[k].astype(F32)
    last = total[64:96]
    lane = iota((32, 128), 1)
    crossed = jnp.where((lane >= 88) & (lane < 104), last, 0.0)
    last = last - crossed + split_row(jnp.sum(crossed, axis=0, keepdims=True), 32)
    total = jnp.concatenate([total[0:64], last], axis=0)
    send[...] = jnp.broadcast_to(total.astype(BF16)[None], (FAR, 96, 128))


def far_kernel(got, cross, send, payload):
    total = got[0].astype(F32)
    for k in range(1, FAR):
        total = total + got[k].astype(F32)
    send[...] = jnp.broadcast_to(total.astype(BF16)[None], (NEAR, 96, 128))
    lane = iota((1, 128), 1)
    both = total[64:65] + total[65:66]
    crossed = jnp.where((lane >= 88) & (lane < 104), both, 0.0)
    row = jnp.concatenate([cross[...], crossed], axis=1)
    payload[...] = jnp.broadcast_to(row[None], (GROUPS, 1, 384))


def finish_kernel(got, cross, table, scale, gain, gt, gg, gcw, gcb, gwb, gwc, gswt, gsb, glr, gsg):
    gwb[...] = got[:, 0:32, :].astype(F32).reshape(256, 128)
    gwc[...] = got[:, 32:64, :].astype(F32).reshape(256, 128)
    rows = jnp.transpose(got[:, 64:96, :].astype(F32).reshape(256, 128))
    gswt[...] = rows[0:64]
    sums = rows[64:80]
    here = cross[0]
    for k in range(1, GROUPS):
        here = here + cross[k]
    crossed = jnp.transpose(jnp.broadcast_to(here[:, 256:384], (128, 128)))[88:104, 0:1]
    unit = scale[:, 0:1]
    gt[...] = unit * gain[...] * sums - table[...] * (unit * unit * unit / D) * crossed
    gg[...] = jnp.sum(table[...] * unit * sums, axis=0, keepdims=True)
    gcw[...] = rows[80:84]
    gcb[...] = rows[84:85]
    lane = iota((8, 256), 1)
    tail = rows[80:88]
    picked = iota((8, 4), 1)
    result = jnp.zeros((8, 4), F32)
    for h in range(HEADS):
        part = jnp.sum(jnp.where(lane // 64 == h, tail, 0.0), axis=1, keepdims=True)
        result = jnp.where(picked == h, part, result)
    gsg[...] = result[5:6]
    gsb[...] = result[6:7]
    glr[...] = result[7:8]


def swap(value, axis):
    return lax.all_to_all(value, axis, 0, 0, tiled=True)


def shift(value, pairs):
    return lax.ppermute(value, CTX, pairs)


def mixer(
    token_ids,
    table,
    norm_gain,
    conv_weight,
    conv_bias,
    weight_b,
    weight_c,
    step_weight,
    step_bias,
    log_rate,
    skip_gain,
    out_grad,
):
    size = lax.axis_size(CTX)
    within = [(i, i ^ 1) for i in range(size)]
    across = [pair for i in range(1, size - 1, 2) for pair in ((i, i + 1), (i + 1, i))]
    edge = ((8, 256), F32)
    square = ((ROWS, 256), F32)
    half_square = ((ROWS, 256), BF16)
    squares, ids = call(
        squares_kernel,
        (((GROUPS, 1, 128), F32), ((1, ROWS), jnp.int32)),
        table, token_ids[None],
        near=False,
    )
    squares = swap(squares, "fsdp")
    ids_pair = shift(ids, within)
    ids_side = shift(ids, across)
    place = lax.axis_index(CTX).reshape(1, 1)
    table, gain, cw, cb, wb, wc, swt, swx, bias, rate, skip, dy = call(
        fetch_kernel,
        (
            ((16, 256), F32),
            ((1, 256), F32),
            ((4, 256), F32),
            ((1, 256), F32),
            ((256, 128), BF16),
            ((256, 128), BF16),
            ((64, 256), BF16),
            ((128, 256), BF16),
            ((8, 1), F32),
            ((8, 1), F32),
            ((1, 256), F32),
            half_square,
        ),
        table, norm_gain[None], conv_weight, conv_bias[None], weight_b, weight_c,
        jnp.transpose(step_weight), step_bias[None], log_rate[None], skip_gain[None], out_grad,
        near=False,
    )
    xf, xr, gf, gr, part, oht, scale = call(
        tokens_kernel,
        (
            half_square,
            half_square,
            half_square,
            half_square,
            ((GROUPS, 24, 512), BF16),
            ((128, 256), BF16),
            ((16, 128), F32),
        ),
        ids, ids_pair, ids_side, place, squares, table, gain, cw, cb, wb, wc, swx,
    )
    bc, raw = call(reduce_kernel, (((GROUPS, 16, 512), BF16), ((8, 256), F32)), swap(part, "fsdp"))
    bc = swap(bc, "fsdp").reshape(ROWS, 512)
    half_pair = ((2, ROWS, 256), BF16)
    cols, rows, weighted, turned, packed = call(
        steps_kernel,
        (((ROWS, 128), F32), ((48, ROWS), F32), half_pair, half_pair, edge),
        raw, bias, rate, xf, xr, dy,
    )
    (states,) = call(
        states_kernel, (((NEAR, 72, 256), BF16),), bc, weighted, turned, packed
    )
    arrived = swap(states, BESIDE)
    y0, dxf0, dxr0, dbc0, side, line = call(
        within_kernel,
        (square, square, square, ((ROWS, 512), BF16), edge, edge),
        bc, cols, rows, xf, xr, dy, skip,
    )
    (groups,) = call(group_kernel, (((FAR, 40, 256), BF16),), arrived, place)
    groups = swap(groups, "zh")
    (entering,) = call(chain_kernel, (((NEAR, 64, 256), BF16),), arrived, groups, place)
    entering = swap(entering, BESIDE)
    (dpart,) = call(
        partials_kernel, (((GROUPS, 16, 512), BF16),), entering, weighted, turned, dbc0
    )
    mixer_out, dxf, dxr, draw, small = call(
        carried_kernel,
        (half_square, square, square, ((8, 256), BF16), edge),
        entering, bc, cols, rows, xf, xr, dy, y0, dxf0, dxr0, side, line, rate,
        final=(0,),
    )
    (totals,) = call(total_kernel, (((GROUPS, 40, 256), BF16),), swap(dpart, "fsdp"), draw)
    dpf, dpr, to_pair, to_side, gsend = call(
        project_back_kernel,
        (square, square, edge, edge, ((NEAR, 96, 128), BF16)),
        swap(totals, "fsdp"), xf, xr, gf, gr, dxf, dxr, wb,
        wc, swt, oht, table, scale, gain, cw, small, place,
    )
    from_pair = shift(to_pair, within)
    from_side = shift(to_side, across)
    reduced = swap(gsend, BESIDE)
    (from_pair,) = call(catch_kernel, (edge,), from_pair)
    gn, cross = call(
        normed_kernel,
        (half_square, ((1, 256), F32)),
        dpf, dpr, from_pair, from_side, place, cw, gain, table, oht,
        scratch=[VMEM((ROWS + 8, 256), F32), VMEM((ROWS + 8, 256), F32)],
    )
    (summed,) = call(near_kernel, (((FAR, 96, 128), BF16),), reduced)
    summed = swap(summed, "zh")
    gathered, payload = call(
        far_kernel, (((NEAR, 96, 128), BF16), ((GROUPS, 1, 384), F32)), summed, cross
    )
    crossed = swap(payload, "fsdp")
    (grad_embedded,) = call(
        embedded_kernel, (half_square,), crossed, gn, gain, table, scale, oht, final=(0,)
    )
    outs = call(
        finish_kernel,
        (
            ((16, 256), F32),
            ((1, 256), F32),
            ((4, 256), F32),
            ((1, 256), F32),
            ((256, 128), F32),
            ((256, 128), F32),
            ((64, 256), F32),
            ((1, 4), F32),
            ((1, 4), F32),
            ((1, 4), F32),
        ),
        swap(gathered, BESIDE), crossed, table, scale, gain,
        final=range(10),
    )
    gt, gg, gcw, gcb, gwb, gwc, gswt, gsb, glr, gsg = outs
    return (
        mixer_out,
        grad_embedded,
        gt,
        gg[0],
        gcw,
        gcb[0],
        gwb,
        gwc,
        jnp.transpose(gswt),
        gsb[0],
        glr[0],
        gsg[0],
    )


def solution(mesh):
    devices = mesh.devices.reshape(mesh.shape["fsdp"], FAR, 4, 2)
    mesh = jax.sharding.Mesh(devices, ("fsdp",) + CTX)
    return jax.shard_map(
        mixer,
        mesh=mesh,
        in_specs=(
            P(CTX),
            P(None, "fsdp"),
            P("fsdp"),
            P(None, "fsdp"),
            P("fsdp"),
            P("fsdp", None),
            P("fsdp", None),
            P("fsdp", None),
            P("fsdp"),
            P("fsdp"),
            P("fsdp"),
            P(CTX, "fsdp"),
        ),
        out_specs=(
            P(CTX, "fsdp"),
            P(CTX, "fsdp"),
            P(None, "fsdp"),
            P("fsdp"),
            P(None, "fsdp"),
            P("fsdp"),
            P("fsdp", None),
            P("fsdp", None),
            P("fsdp", None),
            P("fsdp"),
            P("fsdp"),
            P("fsdp"),
        ),
        check_vma=False,
    )
```

```python
import jax
import jax.numpy as jnp
from jax import lax
from jax.sharding import PartitionSpec as P
from jax.experimental import pallas as pl
from jax.experimental.pallas import tpu as pltpu

D = 4096
ROWS = 256
HEADS = 4
STATE = 128
GROUPS = 16
NEAR = 8
FAR = 4
CTX = ("zh", "zl", "xh")
BESIDE = ("zl", "xh")
F32 = jnp.float32
BF16 = jnp.bfloat16
VMEM = pltpu.VMEM


def call(kernel, outs, *args, final=(), scratch=(), near=True):
    shapes = tuple(
        jax.ShapeDtypeStruct(shape, kind) if i in final else VMEM(shape, kind)
        for i, (shape, kind) in enumerate(outs)
    )
    space = VMEM if near else pltpu.HBM
    args = [pltpu.with_memory_space_constraint(arg, space) for arg in args]
    return pl.pallas_call(
        kernel,
        out_shape=shapes,
        scratch_shapes=scratch,
        compiler_params=pltpu.CompilerParams(vmem_limit_bytes=24 << 20),
    )(*args)


def iota(shape, dim):
    return lax.broadcasted_iota(jnp.int32, shape, dim)


def mm(left, right):
    return lax.dot_general(left, right, (((1,), (0,)), ((), ())), preferred_element_type=F32)


def mm_tn(left, right):
    return lax.dot_general(left, right, (((0,), (0,)), ((), ())), preferred_element_type=F32)


def mm_nt(left, right):
    return lax.dot_general(left, right, (((1,), (1,)), ((), ())), preferred_element_type=F32)


def pieces(value, count):
    parts = []
    rest = value
    for _ in range(count):
        part = rest.astype(BF16)
        parts.append(part)
        rest = rest - part.astype(F32)
    return parts


def exact(form, left, right, count, split_left):
    total = None
    for part in pieces(left if split_left else right, count):
        term = form(part, right) if split_left else form(left, part)
        total = term if total is None else total + term
    return total


def head_masks(rows):
    lane_head = iota((rows, 256), 1) // 64
    return [lane_head == h for h in range(HEADS)]


def by_head(values, masks):
    out = values[3]
    for h in range(3):
        out = jnp.where(masks[h], values[h], out)
    return out


def expand(cols, first, masks):
    wide = [jnp.broadcast_to(cols[:, first + h : first + h + 1], (ROWS, 256)) for h in range(HEADS)]
    return by_head(wide, masks)


def columns(rows):
    missing = 128 - rows.shape[0]
    return jnp.transpose(jnp.concatenate([rows, jnp.zeros((missing, ROWS), F32)], axis=0))


def inclusive_masks():
    before = iota((ROWS, ROWS), 0) <= iota((ROWS, ROWS), 1)
    after = iota((ROWS, ROWS), 0) >= iota((ROWS, ROWS), 1)
    return jnp.where(before, 1.0, 0.0).astype(BF16), jnp.where(after, 1.0, 0.0).astype(BF16)


def squares_kernel(table, ids, send, ids_v):
    ids_v[...] = ids[...]
    squares = jnp.concatenate([table[...] * table[...], jnp.zeros((112, 256), F32)], axis=0)
    sums = exact(mm_nt, jnp.ones((8, 256), BF16), squares, 3, False)
    send[...] = jnp.broadcast_to(sums[0:1][None], (GROUPS, 1, 128))


def fetch_kernel(
    table, gain, cw, cb, wb, wc, swt, step_bias, log_rate, skip_gain, dy,
    table_v, gain_v, cw_v, cb_v, wb_v, wc_v, swt_v, swx, bias, rate, skip, dy_v,
):
    table_v[...] = table[...]
    gain_v[...] = gain[...]
    cw_v[...] = cw[...]
    cb_v[...] = cb[...]
    wb_v[...] = wb[...]
    wc_v[...] = wc[...]
    swt_v[...] = swt[...]
    dy_v[...] = dy[...]
    place = iota((128, 64), 0)
    chosen = jnp.where(place // 8 * 4 + place % 4 == iota((128, 64), 1), 1.0, 0.0).astype(BF16)
    swx[...] = mm(chosen, swt[...]).astype(BF16)
    own = iota((8, HEADS), 0) % HEADS == iota((8, HEADS), 1)
    for source, column in ((step_bias, bias), (log_rate, rate)):
        column[...] = jnp.sum(jnp.where(own, source[...], 0.0), axis=1, keepdims=True)
    lane_head = iota((1, 256), 1) // 64
    row = jnp.zeros((1, 256), F32)
    for h in range(HEADS):
        row = jnp.where(lane_head == h, skip_gain[:, h : h + 1], row)
    skip[...] = row


def tokens_kernel(
    ids, ids_pair, ids_side, place, got, table, gain, cw, cb, wb, wc, swx,
    xf, xr, gf, gr, send, oht_ref, scale,
):
    total = got[0]
    for k in range(1, GROUPS):
        total = total + got[k]
    unit = lax.rsqrt(total / D + 1e-05)
    spread = jnp.transpose(jnp.broadcast_to(unit, (128, 128)))[0:16]
    scale[...] = spread
    unit = spread[:, 0:1]
    normed = (table[...] * unit * gain[...]).astype(BF16).astype(F32)
    vocab = iota((16, ROWS), 0)
    lane = iota((1, ROWS), 1)
    here = ids[...]
    even = place[...] % 2 == 0
    following = jnp.where(even, ids_pair[...], ids_side[...])
    following = jnp.where(place[...] == FAR * NEAR - 1, -1, following)
    preceding = jnp.where(even, ids_side[...], ids_pair[...])
    preceding = jnp.where(place[...] == 0, -1, preceding)
    hits = []
    for o in range(7):
        d = o - 3
        if d == 0:
            moved = here
        elif d > 0:
            ahead = pltpu.roll(following, ROWS - d, 1)
            moved = jnp.where(lane < ROWS - d, pltpu.roll(here, ROWS - d, 1), ahead)
        else:
            moved = jnp.where(lane >= -d, pltpu.roll(here, -d, 1), pltpu.roll(preceding, -d, 1))
        hits.append(jnp.where(moved == vocab, 1.0, 0.0))
    hits.append(jnp.zeros((16, ROWS), F32))
    oht = jnp.concatenate(hits, axis=0).astype(BF16)
    oht_ref[...] = oht
    none = jnp.zeros((16, 256), F32)
    taps = [cw[k : k + 1, :] * normed for k in range(4)]
    fwd_rows = jnp.concatenate([taps[3], taps[2], taps[1], taps[0], none, none, none, none], axis=0)
    rev_rows = jnp.concatenate([none, none, none, taps[0], taps[1], taps[2], taps[3], none], axis=0)
    halves = []
    for rows, x_ref, slope_ref in ((fwd_rows, xf, gf), (rev_rows, xr, gr)):
        pre = exact(mm_tn, oht, rows, 3, False) + cb[...]
        gate = 1.0 / (1.0 + jnp.exp(-pre))
        slope_ref[...] = (gate * (1.0 + pre * (1.0 - gate))).astype(BF16)
        half = (pre * gate).astype(BF16)
        x_ref[...] = half
        halves.append(half)
    for member, half in enumerate(halves):
        for side, weight in ((0, wb), (128, wc)):
            at = member * 256 + side
            part = mm(half, weight[...]).astype(BF16).reshape(GROUPS, 16, 128)
            send[:, 0:16, at : at + 128] = part
    own = iota((128, 256), 0) % 8 < 4
    steps = jnp.where(own, mm_nt(swx[...], halves[0]), mm_nt(swx[...], halves[1]))
    high, low = pieces(steps, 2)
    send[:, 16:24, 0:256] = high.reshape(GROUPS, 8, 256)
    send[:, 16:24, 256:512] = low.reshape(GROUPS, 8, 256)


def reduce_kernel(got, bc, raw):
    total = got[0].astype(F32)
    for k in range(1, GROUPS):
        total = total + got[k].astype(F32)
    half = total[0:16].astype(BF16)
    bc[...] = jnp.broadcast_to(half[None], (GROUPS, 16, 512))
    raw[...] = total[16:24, 0:256] + total[16:24, 256:512]


def steps_kernel(
    raw, bias, rate, xf, xr, dy,
    cols_ref, rows_ref, weighted_ref, turned_ref, packed_ref,
):
    shifted = raw[...] + bias[...]
    step = jnp.maximum(shifted, 0.0) + jnp.log1p(jnp.exp(-jnp.abs(shifted)))
    slope = 1.0 / (1.0 + jnp.exp(-shifted))
    logdec = -step * jnp.exp(rate[...])
    before, after = inclusive_masks()
    fwd_row = iota((8, ROWS), 0) < 4
    prefix = exact(mm, logdec, before, 3, True)
    suffix = exact(mm, logdec, after, 3, True)
    cumul = jnp.where(fwd_row, prefix, suffix)
    fwd_one = iota((8, 1), 0) < 4
    ending = jnp.where(fwd_one, prefix[:, ROWS - 1 : ROWS], suffix[:, 0:1])
    closing = jnp.exp(ending - cumul)
    weight = closing * step
    grown = jnp.exp(cumul)
    rows_ref[...] = jnp.concatenate([cumul, step, weight, closing, slope, logdec], axis=0)
    cols = columns(jnp.concatenate([cumul, step, weight, grown], axis=0))
    cols_ref[...] = cols
    masks = head_masks(ROWS)
    dyf = dy[...].astype(F32)
    for br, x in ((0, xf), (1, xr)):
        weight_wide = expand(cols, 16 + 4 * br, masks)
        grown_wide = expand(cols, 24 + 4 * br, masks)
        weighted_ref[br] = (weight_wide * x[...].astype(F32)).astype(BF16)
        turned_ref[br] = (grown_wide * dyf).astype(BF16)
    decay = jnp.exp(ending)
    lane_head = iota((1, 256), 1) // 64
    fwd_decay = jnp.zeros((1, 256), F32)
    rev_decay = jnp.zeros((1, 256), F32)
    for h in range(HEADS):
        fwd_decay = jnp.where(lane_head == h, decay[h : h + 1], fwd_decay)
        rev_decay = jnp.where(lane_head == h, decay[h + 4 : h + 5], rev_decay)
    packed_ref[...] = split_decays(fwd_decay, rev_decay)


def split_decays(fwd_decay, rev_decay):
    row = iota((8, 256), 0)
    f_high = fwd_decay.astype(BF16).astype(F32)
    r_high = rev_decay.astype(BF16).astype(F32)
    packed = jnp.where(row == 0, f_high, 0.0)
    packed = jnp.where(row == 1, fwd_decay - f_high, packed)
    packed = jnp.where(row == 2, r_high, packed)
    return jnp.where(row == 3, rev_decay - r_high, packed)


def join_decays(packed):
    rows = packed.astype(F32)
    return rows[0:1] + rows[1:2], rows[2:3] + rows[3:4]


def states_kernel(bc, weighted, turned, packed, send):
    found = []
    for br in range(2):
        b = bc[:, br * 256 : br * 256 + 128]
        c = bc[:, br * 256 + 128 : br * 256 + 256]
        found.append((mm_tn(b, weighted[br]), mm_tn(c, turned[br])))
    chains = (found[0][0], found[1][1], found[1][0], found[0][1])
    for ch, state in enumerate(chains):
        send[:, ch * 16 : ch * 16 + 16, :] = state.astype(BF16).reshape(NEAR, 16, 256)
    send[:, 64:72, :] = jnp.broadcast_to(packed[...].astype(BF16)[None], (NEAR, 8, 256))


def advance(state, decay_first, decay_second, piece):
    return decay_first * state[0] + piece[0:16], decay_second * state[1] + piece[16:32]


def group_kernel(got, place, send):
    here = place[...] // NEAR
    nothing = jnp.zeros((16, 256), F32)
    up = (nothing, nothing)
    down = (nothing, nothing)
    fwd_all = jnp.ones((1, 256), F32)
    rev_all = jnp.ones((1, 256), F32)
    for i in range(NEAR):
        fwd_decay, rev_decay = join_decays(got[i, 64:72, :])
        fwd_all = fwd_all * fwd_decay
        rev_all = rev_all * rev_decay
        up = advance(up, fwd_decay, rev_decay, got[i, 0:32, :].astype(F32))
        j = NEAR - 1 - i
        fwd_decay, rev_decay = join_decays(got[j, 64:72, :])
        down = advance(down, rev_decay, fwd_decay, got[j, 32:64, :].astype(F32))
    upward = jnp.concatenate(up, axis=0)
    downward = jnp.concatenate(down, axis=0)
    decays = split_decays(fwd_all, rev_all).astype(BF16)
    for g in range(FAR):
        send[g, 0:32, :] = jnp.where(here < g, upward, downward).astype(BF16)
        send[g, 32:40, :] = decays


def chain_kernel(got, far, place, out):
    here = place[...] // NEAR
    nothing = jnp.zeros((16, 256), F32)
    up = (nothing, nothing)
    down = (nothing, nothing)
    for g in range(FAR):
        fwd_decay, rev_decay = join_decays(far[g, 32:40, :])
        moved = advance(up, fwd_decay, rev_decay, far[g, 0:32, :].astype(F32))
        up = tuple(jnp.where(here > g, new, old) for new, old in zip(moved, up))
        k = FAR - 1 - g
        fwd_decay, rev_decay = join_decays(far[k, 32:40, :])
        moved = advance(down, rev_decay, fwd_decay, far[k, 0:32, :].astype(F32))
        down = tuple(jnp.where(here < k, new, old) for new, old in zip(moved, down))
    for i in range(NEAR):
        out[i, 0:16, :] = up[0].astype(BF16)
        out[i, 16:32, :] = up[1].astype(BF16)
        fwd_decay, rev_decay = join_decays(got[i, 64:72, :])
        up = advance(up, fwd_decay, rev_decay, got[i, 0:32, :].astype(F32))
        j = NEAR - 1 - i
        out[j, 32:48, :] = down[0].astype(BF16)
        out[j, 48:64, :] = down[1].astype(BF16)
        fwd_decay, rev_decay = join_decays(got[j, 64:72, :])
        down = advance(down, rev_decay, fwd_decay, got[j, 32:64, :].astype(F32))


def within_kernel(bc, cols_ref, rows_ref, xf, xr, dy, skip, y_ref, dxf, dxr, dbc, side, line):
    masks = head_masks(ROWS)
    t_at = iota((ROWS, ROWS), 0)
    s_at = iota((ROWS, ROWS), 1)
    lane = iota((ROWS, 128), 1)
    cols = cols_ref[...]
    dyh = dy[...]
    dyf = dyh.astype(F32)
    nothing = jnp.zeros((ROWS, 256), BF16)
    direct = skip[...] * dyf
    total = skip[...] * (xf[...].astype(F32) + xr[...].astype(F32))
    side_acc = jnp.zeros((ROWS, 128), F32)
    lines = []
    for br, x, dx_ref in ((0, xf, dxf), (1, xr, dxr)):
        xh = x[...]
        b = bc[:, br * 256 : br * 256 + 128]
        c = bc[:, br * 256 + 128 : br * 256 + 256]
        inner = mm_nt(c, b)
        causal = t_at >= s_at if br == 0 else t_at <= s_at
        dinner = jnp.zeros((ROWS, ROWS), F32)
        intra = []
        back = []
        for h in range(HEADS):
            at = 4 * br + h
            spread = cols[:, at : at + 1] - rows_ref[at : at + 1, :]
            decay = jnp.exp(jnp.where(causal, spread, -jnp.inf))
            step = rows_ref[8 + at : 9 + at, :]
            paced = decay * step
            mixing = (inner * paced).astype(BF16)
            intra.append(mm(mixing, xh))
            back.append(mm_tn(mixing, dyh))
            dmix = mm_nt(jnp.where(masks[h], dyh, nothing), xh)
            dinner = dinner + dmix * paced
            reach = dmix * decay * inner
            lines.append(jnp.sum(reach, axis=0, keepdims=True))
            flow = jnp.sum(reach * step, axis=1, keepdims=True)
            side_acc = jnp.where(lane == at, flow, side_acc)
        total = total + by_head(intra, masks)
        dx_ref[...] = direct + by_head(back, masks)
        dhalf = dinner.astype(BF16)
        dbc[:, br * 256 : br * 256 + 128] = mm_tn(dhalf, c).astype(BF16)
        dbc[:, br * 256 + 128 : br * 256 + 256] = mm(dhalf, b).astype(BF16)
    y_ref[...] = total
    side[...] = jnp.transpose(side_acc)[0:8]
    line[...] = jnp.concatenate(lines, axis=0)


def state(got, ch):
    return got[:, ch * 16 : ch * 16 + 16, :].reshape(STATE, 256)


def partials_kernel(got, weighted, turned, dbc0, send):
    for br, at_state, at_grad in ((0, 0, 3), (1, 2, 1)):
        dc = mm_nt(turned[br], state(got, at_state))
        db = mm_nt(weighted[br], state(got, at_grad))
        at = br * 256
        part = dbc0[:, at : at + 256].astype(F32) + jnp.concatenate([db, dc], axis=1)
        send[:, :, at : at + 256] = part.astype(BF16).reshape(16, 16, 256)


def carried_kernel(
    got, bc, cols_ref, rows_ref, xf, xr, dy, y0, dxf0, dxr0, side, line, rate,
    out, dxf, dxr, draw_ref, small,
):
    dyf = dy[...].astype(F32)

    masks = head_masks(ROWS)
    cols = cols_ref[...]

    row_at = iota((8, 256), 0)
    lane_head = iota((8, 256), 1) // 64
    total = y0[...]
    dp = jnp.zeros((8, ROWS), F32)
    dw = jnp.zeros((8, ROWS), F32)
    d_end = jnp.zeros((8, 1), F32)
    for br, x, dx0, dx_ref, at_state, at_grad in ((0, xf, dxf0, dxf, 0, 3), (1, xr, dxr0, dxr, 2, 1)):
        start_half = state(got, at_state)
        ahead_half = state(got, at_grad)
        b = bc[:, br * 256 : br * 256 + 128]
        c = bc[:, br * 256 + 128 : br * 256 + 256]
        heads = jnp.where(lane_head + 4 * br == row_at, 1.0, 0.0).astype(BF16)
        carried = expand(cols, 24 + 4 * br, masks) * mm(c, start_half)
        total = total + carried
        dp = dp + exact(mm_nt, heads, dyf * carried, 2, False)
        xv = x[...].astype(F32)
        toward = mm(b, ahead_half)
        dx_ref[...] = dx0[...] + expand(cols, 16 + 4 * br, masks) * toward
        dw = dw + exact(mm_nt, heads, xv * toward, 2, False)
        both = jnp.sum(start_half.astype(F32) * ahead_half.astype(F32), axis=0, keepdims=True)
        spread = jnp.where(lane_head + 4 * br == row_at, both, 0.0)
        d_end = d_end + jnp.sum(spread, axis=1, keepdims=True)
    out[...] = total.astype(BF16)
    cumul = rows_ref[0:8]
    step = rows_ref[8:16]
    weight = rows_ref[16:24]
    closing = rows_ref[24:32]
    slope = rows_ref[32:40]
    logdec = rows_ref[40:48]
    at = iota((8, ROWS), 1)
    row = iota((8, ROWS), 0)
    last = at == jnp.where(row < 4, ROWS - 1, 0)
    pull = dw * weight
    ending = jnp.sum(jnp.where(last, cumul, 0.0), axis=1, keepdims=True)
    d_end = jnp.exp(ending) * d_end + jnp.sum(pull, axis=1, keepdims=True)
    dcumul = side[...] - step * line[...] + dp - pull + jnp.where(last, d_end, 0.0)
    before, after = inclusive_masks()
    prefix = exact(mm, dcumul, before, 3, True)
    suffix = exact(mm, dcumul, after, 3, True)
    dlog = jnp.where(row < 4, suffix, prefix)
    dstep = line[...] + dw * closing - dlog * jnp.exp(rate[...])
    draw = dstep * slope
    draw_ref[...] = draw.astype(BF16)
    d_bias = jnp.sum(draw, axis=1, keepdims=True)
    d_rate = jnp.sum(dlog * logdec, axis=1, keepdims=True)
    first = iota((1, 256), 1)
    bias_row = jnp.zeros((1, 256), F32)
    rate_row = jnp.zeros((1, 256), F32)
    for h in range(HEADS):
        bias_row = jnp.where(first == 64 * h, d_bias[h : h + 1] + d_bias[h + 4 : h + 5], bias_row)
        rate_row = jnp.where(first == 64 * h, d_rate[h : h + 1] + d_rate[h + 4 : h + 5], rate_row)
    skip_row = jnp.sum(dyf * (xf[...].astype(F32) + xr[...].astype(F32)), axis=0, keepdims=True)
    none = jnp.zeros((5, 256), F32)
    small[...] = jnp.concatenate([skip_row, bias_row, rate_row, none], axis=0)


def total_kernel(got, draw, send):
    total = got[0].astype(F32)
    for k in range(1, GROUPS):
        total = total + got[k].astype(F32)
    half = total.astype(BF16)
    send[:, 0:16, :] = jnp.broadcast_to(half[None, :, 0:256], (GROUPS, 16, 256))
    send[:, 16:32, :] = jnp.broadcast_to(half[None, :, 256:512], (GROUPS, 16, 256))
    send[:, 32:40, :] = jnp.broadcast_to(draw[...][None], (GROUPS, 8, 256))


def split_row(value, rows):
    row = iota((rows, 128), 0) % 32
    high = value.astype(BF16).astype(F32)
    return jnp.where(row == 0, high, 0.0) + jnp.where(row == 1, value - high, 0.0)


def pack_edge(rows):
    return jnp.concatenate([rows[:, 0:128], rows[:, 128:256], jnp.zeros((2, 128), F32)], axis=0)


def open_edge(packed):
    return jnp.concatenate([packed[0:3], packed[3:6]], axis=1)


def picked(edges, at, count):
    total = jnp.zeros((8, 128), F32)
    for k in range(count):
        total = jnp.where(at == k, edges[k, 96:104, :].astype(F32), total)
    return total


def project_back_kernel(
    got, xf, xr, gf, gr, dxf, dxr, wb, wc, swt, oht, table, scale, gain, cw, small,
    place, dpf, dpr, send,
):
    draw = got[:, 32:40, :].astype(F32).reshape(128, 256).astype(BF16)
    pick_row = iota((128, 64), 0)
    pick_col = iota((128, 64), 1)
    wanted = pick_row // 8 * 4 + pick_row % 4
    normed = (table[...] * scale[:, 0:1] * gain[...]).astype(BF16).astype(F32)
    taps = [jnp.zeros((1, 256), F32)] * 4
    bias_row = jnp.zeros((1, 256), F32)
    wide = jnp.zeros((256, 256), F32)
    thin = jnp.zeros((256, 64), F32)
    ids_sum = jnp.zeros((16, 256), F32)
    for br, x, slope, dx, out in ((0, xf, gf, dxf, dpf), (1, xr, gr, dxr, dpr)):
        mine = (wanted == pick_col) & ((pick_row % 8 < 4) == (br == 0))
        dstep = mm_tn(draw, jnp.where(mine, 1.0, 0.0).astype(BF16)).astype(BF16)
        half = got[:, br * 16 : br * 16 + 16, :].reshape(ROWS, 256)
        into = mm_nt(half[:, 0:128], wb[...]) + mm_nt(half[:, 128:256], wc[...])
        into = into + mm(dstep, swt[...])
        whole = (dx[...] + into).astype(BF16).astype(F32)
        dpre = whole * slope[...].astype(F32)
        out[...] = dpre
        wide = wide + mm_tn(x[...], half)
        thin = thin + mm_tn(x[...], dstep)
        sums = exact(mm, oht[...], dpre, 2, False)
        for k in range(4):
            o = 3 - k if br == 0 else 3 + k
            block = sums[16 * o : 16 * o + 16]
            ids_sum = ids_sum + cw[k : k + 1] * block
            part = jnp.sum(normed * block, axis=0, keepdims=True)
            taps[k] = taps[k] + part
        bias_row = bias_row + jnp.sum(dpre, axis=0, keepdims=True)
    ahead_edge = pack_edge(dpr[ROWS - 3 : ROWS]).astype(BF16)
    behind_edge = pack_edge(dpf[0:3]).astype(BF16)
    onward = (place[...] + 1) % NEAR
    for k in range(NEAR):
        send[k, 96:104, :] = jnp.where(onward == k, ahead_edge, behind_edge)
    shared = table[...] * gain[...] * ids_sum
    placed = jnp.concatenate(
        [jnp.zeros((88, 256), F32), shared, jnp.zeros((24, 256), F32)], axis=0
    )
    crossed = exact(mm_nt, jnp.ones((8, 256), BF16), placed, 3, False)[0:1]
    stacked = jnp.concatenate(
        [jnp.zeros((64, 256), F32), ids_sum] + taps + [bias_row, small[0:3], jnp.zeros((40, 256), F32)],
        axis=0,
    )
    last = jnp.concatenate([thin, jnp.zeros((256, 64), F32)], axis=1) + jnp.transpose(stacked)
    last = last + split_row(crossed, 256)
    send[:, 0:32, :] = wide[:, 0:128].astype(BF16).reshape(NEAR, 32, 128)
    send[:, 32:64, :] = wide[:, 128:256].astype(BF16).reshape(NEAR, 32, 128)
    send[:, 64:96, :] = last.astype(BF16).reshape(NEAR, 32, 128)


def normed_kernel(
    dpf, dpr, far, near_prev, near_next, place, cw, gain, table, oht,
    gn_ref, payload, ahead, behind,
):
    here = place[...] % NEAR
    group = place[...] // NEAR
    prev = jnp.where(here == 0, picked(far, group - 1, FAR), near_prev[...])
    following = jnp.where(here == NEAR - 1, picked(far, group + 1, FAR), near_next[...])
    ahead[0:ROWS] = dpf[...]
    ahead[ROWS : ROWS + 8] = jnp.concatenate([open_edge(following), jnp.zeros((5, 256), F32)], axis=0)
    behind[0:8] = jnp.concatenate([jnp.zeros((5, 256), F32), open_edge(prev)], axis=0)
    behind[8 : ROWS + 8] = dpr[...]
    dn = jnp.zeros((ROWS, 256), F32)
    for k in range(4):
        dn = dn + cw[k : k + 1] * (ahead[k : k + ROWS] + behind[8 - k : 8 - k + ROWS])
    gn = dn.astype(BF16)
    gn_ref[...] = gn
    rated = exact(mm_tn, oht[48:64], table[...] * gain[...], 3, False)
    ones = jnp.ones((8, 256), BF16)
    row = exact(mm_nt, ones, gn.astype(F32) * rated, 3, False)[0:1]
    both = jnp.zeros((1, 128), F32)
    for k in range(FAR):
        both = both + far[k, 64:65, :].astype(F32) + far[k, 65:66, :].astype(F32)
    lane = iota((1, 128), 1)
    crossed = jnp.where((lane >= 88) & (lane < 104), both, 0.0)
    row = jnp.concatenate([row, crossed], axis=1)
    payload[...] = jnp.broadcast_to(row[None], (GROUPS, 1, 384))


def embedded_kernel(got, gn, gain, table, scale, oht, out):
    total = got[0]
    for k in range(1, GROUPS):
        total = total + got[k]
    cross = columns(jnp.broadcast_to(total[:, 0:256], (8, ROWS)))[:, 0:1]
    own = oht[48:64]
    unit = scale[:, 0:1]
    turned = exact(mm_tn, own, unit * gain[...], 3, False)
    shrunk = exact(mm_tn, own, table[...] * (unit * unit * unit / D), 3, False)
    out[...] = (turned * gn[...].astype(F32) - shrunk * cross).astype(BF16)


def near_kernel(got, place, send, near_prev, near_next):
    total = got[0, 0:96, :].astype(F32)
    for k in range(1, NEAR):
        total = total + got[k, 0:96, :].astype(F32)
    last = total[64:96]
    lane = iota((32, 128), 1)
    crossed = jnp.where((lane >= 88) & (lane < 104), last, 0.0)
    last = last - crossed + split_row(jnp.sum(crossed, axis=0, keepdims=True), 32)
    here = place[...] % NEAR
    prev = picked(got, (here + NEAR - 1) % NEAR, NEAR)
    following = picked(got, (here + 1) % NEAR, NEAR)
    near_prev[...] = prev
    near_next[...] = following
    forward = jnp.where(here == 0, prev, following)
    total = jnp.concatenate([total[0:64], last, forward], axis=0)
    send[...] = jnp.broadcast_to(total.astype(BF16)[None], (FAR, 104, 128))


def far_kernel(got, send):
    total = got[0, 0:96, :].astype(F32)
    for k in range(1, FAR):
        total = total + got[k, 0:96, :].astype(F32)
    send[...] = jnp.broadcast_to(total.astype(BF16)[None], (NEAR, 96, 128))


def finish_kernel(got, cross, table, scale, gain, gt, gg, gcw, gcb, gwb, gwc, gswt, gsb, glr, gsg):
    gwb[...] = got[:, 0:32, :].astype(F32).reshape(256, 128)
    gwc[...] = got[:, 32:64, :].astype(F32).reshape(256, 128)
    rows = jnp.transpose(got[:, 64:96, :].astype(F32).reshape(256, 128))
    gswt[...] = rows[0:64]
    sums = rows[64:80]
    here = cross[0]
    for k in range(1, GROUPS):
        here = here + cross[k]
    crossed = jnp.transpose(jnp.broadcast_to(here[:, 256:384], (128, 128)))[88:104, 0:1]
    unit = scale[:, 0:1]
    gt[...] = unit * gain[...] * sums - table[...] * (unit * unit * unit / D) * crossed
    gg[...] = jnp.sum(table[...] * unit * sums, axis=0, keepdims=True)
    gcw[...] = rows[80:84]
    gcb[...] = rows[84:85]
    lane = iota((8, 256), 1)
    tail = rows[80:88]
    picked = iota((8, 4), 1)
    result = jnp.zeros((8, 4), F32)
    for h in range(HEADS):
        part = jnp.sum(jnp.where(lane // 64 == h, tail, 0.0), axis=1, keepdims=True)
        result = jnp.where(picked == h, part, result)
    gsg[...] = result[5:6]
    gsb[...] = result[6:7]
    glr[...] = result[7:8]


def swap(value, axis):
    return lax.all_to_all(value, axis, 0, 0, tiled=True)


def shift(value, pairs):
    return lax.ppermute(value, CTX, pairs)


def mixer(
    token_ids,
    table,
    norm_gain,
    conv_weight,
    conv_bias,
    weight_b,
    weight_c,
    step_weight,
    step_bias,
    log_rate,
    skip_gain,
    out_grad,
):
    size = lax.axis_size(CTX)
    within = [(i, i ^ 1) for i in range(size)]
    across = [pair for i in range(1, size - 1, 2) for pair in ((i, i + 1), (i + 1, i))]
    edge = ((8, 256), F32)
    square = ((ROWS, 256), F32)
    half_square = ((ROWS, 256), BF16)
    squares, ids = call(
        squares_kernel,
        (((GROUPS, 1, 128), F32), ((1, ROWS), jnp.int32)),
        table, token_ids[None],
        near=False,
    )
    squares = swap(squares, "fsdp")
    ids_pair = shift(ids, within)
    ids_side = shift(ids, across)
    place = lax.axis_index(CTX).reshape(1, 1)
    table, gain, cw, cb, wb, wc, swt, swx, bias, rate, skip, dy = call(
        fetch_kernel,
        (
            ((16, 256), F32),
            ((1, 256), F32),
            ((4, 256), F32),
            ((1, 256), F32),
            ((256, 128), BF16),
            ((256, 128), BF16),
            ((64, 256), BF16),
            ((128, 256), BF16),
            ((8, 1), F32),
            ((8, 1), F32),
            ((1, 256), F32),
            half_square,
        ),
        table, norm_gain[None], conv_weight, conv_bias[None], weight_b, weight_c,
        jnp.transpose(step_weight), step_bias[None], log_rate[None], skip_gain[None], out_grad,
        near=False,
    )
    xf, xr, gf, gr, part, oht, scale = call(
        tokens_kernel,
        (
            half_square,
            half_square,
            half_square,
            half_square,
            ((GROUPS, 24, 512), BF16),
            ((128, 256), BF16),
            ((16, 128), F32),
        ),
        ids, ids_pair, ids_side, place, squares, table, gain, cw, cb, wb, wc, swx,
    )
    bc, raw = call(reduce_kernel, (((GROUPS, 16, 512), BF16), ((8, 256), F32)), swap(part, "fsdp"))
    bc = swap(bc, "fsdp").reshape(ROWS, 512)
    half_pair = ((2, ROWS, 256), BF16)
    cols, rows, weighted, turned, packed = call(
        steps_kernel,
        (((ROWS, 128), F32), ((48, ROWS), F32), half_pair, half_pair, edge),
        raw, bias, rate, xf, xr, dy,
    )
    (states,) = call(
        states_kernel, (((NEAR, 72, 256), BF16),), bc, weighted, turned, packed
    )
    arrived = swap(states, BESIDE)
    y0, dxf0, dxr0, dbc0, side, line = call(
        within_kernel,
        (square, square, square, ((ROWS, 512), BF16), edge, edge),
        bc, cols, rows, xf, xr, dy, skip,
    )
    (groups,) = call(group_kernel, (((FAR, 40, 256), BF16),), arrived, place)
    groups = swap(groups, "zh")
    (entering,) = call(chain_kernel, (((NEAR, 64, 256), BF16),), arrived, groups, place)
    entering = swap(entering, BESIDE)
    (dpart,) = call(
        partials_kernel, (((GROUPS, 16, 512), BF16),), entering, weighted, turned, dbc0
    )
    mixer_out, dxf, dxr, draw, small = call(
        carried_kernel,
        (half_square, square, square, ((8, 256), BF16), edge),
        entering, bc, cols, rows, xf, xr, dy, y0, dxf0, dxr0, side, line, rate,
        final=(0,),
    )
    (totals,) = call(total_kernel, (((GROUPS, 40, 256), BF16),), swap(dpart, "fsdp"), draw)
    dpf, dpr, gsend = call(
        project_back_kernel,
        (square, square, ((NEAR, 104, 128), BF16)),
        swap(totals, "fsdp"), xf, xr, gf, gr, dxf, dxr, wb,
        wc, swt, oht, table, scale, gain, cw, small, place,
    )
    small_edge = ((8, 128), F32)
    summed, near_prev, near_next = call(
        near_kernel,
        (((FAR, 104, 128), BF16), small_edge, small_edge),
        swap(gsend, BESIDE), place,
    )
    summed = swap(summed, "zh")
    gn, payload = call(
        normed_kernel,
        (half_square, ((GROUPS, 1, 384), F32)),
        dpf, dpr, summed, near_prev, near_next, place, cw, gain, table, oht,
        scratch=[VMEM((ROWS + 8, 256), F32), VMEM((ROWS + 8, 256), F32)],
    )
    (gathered,) = call(far_kernel, (((NEAR, 96, 128), BF16),), summed)
    crossed = swap(payload, "fsdp")
    (grad_embedded,) = call(
        embedded_kernel, (half_square,), crossed, gn, gain, table, scale, oht, final=(0,)
    )
    outs = call(
        finish_kernel,
        (
            ((16, 256), F32),
            ((1, 256), F32),
            ((4, 256), F32),
            ((1, 256), F32),
            ((256, 128), F32),
            ((256, 128), F32),
            ((64, 256), F32),
            ((1, 4), F32),
            ((1, 4), F32),
            ((1, 4), F32),
        ),
        swap(gathered, BESIDE), crossed, table, scale, gain,
        final=range(10),
    )
    gt, gg, gcw, gcb, gwb, gwc, gswt, gsb, glr, gsg = outs
    return (
        mixer_out,
        grad_embedded,
        gt,
        gg[0],
        gcw,
        gcb[0],
        gwb,
        gwc,
        jnp.transpose(gswt),
        gsb[0],
        glr[0],
        gsg[0],
    )


def solution(mesh):
    devices = mesh.devices.reshape(mesh.shape["fsdp"], FAR, 4, 2)
    mesh = jax.sharding.Mesh(devices, ("fsdp",) + CTX)
    return jax.shard_map(
        mixer,
        mesh=mesh,
        in_specs=(
            P(CTX),
            P(None, "fsdp"),
            P("fsdp"),
            P(None, "fsdp"),
            P("fsdp"),
            P("fsdp", None),
            P("fsdp", None),
            P("fsdp", None),
            P("fsdp"),
            P("fsdp"),
            P("fsdp"),
            P(CTX, "fsdp"),
        ),
        out_specs=(
            P(CTX, "fsdp"),
            P(CTX, "fsdp"),
            P(None, "fsdp"),
            P("fsdp"),
            P(None, "fsdp"),
            P("fsdp"),
            P("fsdp", None),
            P("fsdp", None),
            P("fsdp", None),
            P("fsdp"),
            P("fsdp"),
            P("fsdp"),
        ),
        check_vma=False,
    )
```

```python
import jax
import jax.numpy as jnp
from jax import lax
from jax.sharding import PartitionSpec as P
from jax.experimental import pallas as pl
from jax.experimental.pallas import tpu as pltpu

D = 4096
ROWS = 256
HEADS = 4
STATE = 128
GROUPS = 16
NEAR = 8
FAR = 4
CTX = ("zh", "zl", "xh")
BESIDE = ("zl", "xh")
F32 = jnp.float32
BF16 = jnp.bfloat16
VMEM = pltpu.VMEM


def call(kernel, outs, *args, final=(), scratch=(), near=True):
    shapes = tuple(
        jax.ShapeDtypeStruct(shape, kind) if i in final else VMEM(shape, kind)
        for i, (shape, kind) in enumerate(outs)
    )
    space = VMEM if near else pltpu.HBM
    args = [pltpu.with_memory_space_constraint(arg, space) for arg in args]
    return pl.pallas_call(
        kernel,
        out_shape=shapes,
        scratch_shapes=scratch,
        compiler_params=pltpu.CompilerParams(vmem_limit_bytes=24 << 20),
    )(*args)


def iota(shape, dim):
    return lax.broadcasted_iota(jnp.int32, shape, dim)


def mm(left, right):
    return lax.dot_general(left, right, (((1,), (0,)), ((), ())), preferred_element_type=F32)


def mm_tn(left, right):
    return lax.dot_general(left, right, (((0,), (0,)), ((), ())), preferred_element_type=F32)


def mm_nt(left, right):
    return lax.dot_general(left, right, (((1,), (1,)), ((), ())), preferred_element_type=F32)


def pieces(value, count):
    parts = []
    rest = value
    for _ in range(count):
        part = rest.astype(BF16)
        parts.append(part)
        rest = rest - part.astype(F32)
    return parts


def exact(form, left, right, count, split_left):
    total = None
    for part in pieces(left if split_left else right, count):
        term = form(part, right) if split_left else form(left, part)
        total = term if total is None else total + term
    return total


def head_masks(rows):
    lane_head = iota((rows, 256), 1) // 64
    return [lane_head == h for h in range(HEADS)]


def by_head(values, masks):
    out = values[3]
    for h in range(3):
        out = jnp.where(masks[h], values[h], out)
    return out


def expand(cols, first, masks):
    wide = [jnp.broadcast_to(cols[:, first + h : first + h + 1], (ROWS, 256)) for h in range(HEADS)]
    return by_head(wide, masks)


def columns(rows):
    missing = 128 - rows.shape[0]
    return jnp.transpose(jnp.concatenate([rows, jnp.zeros((missing, ROWS), F32)], axis=0))


def inclusive_masks():
    before = iota((ROWS, ROWS), 0) <= iota((ROWS, ROWS), 1)
    after = iota((ROWS, ROWS), 0) >= iota((ROWS, ROWS), 1)
    return jnp.where(before, 1.0, 0.0).astype(BF16), jnp.where(after, 1.0, 0.0).astype(BF16)


def squares_kernel(table, ids, send, ids_v):
    ids_v[...] = ids[...]
    squares = jnp.concatenate([table[...] * table[...], jnp.zeros((112, 256), F32)], axis=0)
    sums = exact(mm_nt, jnp.ones((8, 256), BF16), squares, 3, False)
    send[...] = jnp.broadcast_to(sums[0:1][None], (GROUPS, 1, 128))


def fetch_kernel(
    table, gain, cw, cb, wb, wc, swt, step_bias, log_rate, skip_gain, dy,
    table_v, gain_v, cw_v, cb_v, wb_v, wc_v, swt_v, swx, bias, rate, skip, dy_v,
):
    table_v[...] = table[...]
    gain_v[...] = gain[...]
    cw_v[...] = cw[...]
    cb_v[...] = cb[...]
    wb_v[...] = wb[...]
    wc_v[...] = wc[...]
    swt_v[...] = swt[...]
    dy_v[...] = dy[...]
    place = iota((128, 64), 0)
    chosen = jnp.where(place // 8 * 4 + place % 4 == iota((128, 64), 1), 1.0, 0.0).astype(BF16)
    swx[...] = mm(chosen, swt[...]).astype(BF16)
    own = iota((8, HEADS), 0) % HEADS == iota((8, HEADS), 1)
    for source, column in ((step_bias, bias), (log_rate, rate)):
        column[...] = jnp.sum(jnp.where(own, source[...], 0.0), axis=1, keepdims=True)
    lane_head = iota((1, 256), 1) // 64
    row = jnp.zeros((1, 256), F32)
    for h in range(HEADS):
        row = jnp.where(lane_head == h, skip_gain[:, h : h + 1], row)
    skip[...] = row


def tokens_kernel(
    ids, ids_pair, ids_side, place, got, table, gain, cw, cb, wb, wc, swx,
    xf, xr, gf, gr, send, oht_ref, scale,
):
    total = got[0]
    for k in range(1, GROUPS):
        total = total + got[k]
    unit = lax.rsqrt(total / D + 1e-05)
    spread = jnp.transpose(jnp.broadcast_to(unit, (128, 128)))[0:16]
    scale[...] = spread
    unit = spread[:, 0:1]
    normed = (table[...] * unit * gain[...]).astype(BF16).astype(F32)
    vocab = iota((16, ROWS), 0)
    lane = iota((1, ROWS), 1)
    here = ids[...]
    even = place[...] % 2 == 0
    following = jnp.where(even, ids_pair[...], ids_side[...])
    following = jnp.where(place[...] == FAR * NEAR - 1, -1, following)
    preceding = jnp.where(even, ids_side[...], ids_pair[...])
    preceding = jnp.where(place[...] == 0, -1, preceding)
    hits = []
    for o in range(7):
        d = o - 3
        if d == 0:
            moved = here
        elif d > 0:
            ahead = pltpu.roll(following, ROWS - d, 1)
            moved = jnp.where(lane < ROWS - d, pltpu.roll(here, ROWS - d, 1), ahead)
        else:
            moved = jnp.where(lane >= -d, pltpu.roll(here, -d, 1), pltpu.roll(preceding, -d, 1))
        hits.append(jnp.where(moved == vocab, 1.0, 0.0))
    hits.append(jnp.zeros((16, ROWS), F32))
    oht = jnp.concatenate(hits, axis=0).astype(BF16)
    oht_ref[...] = oht
    none = jnp.zeros((16, 256), F32)
    taps = [cw[k : k + 1, :] * normed for k in range(4)]
    fwd_rows = jnp.concatenate([taps[3], taps[2], taps[1], taps[0], none, none, none, none], axis=0)
    rev_rows = jnp.concatenate([none, none, none, taps[0], taps[1], taps[2], taps[3], none], axis=0)
    halves = []
    for rows, x_ref, slope_ref in ((fwd_rows, xf, gf), (rev_rows, xr, gr)):
        pre = exact(mm_tn, oht, rows, 3, False) + cb[...]
        gate = 1.0 / (1.0 + jnp.exp(-pre))
        slope_ref[...] = (gate * (1.0 + pre * (1.0 - gate))).astype(BF16)
        half = (pre * gate).astype(BF16)
        x_ref[...] = half
        halves.append(half)
    for member, half in enumerate(halves):
        for side, weight in ((0, wb), (128, wc)):
            part = mm(half, weight[...]).astype(BF16).reshape(GROUPS, 16, 128)
            send[:, member * 16 : member * 16 + 16, side : side + 128] = part
    own = iota((128, 256), 0) % 8 < 4
    steps = jnp.where(own, mm_nt(swx[...], halves[0]), mm_nt(swx[...], halves[1]))
    send[:, 32:40, :] = steps.astype(BF16).reshape(GROUPS, 8, 256)


def reduce_kernel(got, bc, raw):
    total = got[0].astype(F32)
    for k in range(1, GROUPS):
        total = total + got[k].astype(F32)
    half = jnp.concatenate([total[0:16], total[16:32]], axis=1).astype(BF16)
    bc[...] = jnp.broadcast_to(half[None], (GROUPS, 16, 512))
    raw[...] = total[32:40]


def steps_kernel(
    raw, bias, rate, xf, xr, dy,
    cols_ref, rows_ref, weighted_ref, turned_ref, packed_ref,
):
    shifted = raw[...] + bias[...]
    step = jnp.maximum(shifted, 0.0) + jnp.log1p(jnp.exp(-jnp.abs(shifted)))
    slope = 1.0 / (1.0 + jnp.exp(-shifted))
    logdec = -step * jnp.exp(rate[...])
    before, after = inclusive_masks()
    fwd_row = iota((8, ROWS), 0) < 4
    prefix = exact(mm, logdec, before, 3, True)
    suffix = exact(mm, logdec, after, 3, True)
    cumul = jnp.where(fwd_row, prefix, suffix)
    fwd_one = iota((8, 1), 0) < 4
    ending = jnp.where(fwd_one, prefix[:, ROWS - 1 : ROWS], suffix[:, 0:1])
    closing = jnp.exp(ending - cumul)
    weight = closing * step
    grown = jnp.exp(cumul)
    rows_ref[...] = jnp.concatenate([cumul, step, weight, closing, slope, logdec], axis=0)
    cols = columns(jnp.concatenate([cumul, step, weight, grown], axis=0))
    cols_ref[...] = cols
    masks = head_masks(ROWS)
    dyf = dy[...].astype(F32)
    for br, x in ((0, xf), (1, xr)):
        weight_wide = expand(cols, 16 + 4 * br, masks)
        grown_wide = expand(cols, 24 + 4 * br, masks)
        weighted_ref[br] = (weight_wide * x[...].astype(F32)).astype(BF16)
        turned_ref[br] = (grown_wide * dyf).astype(BF16)
    decay = jnp.exp(ending)
    lane_head = iota((1, 256), 1) // 64
    fwd_decay = jnp.zeros((1, 256), F32)
    rev_decay = jnp.zeros((1, 256), F32)
    for h in range(HEADS):
        fwd_decay = jnp.where(lane_head == h, decay[h : h + 1], fwd_decay)
        rev_decay = jnp.where(lane_head == h, decay[h + 4 : h + 5], rev_decay)
    packed_ref[...] = split_decays(fwd_decay, rev_decay)


def split_decays(fwd_decay, rev_decay):
    row = iota((8, 256), 0)
    f_high = fwd_decay.astype(BF16).astype(F32)
    r_high = rev_decay.astype(BF16).astype(F32)
    packed = jnp.where(row == 0, f_high, 0.0)
    packed = jnp.where(row == 1, fwd_decay - f_high, packed)
    packed = jnp.where(row == 2, r_high, packed)
    return jnp.where(row == 3, rev_decay - r_high, packed)


def join_decays(packed):
    rows = packed.astype(F32)
    return rows[0:1] + rows[1:2], rows[2:3] + rows[3:4]


def states_kernel(bc, weighted, turned, packed, send):
    found = []
    for br in range(2):
        b = bc[:, br * 256 : br * 256 + 128]
        c = bc[:, br * 256 + 128 : br * 256 + 256]
        found.append((mm_tn(b, weighted[br]), mm_tn(c, turned[br])))
    chains = (found[0][0], found[1][1], found[1][0], found[0][1])
    for ch, state in enumerate(chains):
        send[:, ch * 16 : ch * 16 + 16, :] = state.astype(BF16).reshape(NEAR, 16, 256)
    send[:, 64:72, :] = jnp.broadcast_to(packed[...].astype(BF16)[None], (NEAR, 8, 256))


def advance(state, decay_first, decay_second, piece):
    return decay_first * state[0] + piece[0:16], decay_second * state[1] + piece[16:32]


def group_kernel(got, place, send):
    here = place[...] // NEAR
    nothing = jnp.zeros((16, 256), F32)
    up = (nothing, nothing)
    down = (nothing, nothing)
    fwd_all = jnp.ones((1, 256), F32)
    rev_all = jnp.ones((1, 256), F32)
    for i in range(NEAR):
        fwd_decay, rev_decay = join_decays(got[i, 64:72, :])
        fwd_all = fwd_all * fwd_decay
        rev_all = rev_all * rev_decay
        up = advance(up, fwd_decay, rev_decay, got[i, 0:32, :].astype(F32))
        j = NEAR - 1 - i
        fwd_decay, rev_decay = join_decays(got[j, 64:72, :])
        down = advance(down, rev_decay, fwd_decay, got[j, 32:64, :].astype(F32))
    upward = jnp.concatenate(up, axis=0)
    downward = jnp.concatenate(down, axis=0)
    decays = split_decays(fwd_all, rev_all).astype(BF16)
    for g in range(FAR):
        send[g, 0:32, :] = jnp.where(here < g, upward, downward).astype(BF16)
        send[g, 32:40, :] = decays


def chain_kernel(got, far, place, out):
    here = place[...] // NEAR
    nothing = jnp.zeros((16, 256), F32)
    up = (nothing, nothing)
    down = (nothing, nothing)
    for g in range(FAR):
        fwd_decay, rev_decay = join_decays(far[g, 32:40, :])
        moved = advance(up, fwd_decay, rev_decay, far[g, 0:32, :].astype(F32))
        up = tuple(jnp.where(here > g, new, old) for new, old in zip(moved, up))
        k = FAR - 1 - g
        fwd_decay, rev_decay = join_decays(far[k, 32:40, :])
        moved = advance(down, rev_decay, fwd_decay, far[k, 0:32, :].astype(F32))
        down = tuple(jnp.where(here < k, new, old) for new, old in zip(moved, down))
    for i in range(NEAR):
        out[i, 0:16, :] = up[0].astype(BF16)
        out[i, 16:32, :] = up[1].astype(BF16)
        fwd_decay, rev_decay = join_decays(got[i, 64:72, :])
        up = advance(up, fwd_decay, rev_decay, got[i, 0:32, :].astype(F32))
        j = NEAR - 1 - i
        out[j, 32:48, :] = down[0].astype(BF16)
        out[j, 48:64, :] = down[1].astype(BF16)
        fwd_decay, rev_decay = join_decays(got[j, 64:72, :])
        down = advance(down, rev_decay, fwd_decay, got[j, 32:64, :].astype(F32))


def within_kernel(bc, cols_ref, rows_ref, xf, xr, dy, skip, y_ref, dxf, dxr, dbc, side, line):
    masks = head_masks(ROWS)
    t_at = iota((ROWS, ROWS), 0)
    s_at = iota((ROWS, ROWS), 1)
    lane = iota((ROWS, 128), 1)
    cols = cols_ref[...]
    dyh = dy[...]
    dyf = dyh.astype(F32)
    nothing = jnp.zeros((ROWS, 256), BF16)
    direct = skip[...] * dyf
    total = skip[...] * (xf[...].astype(F32) + xr[...].astype(F32))
    side_acc = jnp.zeros((ROWS, 128), F32)
    lines = []
    for br, x, dx_ref in ((0, xf, dxf), (1, xr, dxr)):
        xh = x[...]
        b = bc[:, br * 256 : br * 256 + 128]
        c = bc[:, br * 256 + 128 : br * 256 + 256]
        inner = mm_nt(c, b)
        causal = t_at >= s_at if br == 0 else t_at <= s_at
        dinner = jnp.zeros((ROWS, ROWS), F32)
        intra = []
        back = []
        for h in range(HEADS):
            at = 4 * br + h
            spread = cols[:, at : at + 1] - rows_ref[at : at + 1, :]
            decay = jnp.exp(jnp.where(causal, spread, -jnp.inf))
            step = rows_ref[8 + at : 9 + at, :]
            paced = decay * step
            mixing = (inner * paced).astype(BF16)
            intra.append(mm(mixing, xh))
            back.append(mm_tn(mixing, dyh))
            dmix = mm_nt(jnp.where(masks[h], dyh, nothing), xh)
            dinner = dinner + dmix * paced
            reach = dmix * decay * inner
            lines.append(jnp.sum(reach, axis=0, keepdims=True))
            flow = jnp.sum(reach * step, axis=1, keepdims=True)
            side_acc = jnp.where(lane == at, flow, side_acc)
        total = total + by_head(intra, masks)
        dx_ref[...] = direct + by_head(back, masks)
        dhalf = dinner.astype(BF16)
        dbc[:, br * 256 : br * 256 + 128] = mm_tn(dhalf, c).astype(BF16)
        dbc[:, br * 256 + 128 : br * 256 + 256] = mm(dhalf, b).astype(BF16)
    y_ref[...] = total
    side[...] = jnp.transpose(side_acc)[0:8]
    line[...] = jnp.concatenate(lines, axis=0)


def state(got, ch):
    return got[:, ch * 16 : ch * 16 + 16, :].reshape(STATE, 256)


def partials_kernel(got, weighted, turned, dbc0, send):
    for br, at_state, at_grad in ((0, 0, 3), (1, 2, 1)):
        dc = mm_nt(turned[br], state(got, at_state))
        db = mm_nt(weighted[br], state(got, at_grad))
        at = br * 256
        part = dbc0[:, at : at + 256].astype(F32) + jnp.concatenate([db, dc], axis=1)
        send[:, :, at : at + 256] = part.astype(BF16).reshape(16, 16, 256)


def carried_kernel(
    got, bc, cols_ref, rows_ref, xf, xr, dy, y0, dxf0, dxr0, side, line, rate,
    out, dxf, dxr, draw_ref, small,
):
    dyf = dy[...].astype(F32)

    masks = head_masks(ROWS)
    cols = cols_ref[...]

    row_at = iota((8, 256), 0)
    lane_head = iota((8, 256), 1) // 64
    total = y0[...]
    dp = jnp.zeros((8, ROWS), F32)
    dw = jnp.zeros((8, ROWS), F32)
    d_end = jnp.zeros((8, 1), F32)
    for br, x, dx0, dx_ref, at_state, at_grad in ((0, xf, dxf0, dxf, 0, 3), (1, xr, dxr0, dxr, 2, 1)):
        start_half = state(got, at_state)
        ahead_half = state(got, at_grad)
        b = bc[:, br * 256 : br * 256 + 128]
        c = bc[:, br * 256 + 128 : br * 256 + 256]
        heads = jnp.where(lane_head + 4 * br == row_at, 1.0, 0.0).astype(BF16)
        carried = expand(cols, 24 + 4 * br, masks) * mm(c, start_half)
        total = total + carried
        dp = dp + exact(mm_nt, heads, dyf * carried, 2, False)
        xv = x[...].astype(F32)
        toward = mm(b, ahead_half)
        dx_ref[...] = dx0[...] + expand(cols, 16 + 4 * br, masks) * toward
        dw = dw + exact(mm_nt, heads, xv * toward, 2, False)
        both = jnp.sum(start_half.astype(F32) * ahead_half.astype(F32), axis=0, keepdims=True)
        spread = jnp.where(lane_head + 4 * br == row_at, both, 0.0)
        d_end = d_end + jnp.sum(spread, axis=1, keepdims=True)
    out[...] = total.astype(BF16)
    cumul = rows_ref[0:8]
    step = rows_ref[8:16]
    weight = rows_ref[16:24]
    closing = rows_ref[24:32]
    slope = rows_ref[32:40]
    logdec = rows_ref[40:48]
    at = iota((8, ROWS), 1)
    row = iota((8, ROWS), 0)
    last = at == jnp.where(row < 4, ROWS - 1, 0)
    pull = dw * weight
    ending = jnp.sum(jnp.where(last, cumul, 0.0), axis=1, keepdims=True)
    d_end = jnp.exp(ending) * d_end + jnp.sum(pull, axis=1, keepdims=True)
    dcumul = side[...] - step * line[...] + dp - pull + jnp.where(last, d_end, 0.0)
    before, after = inclusive_masks()
    prefix = exact(mm, dcumul, before, 3, True)
    suffix = exact(mm, dcumul, after, 3, True)
    dlog = jnp.where(row < 4, suffix, prefix)
    dstep = line[...] + dw * closing - dlog * jnp.exp(rate[...])
    draw = dstep * slope
    draw_ref[...] = draw.astype(BF16)
    d_bias = jnp.sum(draw, axis=1, keepdims=True)
    d_rate = jnp.sum(dlog * logdec, axis=1, keepdims=True)
    first = iota((1, 256), 1)
    bias_row = jnp.zeros((1, 256), F32)
    rate_row = jnp.zeros((1, 256), F32)
    for h in range(HEADS):
        bias_row = jnp.where(first == 64 * h, d_bias[h : h + 1] + d_bias[h + 4 : h + 5], bias_row)
        rate_row = jnp.where(first == 64 * h, d_rate[h : h + 1] + d_rate[h + 4 : h + 5], rate_row)
    skip_row = jnp.sum(dyf * (xf[...].astype(F32) + xr[...].astype(F32)), axis=0, keepdims=True)
    none = jnp.zeros((5, 256), F32)
    small[...] = jnp.concatenate([skip_row, bias_row, rate_row, none], axis=0)


def total_kernel(got, draw, send):
    total = got[0].astype(F32)
    for k in range(1, GROUPS):
        total = total + got[k].astype(F32)
    half = total.astype(BF16)
    send[:, 0:16, :] = jnp.broadcast_to(half[None, :, 0:256], (GROUPS, 16, 256))
    send[:, 16:32, :] = jnp.broadcast_to(half[None, :, 256:512], (GROUPS, 16, 256))
    send[:, 32:40, :] = jnp.broadcast_to(draw[...][None], (GROUPS, 8, 256))


def split_row(value, rows):
    row = iota((rows, 128), 0) % 32
    high = value.astype(BF16).astype(F32)
    return jnp.where(row == 0, high, 0.0) + jnp.where(row == 1, value - high, 0.0)


def pack_edge(rows):
    return jnp.concatenate([rows[:, 0:128], rows[:, 128:256], jnp.zeros((2, 128), F32)], axis=0)


def open_edge(packed):
    return jnp.concatenate([packed[0:3], packed[3:6]], axis=1)


def picked(edges, at, count):
    total = jnp.zeros((8, 128), F32)
    for k in range(count):
        total = jnp.where(at == k, edges[k, 96:104, :].astype(F32), total)
    return total


def project_back_kernel(
    got, xf, xr, gf, gr, dxf, dxr, wb, wc, swt, oht, table, scale, gain, cw, small,
    place, dpf, dpr, send,
):
    draw = got[:, 32:40, :].astype(F32).reshape(128, 256).astype(BF16)
    pick_row = iota((128, 64), 0)
    pick_col = iota((128, 64), 1)
    wanted = pick_row // 8 * 4 + pick_row % 4
    normed = (table[...] * scale[:, 0:1] * gain[...]).astype(BF16).astype(F32)
    taps = [jnp.zeros((1, 256), F32)] * 4
    bias_row = jnp.zeros((1, 256), F32)
    wide = jnp.zeros((256, 256), F32)
    thin = jnp.zeros((256, 64), F32)
    ids_sum = jnp.zeros((16, 256), F32)
    for br, x, slope, dx, out in ((0, xf, gf, dxf, dpf), (1, xr, gr, dxr, dpr)):
        mine = (wanted == pick_col) & ((pick_row % 8 < 4) == (br == 0))
        dstep = mm_tn(draw, jnp.where(mine, 1.0, 0.0).astype(BF16)).astype(BF16)
        half = got[:, br * 16 : br * 16 + 16, :].reshape(ROWS, 256)
        into = mm_nt(half[:, 0:128], wb[...]) + mm_nt(half[:, 128:256], wc[...])
        into = into + mm(dstep, swt[...])
        whole = (dx[...] + into).astype(BF16).astype(F32)
        dpre = whole * slope[...].astype(F32)
        out[...] = dpre
        wide = wide + mm_tn(x[...], half)
        thin = thin + mm_tn(x[...], dstep)
        sums = exact(mm, oht[...], dpre, 2, False)
        for k in range(4):
            o = 3 - k if br == 0 else 3 + k
            block = sums[16 * o : 16 * o + 16]
            ids_sum = ids_sum + cw[k : k + 1] * block
            part = jnp.sum(normed * block, axis=0, keepdims=True)
            taps[k] = taps[k] + part
        bias_row = bias_row + jnp.sum(dpre, axis=0, keepdims=True)
    ahead_edge = pack_edge(dpr[ROWS - 3 : ROWS]).astype(BF16)
    behind_edge = pack_edge(dpf[0:3]).astype(BF16)
    onward = (place[...] + 1) % NEAR
    for k in range(NEAR):
        send[k, 96:104, :] = jnp.where(onward == k, ahead_edge, behind_edge)
    shared = table[...] * gain[...] * ids_sum
    placed = jnp.concatenate(
        [jnp.zeros((88, 256), F32), shared, jnp.zeros((24, 256), F32)], axis=0
    )
    crossed = exact(mm_nt, jnp.ones((8, 256), BF16), placed, 3, False)[0:1]
    stacked = jnp.concatenate(
        [jnp.zeros((64, 256), F32), ids_sum] + taps + [bias_row, small[0:3], jnp.zeros((40, 256), F32)],
        axis=0,
    )
    last = jnp.concatenate([thin, jnp.zeros((256, 64), F32)], axis=1) + jnp.transpose(stacked)
    last = last + split_row(crossed, 256)
    send[:, 0:32, :] = wide[:, 0:128].astype(BF16).reshape(NEAR, 32, 128)
    send[:, 32:64, :] = wide[:, 128:256].astype(BF16).reshape(NEAR, 32, 128)
    send[:, 64:96, :] = last.astype(BF16).reshape(NEAR, 32, 128)


def normed_kernel(
    dpf, dpr, far, near_prev, near_next, place, cw, gain, table, oht,
    gn_ref, payload, ahead, behind,
):
    here = place[...] % NEAR
    group = place[...] // NEAR
    prev = jnp.where(here == 0, picked(far, group - 1, FAR), near_prev[...])
    following = jnp.where(here == NEAR - 1, picked(far, group + 1, FAR), near_next[...])
    ahead[0:ROWS] = dpf[...]
    ahead[ROWS : ROWS + 8] = jnp.concatenate([open_edge(following), jnp.zeros((5, 256), F32)], axis=0)
    behind[0:8] = jnp.concatenate([jnp.zeros((5, 256), F32), open_edge(prev)], axis=0)
    behind[8 : ROWS + 8] = dpr[...]
    dn = jnp.zeros((ROWS, 256), F32)
    for k in range(4):
        dn = dn + cw[k : k + 1] * (ahead[k : k + ROWS] + behind[8 - k : 8 - k + ROWS])
    gn = dn.astype(BF16)
    gn_ref[...] = gn
    rated = exact(mm_tn, oht[48:64], table[...] * gain[...], 3, False)
    ones = jnp.ones((8, 256), BF16)
    row = exact(mm_nt, ones, gn.astype(F32) * rated, 3, False)[0:1]
    both = jnp.zeros((1, 128), F32)
    for k in range(FAR):
        both = both + far[k, 64:65, :].astype(F32) + far[k, 65:66, :].astype(F32)
    lane = iota((1, 128), 1)
    crossed = jnp.where((lane >= 88) & (lane < 104), both, 0.0)
    row = jnp.concatenate([row, crossed], axis=1)
    payload[...] = jnp.broadcast_to(row[None], (GROUPS, 1, 384))


def embedded_kernel(got, gn, gain, table, scale, oht, out):
    total = got[0]
    for k in range(1, GROUPS):
        total = total + got[k]
    cross = columns(jnp.broadcast_to(total[:, 0:256], (8, ROWS)))[:, 0:1]
    own = oht[48:64]
    unit = scale[:, 0:1]
    turned = exact(mm_tn, own, unit * gain[...], 3, False)
    shrunk = exact(mm_tn, own, table[...] * (unit * unit * unit / D), 3, False)
    out[...] = (turned * gn[...].astype(F32) - shrunk * cross).astype(BF16)


def near_kernel(got, place, send, near_prev, near_next):
    total = got[0, 0:96, :].astype(F32)
    for k in range(1, NEAR):
        total = total + got[k, 0:96, :].astype(F32)
    last = total[64:96]
    lane = iota((32, 128), 1)
    crossed = jnp.where((lane >= 88) & (lane < 104), last, 0.0)
    last = last - crossed + split_row(jnp.sum(crossed, axis=0, keepdims=True), 32)
    here = place[...] % NEAR
    prev = picked(got, (here + NEAR - 1) % NEAR, NEAR)
    following = picked(got, (here + 1) % NEAR, NEAR)
    near_prev[...] = prev
    near_next[...] = following
    forward = jnp.where(here == 0, prev, following)
    total = jnp.concatenate([total[0:64], last, forward], axis=0)
    send[...] = jnp.broadcast_to(total.astype(BF16)[None], (FAR, 104, 128))


def far_kernel(got, send):
    total = got[0, 0:96, :].astype(F32)
    for k in range(1, FAR):
        total = total + got[k, 0:96, :].astype(F32)
    send[...] = jnp.broadcast_to(total.astype(BF16)[None], (NEAR, 96, 128))


def finish_kernel(got, cross, table, scale, gain, gt, gg, gcw, gcb, gwb, gwc, gswt, gsb, glr, gsg):
    gwb[...] = got[:, 0:32, :].astype(F32).reshape(256, 128)
    gwc[...] = got[:, 32:64, :].astype(F32).reshape(256, 128)
    rows = jnp.transpose(got[:, 64:96, :].astype(F32).reshape(256, 128))
    gswt[...] = rows[0:64]
    sums = rows[64:80]
    here = cross[0]
    for k in range(1, GROUPS):
        here = here + cross[k]
    crossed = jnp.transpose(jnp.broadcast_to(here[:, 256:384], (128, 128)))[88:104, 0:1]
    unit = scale[:, 0:1]
    gt[...] = unit * gain[...] * sums - table[...] * (unit * unit * unit / D) * crossed
    gg[...] = jnp.sum(table[...] * unit * sums, axis=0, keepdims=True)
    gcw[...] = rows[80:84]
    gcb[...] = rows[84:85]
    lane = iota((8, 256), 1)
    tail = rows[80:88]
    picked = iota((8, 4), 1)
    result = jnp.zeros((8, 4), F32)
    for h in range(HEADS):
        part = jnp.sum(jnp.where(lane // 64 == h, tail, 0.0), axis=1, keepdims=True)
        result = jnp.where(picked == h, part, result)
    gsg[...] = result[5:6]
    gsb[...] = result[6:7]
    glr[...] = result[7:8]


def swap(value, axis):
    return lax.all_to_all(value, axis, 0, 0, tiled=True)


def shift(value, pairs):
    return lax.ppermute(value, CTX, pairs)


def mixer(
    token_ids,
    table,
    norm_gain,
    conv_weight,
    conv_bias,
    weight_b,
    weight_c,
    step_weight,
    step_bias,
    log_rate,
    skip_gain,
    out_grad,
):
    size = lax.axis_size(CTX)
    within = [(i, i ^ 1) for i in range(size)]
    across = [pair for i in range(1, size - 1, 2) for pair in ((i, i + 1), (i + 1, i))]
    edge = ((8, 256), F32)
    square = ((ROWS, 256), F32)
    half_square = ((ROWS, 256), BF16)
    squares, ids = call(
        squares_kernel,
        (((GROUPS, 1, 128), F32), ((1, ROWS), jnp.int32)),
        table, token_ids[None],
        near=False,
    )
    squares = swap(squares, "fsdp")
    ids_pair = shift(ids, within)
    ids_side = shift(ids, across)
    place = lax.axis_index(CTX).reshape(1, 1)
    table, gain, cw, cb, wb, wc, swt, swx, bias, rate, skip, dy = call(
        fetch_kernel,
        (
            ((16, 256), F32),
            ((1, 256), F32),
            ((4, 256), F32),
            ((1, 256), F32),
            ((256, 128), BF16),
            ((256, 128), BF16),
            ((64, 256), BF16),
            ((128, 256), BF16),
            ((8, 1), F32),
            ((8, 1), F32),
            ((1, 256), F32),
            half_square,
        ),
        table, norm_gain[None], conv_weight, conv_bias[None], weight_b, weight_c,
        jnp.transpose(step_weight), step_bias[None], log_rate[None], skip_gain[None], out_grad,
        near=False,
    )
    xf, xr, gf, gr, part, oht, scale = call(
        tokens_kernel,
        (
            half_square,
            half_square,
            half_square,
            half_square,
            ((GROUPS, 40, 256), BF16),
            ((128, 256), BF16),
            ((16, 128), F32),
        ),
        ids, ids_pair, ids_side, place, squares, table, gain, cw, cb, wb, wc, swx,
    )
    bc, raw = call(reduce_kernel, (((GROUPS, 16, 512), BF16), ((8, 256), F32)), swap(part, "fsdp"))
    bc = swap(bc, "fsdp").reshape(ROWS, 512)
    half_pair = ((2, ROWS, 256), BF16)
    cols, rows, weighted, turned, packed = call(
        steps_kernel,
        (((ROWS, 128), F32), ((48, ROWS), F32), half_pair, half_pair, edge),
        raw, bias, rate, xf, xr, dy,
    )
    (states,) = call(
        states_kernel, (((NEAR, 72, 256), BF16),), bc, weighted, turned, packed
    )
    arrived = swap(states, BESIDE)
    y0, dxf0, dxr0, dbc0, side, line = call(
        within_kernel,
        (square, square, square, ((ROWS, 512), BF16), edge, edge),
        bc, cols, rows, xf, xr, dy, skip,
    )
    (groups,) = call(group_kernel, (((FAR, 40, 256), BF16),), arrived, place)
    groups = swap(groups, "zh")
    (entering,) = call(chain_kernel, (((NEAR, 64, 256), BF16),), arrived, groups, place)
    entering = swap(entering, BESIDE)
    (dpart,) = call(
        partials_kernel, (((GROUPS, 16, 512), BF16),), entering, weighted, turned, dbc0
    )
    mixer_out, dxf, dxr, draw, small = call(
        carried_kernel,
        (half_square, square, square, ((8, 256), BF16), edge),
        entering, bc, cols, rows, xf, xr, dy, y0, dxf0, dxr0, side, line, rate,
        final=(0,),
    )
    (totals,) = call(total_kernel, (((GROUPS, 40, 256), BF16),), swap(dpart, "fsdp"), draw)
    dpf, dpr, gsend = call(
        project_back_kernel,
        (square, square, ((NEAR, 104, 128), BF16)),
        swap(totals, "fsdp"), xf, xr, gf, gr, dxf, dxr, wb,
        wc, swt, oht, table, scale, gain, cw, small, place,
    )
    small_edge = ((8, 128), F32)
    summed, near_prev, near_next = call(
        near_kernel,
        (((FAR, 104, 128), BF16), small_edge, small_edge),
        swap(gsend, BESIDE), place,
    )
    summed = swap(summed, "zh")
    gn, payload = call(
        normed_kernel,
        (half_square, ((GROUPS, 1, 384), F32)),
        dpf, dpr, summed, near_prev, near_next, place, cw, gain, table, oht,
        scratch=[VMEM((ROWS + 8, 256), F32), VMEM((ROWS + 8, 256), F32)],
    )
    (gathered,) = call(far_kernel, (((NEAR, 96, 128), BF16),), summed)
    crossed = swap(payload, "fsdp")
    (grad_embedded,) = call(
        embedded_kernel, (half_square,), crossed, gn, gain, table, scale, oht, final=(0,)
    )
    outs = call(
        finish_kernel,
        (
            ((16, 256), F32),
            ((1, 256), F32),
            ((4, 256), F32),
            ((1, 256), F32),
            ((256, 128), F32),
            ((256, 128), F32),
            ((64, 256), F32),
            ((1, 4), F32),
            ((1, 4), F32),
            ((1, 4), F32),
        ),
        swap(gathered, BESIDE), crossed, table, scale, gain,
        final=range(10),
    )
    gt, gg, gcw, gcb, gwb, gwc, gswt, gsb, glr, gsg = outs
    return (
        mixer_out,
        grad_embedded,
        gt,
        gg[0],
        gcw,
        gcb[0],
        gwb,
        gwc,
        jnp.transpose(gswt),
        gsb[0],
        glr[0],
        gsg[0],
    )


def solution(mesh):
    devices = mesh.devices.reshape(mesh.shape["fsdp"], FAR, 4, 2)
    mesh = jax.sharding.Mesh(devices, ("fsdp",) + CTX)
    return jax.shard_map(
        mixer,
        mesh=mesh,
        in_specs=(
            P(CTX),
            P(None, "fsdp"),
            P("fsdp"),
            P(None, "fsdp"),
            P("fsdp"),
            P("fsdp", None),
            P("fsdp", None),
            P("fsdp", None),
            P("fsdp"),
            P("fsdp"),
            P("fsdp"),
            P(CTX, "fsdp"),
        ),
        out_specs=(
            P(CTX, "fsdp"),
            P(CTX, "fsdp"),
            P(None, "fsdp"),
            P("fsdp"),
            P(None, "fsdp"),
            P("fsdp"),
            P("fsdp", None),
            P("fsdp", None),
            P("fsdp", None),
            P("fsdp"),
            P("fsdp"),
            P("fsdp"),
        ),
        check_vma=False,
    )
```
